32 devices in a mesh: clips: 2 (over x), tile: 4 (over y, core), tm: 4 (over z).
Axes of the slice: x: 2, y: 2, z: 4, core: 2. Of those that a mesh axis runs over, the one named last changes fastest.
Arguments:
- clip_frames: bfloat16 [16, 16, 128, 256], P(('clips', 'tm'), 'tile'), parts along dimension 0, may hold values from -6 to 6
- weight_first: bfloat16 [3, 3, 3, 256, 256], replicated, may hold values from -0.078125 to 0.078125
- bias_first: float32 [256], replicated, may hold values from -3 to 3
- weight_second: bfloat16 [3, 3, 3, 256, 256], replicated, may hold values from -0.078125 to 0.078125
- bias_second: float32 [256], replicated, may hold values from -3 to 3
Outputs:
- pooled_frames: bfloat16 [8, 16, 128, 256], P(('clips', 'tm'), 'tile'), parts along dimension 0
The draws below stay inside these ranges and needn't reach their ends.
There are 2 independent parts, one for each index of `clips`. The reference program is written for one: setup_inputs(seed, part) draws one part's arguments, and reference() takes and returns one part's arrays. A program takes and returns all parts, laid end to end along the dimension named above; an argument that names none is the same for every part. Nothing has to cross between parts.
All inputs are finite; a program needn't handle non-finite values.
Results may differ from the reference program's by a relative error of at most 0.0029.
Values may be sent and summed in bfloat16 or wider, within the bound.
No kernel may reach another device: no remote copies, remote signals or barrier semaphores. Data moves between devices by JAX's collectives and lax.ppermute only.
A program may use at most 128 MiB of HBM per device.

```python
import jax
import jax.numpy as jnp

C = 256
W = 128
NT = 8
H = 16


def shard_levels(key, dims, cuts, smallest, top_value):
    def one(position, shards_of):
        steps = jax.random.uniform(jax.random.fold_in(jax.random.fold_in(key, 6), position), (shards_of,), jnp.float32, smallest / len(cuts), top_value / len(cuts))
        return jnp.repeat(jnp.exp(steps), dims[position] // shards_of).reshape((-1,) + (1,) * (len(dims) - position - 1))

    gain = one(*cuts[0])
    for cut in cuts[1:]:
        gain = gain * one(*cut)
    return gain


def gaussian(key, shape, width, limit, split=(), held_as=jnp.bfloat16):
    entries = jax.random.normal(key, shape, jnp.float32) * width
    if len(split) > 0:
        entries = shard_levels(key, shape, split, -0.22, 0.18) * entries
    return jnp.clip(entries, min=-limit, max=limit).astype(held_as)


def setup_inputs(seed: int = 0, part: int = 0) -> dict:
    splits = jax.random.split(jax.random.key(seed), 6)
    own_keys = jax.random.split(jax.random.fold_in(splits[5], part), 6)
    return {
        "clip_frames": gaussian(own_keys[0], (NT, H, W, C), 1.0, 6.0, ((0, 4), (1, 4))),
        "weight_first": gaussian(splits[1], (3, 3, 3, C, C), (27 * C) ** -0.5, 0.078125),
        "bias_first": gaussian(splits[2], (C,), 0.5, 3.0, (), jnp.float32),
        "weight_second": gaussian(splits[3], (3, 3, 3, C, C), (27 * C) ** -0.5, 0.078125),
        "bias_second": gaussian(splits[4], (C,), 0.5, 3.0, (), jnp.float32),
    }


def causal_taps(padded_input, weight, bias):
    frame_count = padded_input.shape[0] - 2
    row_count = padded_input.shape[1] - 2
    width_cells = padded_input.shape[2]
    channels = padded_input.shape[3]
    widened = jnp.pad(padded_input, ((0, 0), (0, 0), (1, 1), (0, 0)))
    accumulated = jnp.zeros((frame_count, row_count, width_cells, channels), jnp.float32) + bias
    for depth_tap in range(3):
        for row_tap in range(3):
            slab_taps = jnp.concatenate([widened[depth_tap:depth_tap + frame_count, row_tap:row_tap + row_count, width_tap:width_tap + width_cells] for width_tap in range(3)], axis=-1)
            product = jnp.dot(slab_taps.reshape(-1, 3 * channels), weight[depth_tap, row_tap].reshape(3 * channels, channels), preferred_element_type=jnp.float32)
            accumulated = accumulated + product.reshape(frame_count, row_count, width_cells, channels)
    return accumulated


def reference(clip_frames, weight_first, bias_first, weight_second, bias_second):
    padded_input = jnp.pad(clip_frames, ((2, 0), (1, 1), (0, 0), (0, 0)))
    hidden = jax.nn.silu(causal_taps(padded_input, weight_first, bias_first)).astype(jnp.bfloat16)
    padded_hidden = jnp.pad(hidden, ((2, 0), (1, 1), (0, 0), (0, 0)))
    summed = clip_frames.astype(jnp.float32) + causal_taps(padded_hidden, weight_second, bias_second)
    return ((summed[0::2] + summed[1::2]) * 0.5).astype(jnp.bfloat16)
```

```python
import functools

import jax
import jax.numpy as jnp
from jax import lax
from jax.experimental import pallas as pl
from jax.experimental.pallas import tpu as pltpu
from jax.sharding import PartitionSpec as P


VMEM = pl.BlockSpec(memory_space=pltpu.VMEM)


def call(body, outs, args, flops):
    return pl.pallas_call(
        body,
        out_shape=outs,
        in_specs=[VMEM] * len(args),
        out_specs=[VMEM] * len(outs),
        compiler_params=pltpu.CompilerParams(vmem_limit_bytes=16 << 20),
        cost_estimate=pl.CostEstimate(flops=flops, bytes_accessed=0, transcendentals=0),
    )(*args)


def flat(value):
    return value.reshape(-1, value.shape[-1])


def row_taps(slab, rows):
    return [flat(slab[p : p + rows]) for p in range(3)]


def convolved(lhs, weights, rows, cols):
    stacked = jnp.concatenate(lhs, axis=1)
    total = None
    for q in range(3):
        taps = jnp.concatenate([w[q] for w in weights], axis=0)
        part = jnp.dot(stacked, taps, preferred_element_type=jnp.float32)
        part = part.reshape(rows, cols, part.shape[-1])
        if q != 1:
            col = lax.broadcasted_iota(jnp.int32, part.shape, 1)
            edge = 0 if q == 0 else cols - 1
            part = jnp.where(col == edge, 0.0, pltpu.roll(part, 1 if q == 0 else cols - 1, 1))
        total = part if total is None else total + part
    return total


def slab_of(main, inner, outer, parity):
    even = parity == 0
    up = jnp.where(even, outer, inner)
    down = jnp.where(even, inner, outer)
    return jnp.concatenate([up, main, down], axis=0)


def weight_rows(w_ref, a):
    return [[w_ref[a, p, q] for q in range(3)] for p in range(3)]


def silu_rows(value, tile, tiles):
    hidden = (value / (1.0 + jnp.exp(-value))).astype(jnp.bfloat16)
    row = lax.broadcasted_iota(jnp.int32, hidden.shape, 0)
    outside = ((row == 0) & (tile == 0)) | ((row == hidden.shape[0] - 1) & (tile == tiles - 1))
    return jnp.where(outside, jnp.zeros_like(hidden), hidden)


def own_body(x_ref, inner_ref, outer_ref, w_ref, b_ref, acc0_ref, acc1_ref):
    parity = lax.rem(lax.axis_index("tile"), 2)
    rows, cols = acc0_ref.shape[:2]
    slabs = [slab_of(x_ref[f], inner_ref[f], outer_ref[f], parity) for f in range(2)]
    taps = [row_taps(slab, rows) for slab in slabs]
    bias = b_ref[...]
    acc0_ref[...] = bias + convolved(taps[0], weight_rows(w_ref, 2), rows, cols)
    acc1_ref[...] = bias + convolved(
        taps[0] + taps[1], weight_rows(w_ref, 1) + weight_rows(w_ref, 2), rows, cols
    )


def late_body(tiles, m_ref, inner_ref, outer_ref, w_ref, acc0_ref, acc1_ref, sum0_ref, h1_ref):
    tile = lax.axis_index("tile")
    rows, cols = acc0_ref.shape[:2]
    taps = row_taps(slab_of(m_ref[0], inner_ref[0], outer_ref[1], lax.rem(tile, 2)), rows)
    acc1 = acc1_ref[...] + convolved(taps, weight_rows(w_ref, 0), rows, cols)
    h1_ref[...] = silu_rows(acc1, tile, tiles)
    sum0_ref[...] = acc0_ref[...] + convolved(taps, weight_rows(w_ref, 1), rows, cols)


def early_body(
    tiles, m_ref, inner_ref, outer_ref, w_ref, v_ref, sum0_ref, h1_ref, part_ref, h0_ref, both_ref
):
    tile = lax.axis_index("tile")
    rows, cols = sum0_ref.shape[:2]
    taps = row_taps(slab_of(m_ref[0], inner_ref[0], outer_ref[0], lax.rem(tile, 2)), rows)
    acc0 = sum0_ref[...] + convolved(taps, weight_rows(w_ref, 0), rows, cols)
    h0 = silu_rows(acc0, tile, tiles)
    h1 = h1_ref[...]
    both = (h0.astype(jnp.float32) + h1.astype(jnp.float32)).astype(jnp.bfloat16)
    h0_ref[...] = h0
    both_ref[...] = both
    lhs = row_taps(both, rows - 2) + row_taps(h1, rows - 2)
    part = convolved(lhs, weight_rows(v_ref, 0) + weight_rows(v_ref, 1), rows - 2, cols)
    part_ref[0] = part.astype(jnp.bfloat16)


def rest_body(x_ref, h0_ref, both_ref, v_ref, b_ref, rest_ref):
    rows, cols = x_ref.shape[1:3]
    lhs = row_taps(h0_ref[...], rows) + row_taps(both_ref[...], rows)
    part = convolved(lhs, weight_rows(v_ref, 1) + weight_rows(v_ref, 2), rows, cols)
    mean = x_ref[0].astype(jnp.float32) + x_ref[1].astype(jnp.float32) + part
    rest_ref[0] = mean * 0.5 + b_ref[...]


def shards(x, weight_first, bias_first, weight_second, bias_second):
    _, rows, cols, channels = x.shape
    tiles, times = lax.axis_size("tile"), lax.axis_size("tm")
    even = lax.rem(lax.axis_index("tile"), 2) == 0

    def edges(value):
        top, bottom = value[:, :2], value[:, rows - 2 :]
        return jnp.where(even, bottom, top), jnp.where(even, top, bottom)

    forward = [(i, i + 1) for i in range(times - 1)]
    inner_pairs = [(i, i + 1) for i in range(0, tiles - 1, 2)]
    outer_pairs = [(i, i + 1) for i in range(1, tiles - 1, 2)]
    inner_pairs += [(j, i) for i, j in inner_pairs]
    outer_pairs += [(j, i) for i, j in outer_pairs]
    diagonal = [(i * times + s, j * times + t) for i, j in outer_pairs for s, t in forward]

    inner_edge, outer_edge = edges(x)
    late = lax.ppermute(x[1:2], "tm", forward)
    outer = lax.ppermute(outer_edge, "tile", outer_pairs)
    inner = lax.ppermute(inner_edge, "tile", inner_pairs)
    corner = lax.ppermute(outer_edge, ("tile", "tm"), diagonal)
    early = lax.ppermute(x[0:1], "tm", forward)
    late_inner = lax.ppermute(edges(late)[0], "tile", inner_pairs)
    early_inner = lax.ppermute(edges(early)[0], "tile", inner_pairs)

    wide = (rows + 2, cols, channels)
    f32 = jax.ShapeDtypeStruct(wide, jnp.float32)
    bf16 = jax.ShapeDtypeStruct(wide, jnp.bfloat16)
    bias_first = bias_first.reshape(1, 1, -1)
    bias_second = bias_second.reshape(1, 1, -1)
    unit = 2 * 9 * channels * channels * cols
    acc0, acc1 = call(
        own_body, [f32, f32], (x, inner, outer, weight_first, bias_first), 3 * unit * (rows + 2)
    )
    sum0, h1 = call(
        functools.partial(late_body, tiles),
        [f32, bf16],
        (late, late_inner, corner, weight_first, acc0, acc1),
        2 * unit * (rows + 2),
    )
    part, h0, both = call(
        functools.partial(early_body, tiles),
        [jax.ShapeDtypeStruct((1, rows, cols, channels), jnp.bfloat16), bf16, bf16],
        (early, early_inner, corner, weight_first, weight_second, sum0, h1),
        unit * (3 * rows + 2),
    )
    before = lax.ppermute(part, "tm", forward)
    (rest,) = call(
        rest_body,
        [jax.ShapeDtypeStruct((1, rows, cols, channels), jnp.float32)],
        (x, h0, both, weight_second, bias_second),
        2 * unit * rows,
    )
    return (rest + 0.5 * before.astype(jnp.float32)).astype(jnp.bfloat16)


def solution(mesh):
    in_specs = (P(("clips", "tm"), "tile", None, None), P(), P(), P(), P())
    out_specs = P(("clips", "tm"), "tile", None, None)
    return jax.shard_map(shards, mesh=mesh, in_specs=in_specs, out_specs=out_specs, check_vma=False)
```

```python
import functools

import jax
import jax.numpy as jnp
from jax import lax
from jax.experimental import pallas as pl
from jax.experimental.pallas import tpu as pltpu
from jax.sharding import PartitionSpec as P


VMEM = pl.BlockSpec(memory_space=pltpu.VMEM)
HBM = pl.BlockSpec(memory_space=pltpu.HBM)


def call(body, outs, args, flops, in_specs=None, scratch=()):
    return pl.pallas_call(
        body,
        out_shape=outs,
        in_specs=in_specs or [VMEM] * len(args),
        out_specs=[VMEM] * len(outs),
        scratch_shapes=scratch,
        compiler_params=pltpu.CompilerParams(vmem_limit_bytes=16 << 20),
        cost_estimate=pl.CostEstimate(flops=flops, bytes_accessed=0, transcendentals=0),
    )(*args)


def flat(value):
    return value.reshape(-1, value.shape[-1])


def row_taps(slab, rows):
    return [flat(slab[p : p + rows]) for p in range(3)]


def convolved(lhs, weights, rows, cols):
    stacked = jnp.concatenate(lhs, axis=1)
    total = None
    for q in range(3):
        taps = jnp.concatenate([w[q] for w in weights], axis=0)
        part = jnp.dot(stacked, taps, preferred_element_type=jnp.float32)
        part = part.reshape(rows, cols, part.shape[-1])
        if q != 1:
            col = lax.broadcasted_iota(jnp.int32, part.shape, 1)
            edge = 0 if q == 0 else cols - 1
            part = jnp.where(col == edge, 0.0, pltpu.roll(part, 1 if q == 0 else cols - 1, 1))
        total = part if total is None else total + part
    return total


def parity():
    return lax.rem(lax.axis_index("tile"), 2)


def slab_of(outer, outer_half, inner_half, inner):
    even = parity() == 0
    blocks = [(outer, inner), (outer_half, inner_half), (inner_half, outer_half), (inner, outer)]
    return jnp.concatenate([jnp.where(even, a, b) for a, b in blocks], axis=0)


def own_slab(x, outer, inner):
    even = parity() == 0
    up, down = jnp.where(even, outer, inner), jnp.where(even, inner, outer)
    return jnp.concatenate([up, x, down], axis=0)


def weight_rows(w_ref, a):
    return [[w_ref[a, p, q] for q in range(3)] for p in range(3)]


def silu_rows(value, tiles):
    tile = lax.axis_index("tile")
    hidden = (value / (1.0 + jnp.exp(-value))).astype(jnp.bfloat16)
    row = lax.broadcasted_iota(jnp.int32, hidden.shape, 0)
    outside = ((row == 0) & (tile == 0)) | ((row == hidden.shape[0] - 1) & (tile == tiles - 1))
    return jnp.where(outside, jnp.zeros_like(hidden), hidden)


def pick_body(x_ref, own_ref, first_ref, second_ref, outer_ref, inner_ref, sems):
    rows = x_ref.shape[1]
    half = rows // 2
    odd = parity()
    outer_half, inner_half = pl.ds(odd * half, half), pl.ds((1 - odd) * half, half)
    outer, inner = pl.ds(odd * (rows - 2), 2), pl.ds((1 - odd) * (rows - 2), 2)
    moves = [
        (x_ref.at[1, outer_half], first_ref.at[pl.ds(0, half)]),
        (x_ref.at[1, inner_half], first_ref.at[pl.ds(half, half)]),
        (x_ref.at[0, inner_half], first_ref.at[pl.ds(2 * half, half)]),
        (x_ref.at[0, outer_half], second_ref),
        (x_ref.at[:, outer], outer_ref),
        (x_ref.at[:, inner], inner_ref),
        (x_ref, own_ref),
    ]
    copies = [pltpu.make_async_copy(a, b, sems.at[i]) for i, (a, b) in enumerate(moves)]
    for copy in copies:
        copy.start()
    for copy in copies:
        copy.wait()


def own1_body(x_ref, outer_ref, inner_ref, w_ref, b_ref, acc_ref):
    rows, cols = acc_ref.shape[:2]
    taps = []
    for f in range(2):
        taps += row_taps(own_slab(x_ref[f], outer_ref[f], inner_ref[f]), rows)
    weights = weight_rows(w_ref, 1) + weight_rows(w_ref, 2)
    acc_ref[...] = b_ref[...] + convolved(taps, weights, rows, cols)


def own0_body(x_ref, outer_ref, inner_ref, w_ref, b_ref, acc_ref):
    rows, cols = acc_ref.shape[:2]
    taps = row_taps(own_slab(x_ref[0], outer_ref[0], inner_ref[0]), rows)
    acc_ref[...] = b_ref[...] + convolved(taps, weight_rows(w_ref, 2), rows, cols)


def late_body(
    tiles, first_ref, inner_ref, outer_ref, w_ref, v_ref, acc0_ref, acc1_ref,
    sum0_ref, part_ref, rest_ref,
):
    rows, cols = acc0_ref.shape[:2]
    half = (rows - 2) // 2
    slab = slab_of(outer_ref[1], first_ref[:half], first_ref[half : 2 * half], inner_ref[0])
    taps = row_taps(slab, rows)
    acc1 = acc1_ref[...] + convolved(taps, weight_rows(w_ref, 0), rows, cols)
    h1 = silu_rows(acc1, tiles)
    sum0_ref[...] = acc0_ref[...] + convolved(taps, weight_rows(w_ref, 1), rows, cols)
    taps = row_taps(h1, rows - 2)
    part_ref[...] = convolved(
        taps + taps, weight_rows(v_ref, 0) + weight_rows(v_ref, 1), rows - 2, cols
    )
    rest_ref[...] = convolved(taps, weight_rows(v_ref, 2), rows - 2, cols)


def early_body(
    tiles, first_ref, second_ref, inner_ref, outer_ref, w_ref, v_ref, sum0_ref, part_ref,
    send_ref, h0_ref,
):
    rows, cols = sum0_ref.shape[:2]
    half = (rows - 2) // 2
    slab = slab_of(outer_ref[0], second_ref[...], first_ref[2 * half :], inner_ref[1])
    acc0 = sum0_ref[...] + convolved(row_taps(slab, rows), weight_rows(w_ref, 0), rows, cols)
    h0 = silu_rows(acc0, tiles)
    h0_ref[...] = h0
    part = part_ref[...] + convolved(
        row_taps(h0, rows - 2), weight_rows(v_ref, 0), rows - 2, cols
    )
    send_ref[0] = part.astype(jnp.bfloat16)


def rest_body(x_ref, h0_ref, rest_ref, v_ref, b_ref, out_ref):
    rows, cols = x_ref.shape[1:3]
    taps = row_taps(h0_ref[...], rows)
    part = rest_ref[...] + convolved(
        taps + taps, weight_rows(v_ref, 1) + weight_rows(v_ref, 2), rows, cols
    )
    both = x_ref[0].astype(jnp.float32) + x_ref[1].astype(jnp.float32)
    out_ref[0] = (both + part) * 0.5 + b_ref[...]


def block(x, weight_first, bias_first, weight_second, bias_second):
    _, rows, cols, channels = x.shape
    half = rows // 2
    tiles, times = lax.axis_size("tile"), lax.axis_size("tm")
    forward = [(i, i + 1) for i in range(times - 1)]
    inner_pairs = [(i, i + 1) for i in range(0, tiles - 1, 2)]
    outer_pairs = [(i, i + 1) for i in range(1, tiles - 1, 2)]
    inner_pairs += [(j, i) for i, j in inner_pairs]
    outer_pairs += [(j, i) for i, j in outer_pairs]
    diagonal = [(i * times + s, j * times + t) for i, j in outer_pairs for s, t in forward]

    def frames(*lead, dtype=jnp.bfloat16):
        return jax.ShapeDtypeStruct((*lead, cols, channels), dtype)

    f32 = jnp.float32
    own, first, second, outer_edge, inner_edge = call(
        pick_body,
        [frames(2, rows), frames(3 * half), frames(half), frames(2, 2), frames(2, 2)],
        (x,),
        10**10,
        in_specs=[HBM],
        scratch=[pltpu.SemaphoreType.DMA((7,))],
    )
    first = lax.ppermute(first, "tm", forward)
    outer = lax.ppermute(outer_edge, "tile", outer_pairs)
    inner = lax.ppermute(inner_edge, "tile", inner_pairs)
    corner = lax.ppermute(outer_edge, ("tile", "tm"), diagonal)
    second = lax.ppermute(second, "tm", forward)

    bias_first = bias_first.reshape(1, 1, -1)
    bias_second = bias_second.reshape(1, 1, -1)
    unit = 2 * 9 * channels * channels * cols
    wide = rows + 2
    (acc1,) = call(
        own1_body,
        [frames(wide, dtype=f32)],
        (own, outer, inner, weight_first, bias_first),
        2 * unit * wide,
    )
    (acc0,) = call(
        own0_body,
        [frames(wide, dtype=f32)],
        (own, outer, inner, weight_first, bias_first),
        unit * wide,
    )
    even = lax.rem(lax.axis_index("tile"), 2) == 0
    late_half, early_half = first[half : 2 * half], first[2 * half :]
    halves = jnp.stack([late_half, early_half])
    inner_corner = lax.ppermute(
        jnp.where(even, halves[:, half - 2 :], halves[:, :2]), "tile", inner_pairs
    )
    sum0, part, rest = call(
        functools.partial(late_body, tiles),
        [frames(wide, dtype=f32), frames(rows, dtype=f32), frames(rows, dtype=f32)],
        (first, inner_corner, corner, weight_first, weight_second, acc0, acc1),
        unit * (2 * wide + 3 * rows),
    )
    send, h0 = call(
        functools.partial(early_body, tiles),
        [frames(1, rows), frames(wide)],
        (first, second, inner_corner, corner, weight_first, weight_second, sum0, part),
        unit * (rows + wide),
    )
    before = lax.ppermute(send, "tm", forward)
    (rest,) = call(
        rest_body,
        [frames(1, rows, dtype=f32)],
        (own, h0, rest, weight_second, bias_second),
        2 * unit * rows,
    )
    return (rest + 0.5 * before.astype(f32)).astype(jnp.bfloat16)


def solution(mesh):
    in_specs = (P(("clips", "tm"), "tile", None, None), P(), P(), P(), P())
    out_specs = P(("clips", "tm"), "tile", None, None)
    return jax.shard_map(block, mesh=mesh, in_specs=in_specs, out_specs=out_specs, check_vma=False)
```

```python
import functools

import jax
import jax.numpy as jnp
from jax import lax
from jax.experimental import pallas as pl
from jax.experimental.pallas import tpu as pltpu
from jax.sharding import PartitionSpec as P


VMEM = pl.BlockSpec(memory_space=pltpu.VMEM)
HBM = pl.BlockSpec(memory_space=pltpu.HBM)


def call(body, outs, args, flops, in_specs=None, scratch=()):
    return pl.pallas_call(
        body,
        out_shape=outs,
        in_specs=in_specs or [VMEM] * len(args),
        out_specs=[VMEM] * len(outs),
        scratch_shapes=scratch,
        compiler_params=pltpu.CompilerParams(vmem_limit_bytes=16 << 20),
        cost_estimate=pl.CostEstimate(flops=flops, bytes_accessed=0, transcendentals=0),
    )(*args)


def flat(value):
    return value.reshape(-1, value.shape[-1])


def row_taps(slab, rows):
    return [flat(slab[p : p + rows]) for p in range(3)]


def convolved(lhs, weights, rows, cols):
    stacked = jnp.concatenate(lhs, axis=1)
    total = None
    for q in range(3):
        taps = jnp.concatenate([w[q] for w in weights], axis=0)
        part = jnp.dot(stacked, taps, preferred_element_type=jnp.float32)
        part = part.reshape(rows, cols, part.shape[-1])
        if q != 1:
            col = lax.broadcasted_iota(jnp.int32, part.shape, 1)
            edge = 0 if q == 0 else cols - 1
            part = jnp.where(col == edge, 0.0, pltpu.roll(part, 1 if q == 0 else cols - 1, 1))
        total = part if total is None else total + part
    return total


def parity():
    return lax.rem(lax.axis_index("tile"), 2)


def slab_of(outer, outer_half, inner_half, inner):
    even = parity() == 0
    blocks = [(outer, inner), (outer_half, inner_half), (inner_half, outer_half), (inner, outer)]
    return jnp.concatenate([jnp.where(even, a, b) for a, b in blocks], axis=0)


def own_slab(x, outer, inner):
    even = parity() == 0
    up, down = jnp.where(even, outer, inner), jnp.where(even, inner, outer)
    return jnp.concatenate([up, x, down], axis=0)


def weight_rows(w_ref, a):
    return [[w_ref[a, p, q] for q in range(3)] for p in range(3)]


def silu_rows(value, tiles):
    tile = lax.axis_index("tile")
    hidden = (value / (1.0 + jnp.exp(-value))).astype(jnp.bfloat16)
    row = lax.broadcasted_iota(jnp.int32, hidden.shape, 0)
    outside = ((row == 0) & (tile == 0)) | ((row == hidden.shape[0] - 1) & (tile == tiles - 1))
    return jnp.where(outside, jnp.zeros_like(hidden), hidden)


def pick_body(x_ref, own_ref, first_ref, second_ref, outer_ref, inner_ref, sems):
    rows = x_ref.shape[1]
    half = rows // 2
    odd = parity()
    outer_half, inner_half = pl.ds(odd * half, half), pl.ds((1 - odd) * half, half)
    outer, inner = pl.ds(odd * (rows - 2), 2), pl.ds((1 - odd) * (rows - 2), 2)
    moves = [
        (x_ref.at[1, outer_half], first_ref.at[pl.ds(0, half)]),
        (x_ref.at[1, inner_half], first_ref.at[pl.ds(half, half)]),
        (x_ref.at[0, inner_half], first_ref.at[pl.ds(2 * half, half)]),
        (x_ref.at[0, outer_half], second_ref),
        (x_ref.at[:, outer], outer_ref),
        (x_ref.at[:, inner], inner_ref),
        (x_ref, own_ref),
    ]
    copies = [pltpu.make_async_copy(a, b, sems.at[i]) for i, (a, b) in enumerate(moves)]
    for copy in copies:
        copy.start()
    for copy in copies:
        copy.wait()


def own1_body(x_ref, outer_ref, inner_ref, w_ref, b_ref, acc_ref):
    rows, cols = acc_ref.shape[:2]
    taps = []
    for f in range(2):
        taps += row_taps(own_slab(x_ref[f], outer_ref[f], inner_ref[f]), rows)
    weights = weight_rows(w_ref, 1) + weight_rows(w_ref, 2)
    acc_ref[...] = b_ref[...] + convolved(taps, weights, rows, cols)


def own0_body(x_ref, outer_ref, inner_ref, w_ref, b_ref, acc_ref):
    rows, cols = acc_ref.shape[:2]
    taps = row_taps(own_slab(x_ref[0], outer_ref[0], inner_ref[0]), rows)
    acc_ref[...] = b_ref[...] + convolved(taps, weight_rows(w_ref, 2), rows, cols)


def late_body(
    tiles, first_ref, inner_ref, outer_ref, w_ref, v_ref, acc0_ref, acc1_ref,
    sum0_ref, part_ref, h1_ref,
):
    rows, cols = acc0_ref.shape[:2]
    half = (rows - 2) // 2
    slab = slab_of(outer_ref[1], first_ref[:half], first_ref[half : 2 * half], inner_ref[0])
    taps = row_taps(slab, rows)
    acc1 = acc1_ref[...] + convolved(taps, weight_rows(w_ref, 0), rows, cols)
    h1 = silu_rows(acc1, tiles)
    h1_ref[...] = h1
    sum0_ref[...] = acc0_ref[...] + convolved(taps, weight_rows(w_ref, 1), rows, cols)
    taps = row_taps(h1, rows - 2)
    part_ref[...] = convolved(
        taps + taps, weight_rows(v_ref, 0) + weight_rows(v_ref, 1), rows - 2, cols
    )


def early_body(
    tiles, first_ref, second_ref, inner_ref, outer_ref, w_ref, v_ref, sum0_ref, part_ref,
    send_ref, h0_ref,
):
    rows, cols = sum0_ref.shape[:2]
    half = (rows - 2) // 2
    slab = slab_of(outer_ref[0], second_ref[...], first_ref[2 * half :], inner_ref[1])
    acc0 = sum0_ref[...] + convolved(row_taps(slab, rows), weight_rows(w_ref, 0), rows, cols)
    h0 = silu_rows(acc0, tiles)
    h0_ref[...] = h0
    part = part_ref[...] + convolved(
        row_taps(h0, rows - 2), weight_rows(v_ref, 0), rows - 2, cols
    )
    send_ref[0] = part.astype(jnp.bfloat16)


def rest_body(x_ref, h0_ref, h1_ref, v_ref, b_ref, out_ref):
    rows, cols = x_ref.shape[1:3]
    taps = row_taps(h0_ref[...], rows)
    weights = weight_rows(v_ref, 1) + 2 * weight_rows(v_ref, 2)
    part = convolved(taps + taps + row_taps(h1_ref[...], rows), weights, rows, cols)
    both = x_ref[0].astype(jnp.float32) + x_ref[1].astype(jnp.float32)
    out_ref[0] = (both + part) * 0.5 + b_ref[...]


def block(x, weight_first, bias_first, weight_second, bias_second):
    _, rows, cols, channels = x.shape
    half = rows // 2
    tiles, times = lax.axis_size("tile"), lax.axis_size("tm")
    forward = [(i, i + 1) for i in range(times - 1)]
    inner_pairs = [(i, i + 1) for i in range(0, tiles - 1, 2)]
    outer_pairs = [(i, i + 1) for i in range(1, tiles - 1, 2)]
    inner_pairs += [(j, i) for i, j in inner_pairs]
    outer_pairs += [(j, i) for i, j in outer_pairs]
    diagonal = [(i * times + s, j * times + t) for i, j in outer_pairs for s, t in forward]

    def frames(*lead, dtype=jnp.bfloat16):
        return jax.ShapeDtypeStruct((*lead, cols, channels), dtype)

    f32 = jnp.float32
    own, first, second, outer_edge, inner_edge = call(
        pick_body,
        [frames(2, rows), frames(3 * half), frames(half), frames(2, 2), frames(2, 2)],
        (pltpu.with_memory_space_constraint(x, pltpu.HBM),),
        10**10,
        in_specs=[HBM],
        scratch=[pltpu.SemaphoreType.DMA((7,))],
    )
    first = lax.ppermute(first, "tm", forward)
    outer = lax.ppermute(outer_edge, "tile", outer_pairs)
    inner = lax.ppermute(inner_edge, "tile", inner_pairs)
    corner = lax.ppermute(outer_edge, ("tile", "tm"), diagonal)
    second = lax.ppermute(second, "tm", forward)

    bias_first = bias_first.reshape(1, 1, -1)
    bias_second = bias_second.reshape(1, 1, -1)
    unit = 2 * 9 * channels * channels * cols
    wide = rows + 2
    (acc1,) = call(
        own1_body,
        [frames(wide, dtype=f32)],
        (own, outer, inner, weight_first, bias_first),
        2 * unit * wide,
    )
    (acc0,) = call(
        own0_body,
        [frames(wide, dtype=f32)],
        (own, outer, inner, weight_first, bias_first),
        unit * wide,
    )
    even = lax.rem(lax.axis_index("tile"), 2) == 0
    late_half, early_half = first[half : 2 * half], first[2 * half :]
    halves = jnp.stack([late_half, early_half])
    inner_corner = lax.ppermute(
        jnp.where(even, halves[:, half - 2 :], halves[:, :2]), "tile", inner_pairs
    )
    sum0, part, h1 = call(
        functools.partial(late_body, tiles),
        [frames(wide, dtype=f32), frames(rows, dtype=f32), frames(wide)],
        (first, inner_corner, corner, weight_first, weight_second, acc0, acc1),
        unit * 2 * (wide + rows),
    )
    send, h0 = call(
        functools.partial(early_body, tiles),
        [frames(1, rows), frames(wide)],
        (first, second, inner_corner, corner, weight_first, weight_second, sum0, part),
        unit * (rows + wide),
    )
    before = lax.ppermute(send, "tm", forward)
    (rest,) = call(
        rest_body,
        [frames(1, rows, dtype=f32)],
        (own, h0, h1, weight_second, bias_second),
        3 * unit * rows,
    )
    return (rest + 0.5 * before.astype(f32)).astype(jnp.bfloat16)


def solution(mesh):
    in_specs = (P(("clips", "tm"), "tile", None, None), P(), P(), P(), P())
    out_specs = P(("clips", "tm"), "tile", None, None)
    return jax.shard_map(block, mesh=mesh, in_specs=in_specs, out_specs=out_specs, check_vma=False)
```

```python
import functools

import jax
import jax.numpy as jnp
from jax import lax
from jax.experimental import pallas as pl
from jax.experimental.pallas import tpu as pltpu
from jax.sharding import PartitionSpec as P


VMEM = pl.BlockSpec(memory_space=pltpu.VMEM)
HBM = pl.BlockSpec(memory_space=pltpu.HBM)


def call(body, outs, args, flops, in_specs=None, scratch=()):
    return pl.pallas_call(
        body,
        out_shape=outs,
        in_specs=in_specs or [VMEM] * len(args),
        out_specs=[VMEM] * len(outs),
        scratch_shapes=scratch,
        compiler_params=pltpu.CompilerParams(vmem_limit_bytes=16 << 20),
        cost_estimate=pl.CostEstimate(flops=flops, bytes_accessed=0, transcendentals=0),
    )(*args)


def flat(value):
    return value.reshape(-1, value.shape[-1])


def row_taps(slab, rows):
    return [flat(slab[p : p + rows]) for p in range(3)]


def convolved(lhs, weights, rows, cols):
    stacked = jnp.concatenate(lhs, axis=1)
    total = None
    for q in range(3):
        taps = jnp.concatenate([w[q] for w in weights], axis=0)
        part = jnp.dot(stacked, taps, preferred_element_type=jnp.float32)
        part = part.reshape(rows, cols, part.shape[-1])
        if q != 1:
            col = lax.broadcasted_iota(jnp.int32, part.shape, 1)
            edge = 0 if q == 0 else cols - 1
            part = jnp.where(col == edge, 0.0, pltpu.roll(part, 1 if q == 0 else cols - 1, 1))
        total = part if total is None else total + part
    return total


def parity():
    return lax.rem(lax.axis_index("tile"), 2)


def bounded(up, main, down, tiles):
    tile = lax.axis_index("tile")
    up = jnp.where(tile == 0, jnp.zeros_like(up), up)
    down = jnp.where(tile == tiles - 1, jnp.zeros_like(down), down)
    return jnp.concatenate([up, *main, down], axis=0)


def slab_of(outer, outer_half, inner_half, inner, tiles):
    even = parity() == 0
    main = [jnp.where(even, outer_half, inner_half), jnp.where(even, inner_half, outer_half)]
    up, down = jnp.where(even, outer, inner), jnp.where(even, inner, outer)
    slab = bounded(up, main, down, tiles)
    return jnp.where(lax.axis_index("tm") == 0, jnp.zeros_like(slab), slab)


def own_slab(x, outer, inner, tiles):
    even = parity() == 0
    up, down = jnp.where(even, outer, inner), jnp.where(even, inner, outer)
    return bounded(up, [x], down, tiles)


def weight_rows(w_ref, a):
    return [[w_ref[a, p, q] for q in range(3)] for p in range(3)]


def silu_rows(value, tiles):
    tile = lax.axis_index("tile")
    hidden = (value / (1.0 + jnp.exp(-value))).astype(jnp.bfloat16)
    row = lax.broadcasted_iota(jnp.int32, hidden.shape, 0)
    outside = ((row == 0) & (tile == 0)) | ((row == hidden.shape[0] - 1) & (tile == tiles - 1))
    return jnp.where(outside, jnp.zeros_like(hidden), hidden)


def move(pairs, sems):
    copies = [pltpu.make_async_copy(a, b, sems.at[i]) for i, (a, b) in enumerate(pairs)]
    for copy in copies:
        copy.start()
    for copy in copies:
        copy.wait()


def halves_of(rows):
    half, odd = rows // 2, parity()
    return pl.ds(odd * half, half), pl.ds((1 - odd) * half, half)


def cut_body(x_ref, first_ref, sems):
    half = x_ref.shape[1] // 2
    outer, inner = halves_of(2 * half)
    pairs = [
        (x_ref.at[1, outer], first_ref.at[pl.ds(0, half)]),
        (x_ref.at[1, inner], first_ref.at[pl.ds(half, half)]),
        (x_ref.at[0, inner], first_ref.at[pl.ds(2 * half, half)]),
    ]
    move(pairs, sems)


def pick_body(x_ref, own_ref, second_ref, outer_ref, inner_ref, sems):
    rows = x_ref.shape[1]
    odd = parity()
    outer, inner = pl.ds(odd * (rows - 2), 2), pl.ds((1 - odd) * (rows - 2), 2)
    pairs = [
        (x_ref.at[:, outer], outer_ref),
        (x_ref.at[:, inner], inner_ref),
        (x_ref.at[0, halves_of(rows)[0]], second_ref),
        (x_ref, own_ref),
    ]
    move(pairs, sems)


def own1_body(tiles, x_ref, outer_ref, inner_ref, w_ref, b_ref, acc_ref):
    rows, cols = acc_ref.shape[:2]
    taps = []
    for f in range(2):
        taps += row_taps(own_slab(x_ref[f], outer_ref[f], inner_ref[f], tiles), rows)
    weights = weight_rows(w_ref, 1) + weight_rows(w_ref, 2)
    acc_ref[...] = b_ref[...] + convolved(taps, weights, rows, cols)


def own0_body(tiles, x_ref, outer_ref, inner_ref, w_ref, b_ref, acc_ref):
    rows, cols = acc_ref.shape[:2]
    taps = row_taps(own_slab(x_ref[0], outer_ref[0], inner_ref[0], tiles), rows)
    acc_ref[...] = b_ref[...] + convolved(taps, weight_rows(w_ref, 2), rows, cols)


def late_body(
    tiles, first_ref, inner_ref, outer_ref, w_ref, v_ref, acc0_ref, acc1_ref,
    sum0_ref, part_ref, h1_ref,
):
    rows, cols = acc0_ref.shape[:2]
    half = (rows - 2) // 2
    slab = slab_of(outer_ref[1], first_ref[:half], first_ref[half : 2 * half], inner_ref[0], tiles)
    taps = row_taps(slab, rows)
    acc1 = acc1_ref[...] + convolved(taps, weight_rows(w_ref, 0), rows, cols)
    h1 = silu_rows(acc1, tiles)
    h1_ref[...] = h1
    sum0_ref[...] = acc0_ref[...] + convolved(taps, weight_rows(w_ref, 1), rows, cols)
    taps = row_taps(h1, rows - 2)
    part_ref[...] = convolved(
        taps + taps, weight_rows(v_ref, 0) + weight_rows(v_ref, 1), rows - 2, cols
    )


def early_body(
    tiles, first_ref, second_ref, inner_ref, outer_ref, w_ref, v_ref, sum0_ref, part_ref,
    send_ref, h0_ref,
):
    rows, cols = sum0_ref.shape[:2]
    half = (rows - 2) // 2
    slab = slab_of(outer_ref[0], second_ref[...], first_ref[2 * half :], inner_ref[1], tiles)
    acc0 = sum0_ref[...] + convolved(row_taps(slab, rows), weight_rows(w_ref, 0), rows, cols)
    h0 = silu_rows(acc0, tiles)
    h0_ref[...] = h0
    part = part_ref[...] + convolved(
        row_taps(h0, rows - 2), weight_rows(v_ref, 0), rows - 2, cols
    )
    send_ref[0] = part.astype(jnp.bfloat16)


def rest_body(x_ref, h0_ref, h1_ref, v_ref, b_ref, out_ref):
    rows, cols = x_ref.shape[1:3]
    taps = row_taps(h0_ref[...], rows)
    weights = weight_rows(v_ref, 1) + 2 * weight_rows(v_ref, 2)
    part = convolved(taps + taps + row_taps(h1_ref[...], rows), weights, rows, cols)
    both = x_ref[0].astype(jnp.float32) + x_ref[1].astype(jnp.float32)
    out_ref[0] = (both + part) * 0.5 + b_ref[...]


def block(x, weight_first, bias_first, weight_second, bias_second):
    _, rows, cols, channels = x.shape
    half = rows // 2
    tiles, times = lax.axis_size("tile"), lax.axis_size("tm")
    forward = [(i, i + 1) for i in range(times - 1)]
    ring = forward + [(times - 1, 0)]
    inner_pairs = [(i, i + 1) for i in range(0, tiles - 1, 2)]
    outer_pairs = [(i, i + 1) for i in range(1, tiles - 1, 2)]
    inner_pairs += [(j, i) for i, j in inner_pairs]
    outer_pairs += [(j, i) for i, j in outer_pairs]
    unpaired = [(0, tiles - 1), (tiles - 1, 0)] if tiles % 2 == 0 else []
    diagonal = [(i * times + s, j * times + t) for i, j in outer_pairs for s, t in forward]

    def frames(*lead, dtype=jnp.bfloat16):
        return jax.ShapeDtypeStruct((*lead, cols, channels), dtype)

    f32 = jnp.float32
    x_hbm = pltpu.with_memory_space_constraint(x, pltpu.HBM)
    (first,) = call(
        cut_body,
        [frames(3 * half)],
        (x_hbm,),
        0,
        in_specs=[HBM],
        scratch=[pltpu.SemaphoreType.DMA((3,))],
    )
    own, second, outer_edge, inner_edge = call(
        pick_body,
        [frames(2, rows), frames(half), frames(2, 2), frames(2, 2)],
        (x_hbm,),
        10**10,
        in_specs=[HBM],
        scratch=[pltpu.SemaphoreType.DMA((4,))],
    )
    first = lax.ppermute(first, "tm", ring)
    outer = lax.ppermute(outer_edge, "tile", outer_pairs + unpaired)
    inner = lax.ppermute(inner_edge, "tile", inner_pairs)
    corner = lax.ppermute(outer_edge, ("tile", "tm"), diagonal)
    second = lax.ppermute(second, "tm", ring)

    bias_first = bias_first.reshape(1, 1, -1)
    bias_second = bias_second.reshape(1, 1, -1)
    unit = 2 * 9 * channels * channels * cols
    wide = rows + 2
    (acc1,) = call(
        functools.partial(own1_body, tiles),
        [frames(wide, dtype=f32)],
        (own, outer, inner, weight_first, bias_first),
        2 * unit * wide,
    )
    (acc0,) = call(
        functools.partial(own0_body, tiles),
        [frames(wide, dtype=f32)],
        (own, outer, inner, weight_first, bias_first),
        unit * wide,
    )
    even = lax.rem(lax.axis_index("tile"), 2) == 0
    late_half, early_half = first[half : 2 * half], first[2 * half :]
    halves = jnp.stack([late_half, early_half])
    inner_corner = lax.ppermute(
        jnp.where(even, halves[:, half - 2 :], halves[:, :2]), "tile", inner_pairs
    )
    sum0, part, h1 = call(
        functools.partial(late_body, tiles),
        [frames(wide, dtype=f32), frames(rows, dtype=f32), frames(wide)],
        (first, inner_corner, corner, weight_first, weight_second, acc0, acc1),
        unit * 2 * (wide + rows),
    )
    send, h0 = call(
        functools.partial(early_body, tiles),
        [frames(1, rows), frames(wide)],
        (first, second, inner_corner, corner, weight_first, weight_second, sum0, part),
        unit * (rows + wide),
    )
    before = lax.ppermute(send, "tm", forward)
    (rest,) = call(
        rest_body,
        [frames(1, rows, dtype=f32)],
        (own, h0, h1, weight_second, bias_second),
        3 * unit * rows,
    )
    return (rest + 0.5 * before.astype(f32)).astype(jnp.bfloat16)


def solution(mesh):
    in_specs = (P(("clips", "tm"), "tile", None, None), P(), P(), P(), P())
    out_specs = P(("clips", "tm"), "tile", None, None)
    return jax.shard_map(block, mesh=mesh, in_specs=in_specs, out_specs=out_specs, check_vma=False)
```

```python
import functools

import jax
import jax.numpy as jnp
from jax import lax
from jax.experimental import pallas as pl
from jax.experimental.pallas import tpu as pltpu
from jax.sharding import PartitionSpec as P


VMEM = pl.BlockSpec(memory_space=pltpu.VMEM)
HBM = pl.BlockSpec(memory_space=pltpu.HBM)


def call(body, outs, args, flops, in_specs=None, scratch=()):
    return pl.pallas_call(
        body,
        out_shape=outs,
        in_specs=in_specs or [VMEM] * len(args),
        out_specs=[VMEM] * len(outs),
        scratch_shapes=scratch,
        compiler_params=pltpu.CompilerParams(vmem_limit_bytes=16 << 20),
        cost_estimate=pl.CostEstimate(flops=flops, bytes_accessed=0, transcendentals=0),
    )(*args)


def flat(value):
    return value.reshape(-1, value.shape[-1])


def row_taps(slab, rows):
    return [flat(slab[p : p + rows]) for p in range(3)]


def convolved(lhs, weights, rows, cols):
    stacked = jnp.concatenate(lhs, axis=1)
    total = None
    for q in range(3):
        taps = jnp.concatenate([w[q] for w in weights], axis=0)
        part = jnp.dot(stacked, taps, preferred_element_type=jnp.float32)
        part = part.reshape(rows, cols, part.shape[-1])
        if q != 1:
            col = lax.broadcasted_iota(jnp.int32, part.shape, 1)
            edge = 0 if q == 0 else cols - 1
            part = jnp.where(col == edge, 0.0, pltpu.roll(part, 1 if q == 0 else cols - 1, 1))
        total = part if total is None else total + part
    return total


def parity():
    return lax.rem(lax.axis_index("tile"), 2)


def either(first, second):
    even = parity() == 0
    return jnp.concatenate([jnp.where(even, a, b) for a, b in zip(first, second)], axis=0)


def inner_slab(outer_half, inner_half, inner):
    if inner.shape[0] == inner_half.shape[0] == outer_half.shape[0]:
        return either([outer_half, inner_half, inner], [inner, inner_half, outer_half])
    below = jnp.concatenate([outer_half, inner_half, inner], axis=0)
    above = jnp.concatenate([inner, inner_half, outer_half], axis=0)
    return either([below], [above])


def outer_slab(outer, outer_half, tiles):
    tile = lax.axis_index("tile")
    beyond = (tile == 0) | ((tile == tiles - 1) & (parity() == 1))
    outer = jnp.where(beyond, jnp.zeros_like(outer), outer)
    return either([outer, outer_half[:2]], [outer_half[-2:], outer])


def received(slab):
    return jnp.where(lax.axis_index("tm") == 0, jnp.zeros_like(slab), slab)


def places(rows):
    even = 1 - parity()
    return pl.ds(2 * even, rows), pl.ds(rows * (1 - even), 2)


def weight_rows(w_ref, a):
    return [[w_ref[a, p, q] for q in range(3)] for p in range(3)]


def silu_rows(value, start, rows, tiles):
    hidden = (value / (1.0 + jnp.exp(-value))).astype(jnp.bfloat16)
    row = lax.broadcasted_iota(jnp.int32, hidden.shape, 0) + start
    row = row + lax.axis_index("tile") * rows - 1
    inside = (row >= 0) & (row < tiles * rows)
    return jnp.where(inside, hidden, jnp.zeros_like(hidden))


def move(pairs, sems):
    copies = [pltpu.make_async_copy(a, b, sems.at[i]) for i, (a, b) in enumerate(pairs)]
    for copy in copies:
        copy.start()
    for copy in copies:
        copy.wait()


def halves_of(rows):
    half, odd = rows // 2, parity()
    return pl.ds(odd * half, half), pl.ds((1 - odd) * half, half)


def cut_body(x_ref, first_ref, sems):
    half = x_ref.shape[1] // 2
    outer, inner = halves_of(2 * half)
    pairs = [
        (x_ref.at[1, outer], first_ref.at[pl.ds(0, half)]),
        (x_ref.at[1, inner], first_ref.at[pl.ds(half, half)]),
        (x_ref.at[0, inner], first_ref.at[pl.ds(2 * half, half)]),
    ]
    move(pairs, sems)


def pick_body(x_ref, own_ref, second_ref, outer_ref, inner_ref, sems):
    rows = x_ref.shape[1]
    odd = parity()
    outer, inner = pl.ds(odd * (rows - 2), 2), pl.ds((1 - odd) * (rows - 2), 2)
    pairs = [
        (x_ref.at[:, outer], outer_ref),
        (x_ref.at[:, inner], inner_ref),
        (x_ref.at[0, halves_of(rows)[0]], second_ref),
        (x_ref, own_ref),
    ]
    move(pairs, sems)


def own_halves(x_ref, f):
    half = x_ref.shape[1] // 2
    top, bottom = x_ref[f, :half], x_ref[f, half:]
    even = parity() == 0
    return jnp.where(even, top, bottom), jnp.where(even, bottom, top)


def own_sums(slabs, w_ref, b_ref, acc0_ref, acc1_ref):
    rows, cols = acc0_ref.shape[:2]
    taps = [row_taps(slab, rows) for slab in slabs]
    acc0_ref[...] = b_ref[...] + convolved(taps[0], weight_rows(w_ref, 2), rows, cols)
    weights = weight_rows(w_ref, 1) + weight_rows(w_ref, 2)
    acc1_ref[...] = b_ref[...] + convolved(taps[0] + taps[1], weights, rows, cols)


def own_near_body(x_ref, inner_ref, w_ref, b_ref, acc0_ref, acc1_ref):
    slabs = [inner_slab(*own_halves(x_ref, f), inner_ref[f]) for f in range(2)]
    own_sums(slabs, w_ref, b_ref, acc0_ref, acc1_ref)


def own_far_body(tiles, x_ref, outer_ref, w_ref, b_ref, acc0_ref, acc1_ref):
    slabs = [outer_slab(outer_ref[f], own_halves(x_ref, f)[0], tiles) for f in range(2)]
    own_sums(slabs, w_ref, b_ref, acc0_ref, acc1_ref)


def late_near_body(
    tiles, first_ref, inner_ref, w_ref, acc0_ref, acc1_ref, sum0_ref, h1_ref
):
    rows, cols = acc0_ref.shape[:2]
    half = rows // 2
    slab = received(inner_slab(first_ref[:half], first_ref[half : 2 * half], inner_ref[0]))
    taps = row_taps(slab, rows)
    acc1 = acc1_ref[...] + convolved(taps, weight_rows(w_ref, 0), rows, cols)
    h1_ref[...] = silu_rows(acc1, places(rows)[0].start, rows, tiles)
    sum0_ref[...] = acc0_ref[...] + convolved(taps, weight_rows(w_ref, 1), rows, cols)


def late_far_body(
    tiles, first_ref, outer_ref, w_ref, v_ref, acc0_ref, acc1_ref, near0_ref, near1_ref,
    sum0_ref, part_ref, h1_ref,
):
    rows, cols = near0_ref.shape[:2]
    near, far = places(rows)
    slab = received(outer_slab(outer_ref[1], first_ref[: rows // 2], tiles))
    taps = row_taps(slab, 2)
    acc1 = acc1_ref[...] + convolved(taps, weight_rows(w_ref, 0), 2, cols)
    h1_ref[far] = silu_rows(acc1, far.start, rows, tiles)
    h1_ref[near] = near1_ref[...]
    sum0_ref[far] = acc0_ref[...] + convolved(taps, weight_rows(w_ref, 1), 2, cols)
    sum0_ref[near] = near0_ref[...]
    taps = row_taps(h1_ref[...], rows)
    part_ref[...] = convolved(
        taps + taps, weight_rows(v_ref, 0) + weight_rows(v_ref, 1), rows, cols
    )


def early_body(
    tiles, first_ref, second_ref, inner_ref, outer_ref, w_ref, v_ref, sum0_ref, part_ref,
    send_ref, h0_ref,
):
    rows, cols = part_ref.shape[:2]
    half = rows // 2
    near = inner_slab(second_ref[...], first_ref[2 * half :], inner_ref[1])
    far = outer_slab(outer_ref[0], second_ref[...], tiles)
    outer_rows = jnp.where(parity() == 0, far[:2], far[2:])
    slab = either(
        [jnp.concatenate([outer_rows, near], axis=0)], [jnp.concatenate([near, outer_rows], axis=0)]
    )
    taps = row_taps(received(slab), rows + 2)
    acc0 = sum0_ref[...] + convolved(taps, weight_rows(w_ref, 0), rows + 2, cols)
    h0 = silu_rows(acc0, 0, rows, tiles)
    h0_ref[...] = h0
    part = part_ref[...] + convolved(row_taps(h0, rows), weight_rows(v_ref, 0), rows, cols)
    send_ref[0] = part.astype(jnp.bfloat16)


def rest_body(x_ref, h0_ref, h1_ref, v_ref, b_ref, out_ref):
    rows, cols = x_ref.shape[1:3]
    taps = row_taps(h0_ref[...], rows)
    weights = weight_rows(v_ref, 1) + 2 * weight_rows(v_ref, 2)
    part = convolved(taps + taps + row_taps(h1_ref[...], rows), weights, rows, cols)
    both = x_ref[0].astype(jnp.float32) + x_ref[1].astype(jnp.float32)
    out_ref[0] = (both + part) * 0.5 + b_ref[...]


def block(x, weight_first, bias_first, weight_second, bias_second):
    _, rows, cols, channels = x.shape
    half = rows // 2
    tiles, times = lax.axis_size("tile"), lax.axis_size("tm")
    forward = [(i, i + 1) for i in range(times - 1)]
    ring = forward + [(times - 1, 0)]
    inner_pairs = [(i, i + 1) for i in range(0, tiles - 1, 2)]
    outer_pairs = [(i, i + 1) for i in range(1, tiles - 1, 2)]
    inner_pairs += [(j, i) for i, j in inner_pairs]
    outer_pairs += [(j, i) for i, j in outer_pairs]
    unpaired = [(0, tiles - 1), (tiles - 1, 0)] if tiles % 2 == 0 else []
    diagonal = [(i * times + s, j * times + t) for i, j in outer_pairs for s, t in forward]

    def frames(*lead, dtype=jnp.bfloat16):
        return jax.ShapeDtypeStruct((*lead, cols, channels), dtype)

    f32 = jnp.float32
    x_hbm = pltpu.with_memory_space_constraint(x, pltpu.HBM)
    (first,) = call(
        cut_body,
        [frames(3 * half)],
        (x_hbm,),
        0,
        in_specs=[HBM],
        scratch=[pltpu.SemaphoreType.DMA((3,))],
    )
    own, second, outer_edge, inner_edge = call(
        pick_body,
        [frames(2, rows), frames(half), frames(2, 2), frames(2, 2)],
        (x_hbm,),
        10**10,
        in_specs=[HBM],
        scratch=[pltpu.SemaphoreType.DMA((4,))],
    )
    first = lax.ppermute(first, "tm", ring)
    outer = lax.ppermute(outer_edge, "tile", outer_pairs + unpaired)
    inner = lax.ppermute(inner_edge, "tile", inner_pairs)
    corner = lax.ppermute(outer_edge, ("tile", "tm"), diagonal)
    second = lax.ppermute(second, "tm", forward)

    bias_first = bias_first.reshape(1, 1, -1)
    bias_second = bias_second.reshape(1, 1, -1)
    unit = 2 * 9 * channels * channels * cols
    wide = rows + 2
    near0, near1 = call(
        own_near_body,
        [frames(rows, dtype=f32), frames(rows, dtype=f32)],
        (own, inner, weight_first, bias_first),
        3 * unit * rows,
    )
    far0, far1 = call(
        functools.partial(own_far_body, tiles),
        [frames(2, dtype=f32), frames(2, dtype=f32)],
        (own, outer, weight_first, bias_first),
        3 * unit * 2,
    )
    even = lax.rem(lax.axis_index("tile"), 2) == 0
    late_half, early_half = first[half : 2 * half], first[2 * half :]
    halves = jnp.stack([late_half, early_half])
    inner_corner = lax.ppermute(
        jnp.where(even, halves[:, half - 2 :], halves[:, :2]), "tile", inner_pairs
    )
    near0, near1 = call(
        functools.partial(late_near_body, tiles),
        [frames(rows, dtype=f32), frames(rows)],
        (first, inner_corner, weight_first, near0, near1),
        2 * unit * rows,
    )
    sum0, part, h1 = call(
        functools.partial(late_far_body, tiles),
        [frames(wide, dtype=f32), frames(rows, dtype=f32), frames(wide)],
        (first, corner, weight_first, weight_second, far0, far1, near0, near1),
        2 * unit * (rows + 2),
    )
    send, h0 = call(
        functools.partial(early_body, tiles),
        [frames(1, rows), frames(wide)],
        (first, second, inner_corner, corner, weight_first, weight_second, sum0, part),
        unit * (rows + wide),
    )
    before = lax.ppermute(send, "tm", forward)
    (rest,) = call(
        rest_body,
        [frames(1, rows, dtype=f32)],
        (own, h0, h1, weight_second, bias_second),
        3 * unit * rows,
    )
    return (rest + 0.5 * before.astype(f32)).astype(jnp.bfloat16)


def solution(mesh):
    in_specs = (P(("clips", "tm"), "tile", None, None), P(), P(), P(), P())
    out_specs = P(("clips", "tm"), "tile", None, None)
    return jax.shard_map(block, mesh=mesh, in_specs=in_specs, out_specs=out_specs, check_vma=False)
```

```python
import functools

import jax
import jax.numpy as jnp
from jax import lax
from jax.experimental import pallas as pl
from jax.experimental.pallas import tpu as pltpu
from jax.sharding import PartitionSpec as P


VMEM = pl.BlockSpec(memory_space=pltpu.VMEM)
HBM = pl.BlockSpec(memory_space=pltpu.HBM)


def call(body, outs, args, flops, in_specs=None, scratch=()):
    return pl.pallas_call(
        body,
        out_shape=outs,
        in_specs=in_specs or [VMEM] * len(args),
        out_specs=[VMEM] * len(outs),
        scratch_shapes=scratch,
        compiler_params=pltpu.CompilerParams(vmem_limit_bytes=16 << 20),
        cost_estimate=pl.CostEstimate(flops=flops, bytes_accessed=0, transcendentals=0),
    )(*args)


def flat(value):
    return value.reshape(-1, value.shape[-1])


def row_taps(slab, rows):
    return [flat(slab[p : p + rows]) for p in range(3)]


def convolved(lhs, weights, rows, cols):
    stacked = jnp.concatenate(lhs, axis=1)
    total = None
    for q in range(3):
        taps = jnp.concatenate([w[q] for w in weights], axis=0)
        part = jnp.dot(stacked, taps, preferred_element_type=jnp.float32)
        part = part.reshape(rows, cols, part.shape[-1])
        if q != 1:
            col = lax.broadcasted_iota(jnp.int32, part.shape, 1)
            edge = 0 if q == 0 else cols - 1
            part = jnp.where(col == edge, 0.0, pltpu.roll(part, 1 if q == 0 else cols - 1, 1))
        total = part if total is None else total + part
    return total


def parity():
    return lax.rem(lax.axis_index("tile"), 2)


def either(first, second):
    even = parity() == 0
    return jnp.concatenate([jnp.where(even, a, b) for a, b in zip(first, second)], axis=0)


def inner_slab(outer_half, inner_half, inner):
    if inner.shape[0] == inner_half.shape[0] == outer_half.shape[0]:
        return either([outer_half, inner_half, inner], [inner, inner_half, outer_half])
    below = jnp.concatenate([outer_half, inner_half, inner], axis=0)
    above = jnp.concatenate([inner, inner_half, outer_half], axis=0)
    return either([below], [above])


def outer_slab(outer, outer_half, tiles):
    tile = lax.axis_index("tile")
    beyond = (tile == 0) | ((tile == tiles - 1) & (parity() == 1))
    outer = jnp.where(beyond, jnp.zeros_like(outer), outer)
    return either([outer, outer_half[:2]], [outer_half[-2:], outer])


def places(rows):
    even = 1 - parity()
    return pl.ds(2 * even, rows), pl.ds(rows * (1 - even), 2)


def weight_rows(w_ref, a):
    return [[w_ref[a, p, q] for q in range(3)] for p in range(3)]


def silu_rows(value, start, rows, tiles):
    hidden = (value / (1.0 + jnp.exp(-value))).astype(jnp.bfloat16)
    row = lax.broadcasted_iota(jnp.int32, hidden.shape, 0) + start
    row = row + lax.axis_index("tile") * rows - 1
    inside = (row >= 0) & (row < tiles * rows)
    return jnp.where(inside, hidden, jnp.zeros_like(hidden))


def cut_body(x_ref, own_ref, first_ref, sem):
    copy = pltpu.make_async_copy(x_ref, own_ref, sem)
    copy.start()
    copy.wait()
    rows = x_ref.shape[1]
    half, odd = rows // 2, parity()
    outer_half, inner_half = pl.ds(odd * half, half), pl.ds((1 - odd) * half, half)
    first_ref[:half] = own_ref[1, outer_half]
    first_ref[half : 2 * half] = own_ref[1, inner_half]
    first_ref[2 * half :] = own_ref[0, inner_half]


def edges_body(own_ref, second_ref, outer_ref, inner_ref):
    rows = own_ref.shape[1]
    half, odd = rows // 2, parity()
    second_ref[...] = own_ref[0, pl.ds(odd * half, half)]
    for f in range(2):
        outer_ref[f] = own_ref[f, pl.ds(odd * (rows - 2), 2)]
        inner_ref[f] = own_ref[f, pl.ds((1 - odd) * (rows - 2), 2)]


def own_halves(x_ref, f):
    half = x_ref.shape[1] // 2
    top, bottom = x_ref[f, :half], x_ref[f, half:]
    even = parity() == 0
    return jnp.where(even, top, bottom), jnp.where(even, bottom, top)


def own_sums(slabs, w_ref, b_ref, acc0_ref, acc1_ref):
    rows, cols = acc0_ref.shape[:2]
    taps = [row_taps(slab, rows) for slab in slabs]
    acc0_ref[...] = b_ref[...] + convolved(taps[0], weight_rows(w_ref, 2), rows, cols)
    weights = weight_rows(w_ref, 1) + weight_rows(w_ref, 2)
    acc1_ref[...] = b_ref[...] + convolved(taps[0] + taps[1], weights, rows, cols)


def own_near_body(x_ref, inner_ref, w_ref, b_ref, acc0_ref, acc1_ref):
    slabs = [inner_slab(*own_halves(x_ref, f), inner_ref[f]) for f in range(2)]
    own_sums(slabs, w_ref, b_ref, acc0_ref, acc1_ref)


def own_far_body(tiles, x_ref, outer_ref, w_ref, b_ref, acc0_ref, acc1_ref):
    slabs = [outer_slab(outer_ref[f], own_halves(x_ref, f)[0], tiles) for f in range(2)]
    own_sums(slabs, w_ref, b_ref, acc0_ref, acc1_ref)


def add_earlier(pairs, taps, rows, cols):
    started = lax.axis_index("tm") > 0

    @pl.when(started)
    def _():
        lhs = taps()
        for total, base, weights in pairs:
            total[...] = base[...] + convolved(lhs, weights(), rows, cols)

    @pl.when(jnp.logical_not(started))
    def _():
        for total, base, _ in pairs:
            total[...] = base[...]


def late_near_body(
    tiles, first_ref, inner_ref, w_ref, acc0_ref, acc1_ref, sum0_ref, h1_ref, sum1_ref
):
    rows, cols = acc0_ref.shape[:2]
    half = rows // 2

    def taps():
        return row_taps(
            inner_slab(first_ref[:half], first_ref[half : 2 * half], inner_ref[0]), rows
        )

    pairs = [
        (sum1_ref, acc1_ref, lambda: weight_rows(w_ref, 0)),
        (sum0_ref, acc0_ref, lambda: weight_rows(w_ref, 1)),
    ]
    add_earlier(pairs, taps, rows, cols)
    h1_ref[...] = silu_rows(sum1_ref[...], places(rows)[0].start, rows, tiles)


def late_far_body(
    tiles, first_ref, outer_ref, w_ref, v_ref, acc0_ref, acc1_ref, near0_ref, near1_ref,
    sum0_ref, part_ref, h1_ref, sum1_ref,
):
    rows, cols = near0_ref.shape[:2]
    near, far = places(rows)

    def taps():
        return row_taps(outer_slab(outer_ref[1], first_ref[: rows // 2], tiles), 2)

    pairs = [
        (sum1_ref, acc1_ref, lambda: weight_rows(w_ref, 0)),
        (sum0_ref.at[far], acc0_ref, lambda: weight_rows(w_ref, 1)),
    ]
    add_earlier(pairs, taps, 2, cols)
    sum0_ref[near] = near0_ref[...]
    h1_ref[far] = silu_rows(sum1_ref[...], far.start, rows, tiles)
    h1_ref[near] = near1_ref[...]
    part_ref[...] = convolved(row_taps(h1_ref[...], rows), weight_rows(v_ref, 1), rows, cols)


def early_body(
    tiles, first_ref, second_ref, inner_ref, outer_ref, w_ref, v_ref, sum0_ref, part_ref, h1_ref,
    send_ref, h0_ref, both_ref, total_ref,
):
    rows, cols = part_ref.shape[:2]
    half = rows // 2

    def taps():
        near = inner_slab(second_ref[...], first_ref[2 * half :], inner_ref[1])
        far = outer_slab(outer_ref[0], second_ref[...], tiles)
        beyond = jnp.where(parity() == 0, far[:2], far[2:])
        below = jnp.concatenate([beyond, near], axis=0)
        above = jnp.concatenate([near, beyond], axis=0)
        return row_taps(either([below], [above]), rows + 2)

    pairs = [(total_ref, sum0_ref, lambda: weight_rows(w_ref, 0))]
    add_earlier(pairs, taps, rows + 2, cols)
    h0 = silu_rows(total_ref[...], 0, rows, tiles)
    both = (h0.astype(jnp.float32) + h1_ref[...].astype(jnp.float32)).astype(jnp.bfloat16)
    h0_ref[...] = h0
    both_ref[...] = both
    part = part_ref[...] + convolved(row_taps(both, rows), weight_rows(v_ref, 0), rows, cols)
    send_ref[0] = part.astype(jnp.bfloat16)


def rest_body(x_ref, h0_ref, both_ref, v_ref, b_ref, out_ref):
    rows, cols = x_ref.shape[1:3]
    taps = row_taps(h0_ref[...], rows) + row_taps(both_ref[...], rows)
    part = convolved(taps, weight_rows(v_ref, 1) + weight_rows(v_ref, 2), rows, cols)
    total = x_ref[0].astype(jnp.float32) + x_ref[1].astype(jnp.float32) + part
    out_ref[0] = total * 0.5 + b_ref[...]


def block(x, weight_first, bias_first, weight_second, bias_second):
    _, rows, cols, channels = x.shape
    half = rows // 2
    tiles, times = lax.axis_size("tile"), lax.axis_size("tm")
    forward = [(i, i + 1) for i in range(times - 1)]
    ring = forward + [(times - 1, 0)]
    inner_pairs = [(i, i + 1) for i in range(0, tiles - 1, 2)]
    outer_pairs = [(i, i + 1) for i in range(1, tiles - 1, 2)]
    inner_pairs += [(j, i) for i, j in inner_pairs]
    outer_pairs += [(j, i) for i, j in outer_pairs]
    unpaired = [(0, tiles - 1), (tiles - 1, 0)] if tiles % 2 == 0 else []
    diagonal = [(i * times + s, j * times + t) for i, j in outer_pairs for s, t in ring]
    diagonal += [(i * times + s, j * times + s) for i, j in unpaired for s in range(times)]

    def frames(*lead, dtype=jnp.bfloat16):
        return jax.ShapeDtypeStruct((*lead, cols, channels), dtype)

    f32 = jnp.float32
    own, first = call(
        cut_body,
        [frames(2, rows), frames(3 * half)],
        (pltpu.with_memory_space_constraint(x, pltpu.HBM),),
        0,
        in_specs=[HBM],
        scratch=[pltpu.SemaphoreType.DMA(())],
    )
    second, outer_edge, inner_edge = call(
        edges_body, [frames(half), frames(2, 2), frames(2, 2)], (own,), 10**10
    )
    first = lax.ppermute(first, "tm", ring)
    outer = lax.ppermute(outer_edge, "tile", outer_pairs + unpaired)
    inner = lax.ppermute(inner_edge, "tile", inner_pairs)
    corner = lax.ppermute(outer_edge, ("tile", "tm"), diagonal)
    second = lax.ppermute(second, "tm", forward)

    bias_first = bias_first.reshape(1, 1, -1)
    bias_second = bias_second.reshape(1, 1, -1)
    unit = 2 * 9 * channels * channels * cols
    wide = rows + 2
    near0, near1 = call(
        own_near_body,
        [frames(rows, dtype=f32), frames(rows, dtype=f32)],
        (own, inner, weight_first, bias_first),
        3 * unit * rows,
    )
    far0, far1 = call(
        functools.partial(own_far_body, tiles),
        [frames(2, dtype=f32), frames(2, dtype=f32)],
        (own, outer, weight_first, bias_first),
        3 * unit * 2,
    )
    even = lax.rem(lax.axis_index("tile"), 2) == 0
    late_half, early_half = first[half : 2 * half], first[2 * half :]
    halves = jnp.stack([late_half, early_half])
    inner_corner = lax.ppermute(
        jnp.where(even, halves[:, half - 2 :], halves[:, :2]), "tile", inner_pairs
    )
    near0, near1 = call(
        functools.partial(late_near_body, tiles),
        [frames(rows, dtype=f32), frames(rows)],
        (first, inner_corner, weight_first, near0, near1),
        2 * unit * rows,
        scratch=[pltpu.VMEM((rows, cols, channels), f32)],
    )
    sum0, part, h1 = call(
        functools.partial(late_far_body, tiles),
        [frames(wide, dtype=f32), frames(rows, dtype=f32), frames(wide)],
        (first, corner, weight_first, weight_second, far0, far1, near0, near1),
        unit * (rows + 4),
        scratch=[pltpu.VMEM((2, cols, channels), f32)],
    )
    send, h0, both = call(
        functools.partial(early_body, tiles),
        [frames(1, rows), frames(wide), frames(wide)],
        (first, second, inner_corner, corner, weight_first, weight_second, sum0, part, h1),
        unit * (rows + wide),
        scratch=[pltpu.VMEM((wide, cols, channels), f32)],
    )
    before = lax.ppermute(send, "tm", forward)
    (rest,) = call(
        rest_body,
        [frames(1, rows, dtype=f32)],
        (own, h0, both, weight_second, bias_second),
        2 * unit * rows,
    )
    return (rest + 0.5 * before.astype(f32)).astype(jnp.bfloat16)


def solution(mesh):
    in_specs = (P(("clips", "tm"), "tile", None, None), P(), P(), P(), P())
    out_specs = P(("clips", "tm"), "tile", None, None)
    return jax.shard_map(block, mesh=mesh, in_specs=in_specs, out_specs=out_specs, check_vma=False)
```

```python
import functools

import jax
import jax.numpy as jnp
from jax import lax
from jax.experimental import pallas as pl
from jax.experimental.pallas import tpu as pltpu
from jax.sharding import PartitionSpec as P


VMEM = pl.BlockSpec(memory_space=pltpu.VMEM)
HBM = pl.BlockSpec(memory_space=pltpu.HBM)


def call(body, outs, args, flops, in_specs=None, scratch=()):
    return pl.pallas_call(
        body,
        out_shape=outs,
        in_specs=in_specs or [VMEM] * len(args),
        out_specs=[VMEM] * len(outs),
        scratch_shapes=scratch,
        compiler_params=pltpu.CompilerParams(vmem_limit_bytes=16 << 20),
        cost_estimate=pl.CostEstimate(flops=flops, bytes_accessed=0, transcendentals=0),
    )(*args)


def flat(value):
    return value.reshape(-1, value.shape[-1])


def row_taps(slab, rows):
    return [flat(slab[p : p + rows]) for p in range(3)]


def convolved(lhs, weights, rows, cols):
    stacked = jnp.concatenate(lhs, axis=1)
    total = None
    for q in range(3):
        taps = jnp.concatenate([w[q] for w in weights], axis=0)
        part = jnp.dot(stacked, taps, preferred_element_type=jnp.float32)
        part = part.reshape(rows, cols, part.shape[-1])
        if q != 1:
            col = lax.broadcasted_iota(jnp.int32, part.shape, 1)
            edge = 0 if q == 0 else cols - 1
            part = jnp.where(col == edge, 0.0, pltpu.roll(part, 1 if q == 0 else cols - 1, 1))
        total = part if total is None else total + part
    return total


def parity():
    return lax.rem(lax.axis_index("tile"), 2)


def either(first, second):
    even = parity() == 0
    return jnp.concatenate([jnp.where(even, a, b) for a, b in zip(first, second)], axis=0)


def inner_slab(outer_half, inner_half, inner):
    if inner.shape[0] == inner_half.shape[0] == outer_half.shape[0]:
        return either([outer_half, inner_half, inner], [inner, inner_half, outer_half])
    below = jnp.concatenate([outer_half, inner_half, inner], axis=0)
    above = jnp.concatenate([inner, inner_half, outer_half], axis=0)
    return either([below], [above])


def outer_slab(outer, outer_half, tiles):
    tile = lax.axis_index("tile")
    beyond = (tile == 0) | ((tile == tiles - 1) & (parity() == 1))
    outer = jnp.where(beyond, jnp.zeros_like(outer), outer)
    return either([outer, outer_half[:2]], [outer_half[-2:], outer])


def places(rows):
    even = 1 - parity()
    return pl.ds(2 * even, rows), pl.ds(rows * (1 - even), 2)


def weight_rows(w_ref, a):
    return [[w_ref[a, p, q] for q in range(3)] for p in range(3)]


def silu_rows(value, start, rows, tiles):
    hidden = (value / (1.0 + jnp.exp(-value))).astype(jnp.bfloat16)
    row = lax.broadcasted_iota(jnp.int32, hidden.shape, 0) + start
    row = row + lax.axis_index("tile") * rows - 1
    inside = (row >= 0) & (row < tiles * rows)
    return jnp.where(inside, hidden, jnp.zeros_like(hidden))


def cut_body(x_ref, own_ref, first_ref, sem):
    copy = pltpu.make_async_copy(x_ref, own_ref, sem)
    copy.start()
    copy.wait()
    rows = x_ref.shape[1]
    half, odd = rows // 2, parity()
    outer_half, inner_half = pl.ds(odd * half, half), pl.ds((1 - odd) * half, half)
    first_ref[:half] = own_ref[1, outer_half]
    first_ref[half : 2 * half] = own_ref[1, inner_half]
    first_ref[2 * half :] = own_ref[0, inner_half]


def edges_body(own_ref, second_ref, outer_ref, inner_ref):
    rows = own_ref.shape[1]
    half, odd = rows // 2, parity()
    second_ref[...] = own_ref[0, pl.ds(odd * half, half)]
    for f in range(2):
        outer_ref[f] = own_ref[f, pl.ds(odd * (rows - 2), 2)]
        inner_ref[f] = own_ref[f, pl.ds((1 - odd) * (rows - 2), 2)]


def own_halves(x_ref, f):
    half = x_ref.shape[1] // 2
    top, bottom = x_ref[f, :half], x_ref[f, half:]
    even = parity() == 0
    return jnp.where(even, top, bottom), jnp.where(even, bottom, top)


def own_sums(slabs, w_ref, b_ref, acc0_ref, acc1_ref):
    rows, cols = acc0_ref.shape[:2]
    taps = [row_taps(slab, rows) for slab in slabs]
    acc0_ref[...] = b_ref[...] + convolved(taps[0], weight_rows(w_ref, 2), rows, cols)
    weights = weight_rows(w_ref, 1) + weight_rows(w_ref, 2)
    acc1_ref[...] = b_ref[...] + convolved(taps[0] + taps[1], weights, rows, cols)


def own_near_body(x_ref, inner_ref, w_ref, b_ref, acc0_ref, acc1_ref):
    slabs = [inner_slab(*own_halves(x_ref, f), inner_ref[f]) for f in range(2)]
    own_sums(slabs, w_ref, b_ref, acc0_ref, acc1_ref)


def own_far_body(tiles, x_ref, outer_ref, w_ref, b_ref, acc0_ref, acc1_ref):
    slabs = [outer_slab(outer_ref[f], own_halves(x_ref, f)[0], tiles) for f in range(2)]
    own_sums(slabs, w_ref, b_ref, acc0_ref, acc1_ref)


def add_earlier(pairs, taps, rows, cols):
    started = lax.axis_index("tm") > 0

    @pl.when(started)
    def _():
        lhs = taps()
        for total, base, weights in pairs:
            total[...] = base[...] + convolved(lhs, weights(), rows, cols)

    @pl.when(jnp.logical_not(started))
    def _():
        for total, base, _ in pairs:
            total[...] = base[...]


def late_near_body(
    tiles, first_ref, inner_ref, w_ref, acc0_ref, acc1_ref, sum0_ref, h1_ref, sum1_ref
):
    rows, cols = acc0_ref.shape[:2]
    half = rows // 2

    def taps():
        return row_taps(
            inner_slab(first_ref[:half], first_ref[half : 2 * half], inner_ref[0]), rows
        )

    pairs = [
        (sum1_ref, acc1_ref, lambda: weight_rows(w_ref, 0)),
        (sum0_ref, acc0_ref, lambda: weight_rows(w_ref, 1)),
    ]
    add_earlier(pairs, taps, rows, cols)
    h1_ref[...] = silu_rows(sum1_ref[...], places(rows)[0].start, rows, tiles)


def late_far_body(
    tiles, first_ref, outer_ref, w_ref, v_ref, acc0_ref, acc1_ref, near0_ref, near1_ref,
    sum0_ref, part_ref, h1_ref, sum1_ref,
):
    rows, cols = near0_ref.shape[:2]
    near, far = places(rows)

    def taps():
        return row_taps(outer_slab(outer_ref[1], first_ref[: rows // 2], tiles), 2)

    pairs = [
        (sum1_ref, acc1_ref, lambda: weight_rows(w_ref, 0)),
        (sum0_ref.at[far], acc0_ref, lambda: weight_rows(w_ref, 1)),
    ]
    add_earlier(pairs, taps, 2, cols)
    sum0_ref[near] = near0_ref[...]
    h1_ref[far] = silu_rows(sum1_ref[...], far.start, rows, tiles)
    h1_ref[near] = near1_ref[...]
    part_ref[...] = convolved(row_taps(h1_ref[...], rows), weight_rows(v_ref, 1), rows, cols)


def early_body(
    tiles, first_ref, second_ref, inner_ref, outer_ref, w_ref, v_ref, sum0_ref, part_ref, h1_ref,
    send_ref, h0_ref, both_ref, total_ref,
):
    rows, cols = part_ref.shape[:2]
    half = rows // 2

    def taps():
        near = inner_slab(second_ref[...], first_ref[2 * half :], inner_ref[1])
        far = outer_slab(outer_ref[0], second_ref[...], tiles)
        beyond = jnp.where(parity() == 0, far[:2], far[2:])
        below = jnp.concatenate([beyond, near], axis=0)
        above = jnp.concatenate([near, beyond], axis=0)
        return row_taps(either([below], [above]), rows + 2)

    pairs = [(total_ref, sum0_ref, lambda: weight_rows(w_ref, 0))]
    add_earlier(pairs, taps, rows + 2, cols)
    h0 = silu_rows(total_ref[...], 0, rows, tiles)
    both = (h0.astype(jnp.float32) + h1_ref[...].astype(jnp.float32)).astype(jnp.bfloat16)
    h0_ref[...] = h0
    both_ref[...] = both
    part = part_ref[...] + convolved(row_taps(both, rows), weight_rows(v_ref, 0), rows, cols)
    send_ref[0] = part.astype(jnp.bfloat16)


def rest_body(x_ref, h0_ref, both_ref, v_ref, b_ref, out_ref):
    rows, cols = x_ref.shape[1:3]
    taps = row_taps(h0_ref[...], rows) + row_taps(both_ref[...], rows)
    part = convolved(taps, weight_rows(v_ref, 1) + weight_rows(v_ref, 2), rows, cols)
    total = x_ref[0].astype(jnp.float32) + x_ref[1].astype(jnp.float32) + part
    out_ref[0] = total * 0.5 + b_ref[...]


def join_body(rest_ref, before_ref, out_ref):
    before = before_ref[...].astype(jnp.float32)
    before = jnp.where(lax.axis_index("tm") == 0, jnp.zeros_like(before), before)
    out_ref[...] = (rest_ref[...] + 0.5 * before).astype(jnp.bfloat16)


def block(x, weight_first, bias_first, weight_second, bias_second):
    _, rows, cols, channels = x.shape
    half = rows // 2
    tiles, times = lax.axis_size("tile"), lax.axis_size("tm")
    forward = [(i, i + 1) for i in range(times - 1)]
    ring = forward + [(times - 1, 0)]
    inner_pairs = [(i, i + 1) for i in range(0, tiles - 1, 2)]
    outer_pairs = [(i, i + 1) for i in range(1, tiles - 1, 2)]
    inner_pairs += [(j, i) for i, j in inner_pairs]
    outer_pairs += [(j, i) for i, j in outer_pairs]
    unpaired = [(0, tiles - 1), (tiles - 1, 0)] if tiles % 2 == 0 else []
    diagonal = [(i * times + s, j * times + t) for i, j in outer_pairs for s, t in ring]
    diagonal += [(i * times + s, j * times + s) for i, j in unpaired for s in range(times)]

    def frames(*lead, dtype=jnp.bfloat16):
        return jax.ShapeDtypeStruct((*lead, cols, channels), dtype)

    f32 = jnp.float32
    own, first = call(
        cut_body,
        [frames(2, rows), frames(3 * half)],
        (pltpu.with_memory_space_constraint(x, pltpu.HBM),),
        0,
        in_specs=[HBM],
        scratch=[pltpu.SemaphoreType.DMA(())],
    )
    second, outer_edge, inner_edge = call(
        edges_body, [frames(half), frames(2, 2), frames(2, 2)], (own,), 10**10
    )
    first = lax.ppermute(first, "tm", ring)
    outer = lax.ppermute(outer_edge, "tile", outer_pairs + unpaired)
    inner = lax.ppermute(inner_edge, "tile", inner_pairs)
    corner = lax.ppermute(outer_edge, ("tile", "tm"), diagonal)
    second = lax.ppermute(second, "tm", forward)

    bias_first = bias_first.reshape(1, 1, -1)
    bias_second = bias_second.reshape(1, 1, -1)
    unit = 2 * 9 * channels * channels * cols
    wide = rows + 2
    near0, near1 = call(
        own_near_body,
        [frames(rows, dtype=f32), frames(rows, dtype=f32)],
        (own, inner, weight_first, bias_first),
        3 * unit * rows,
    )
    far0, far1 = call(
        functools.partial(own_far_body, tiles),
        [frames(2, dtype=f32), frames(2, dtype=f32)],
        (own, outer, weight_first, bias_first),
        0,
    )
    even = lax.rem(lax.axis_index("tile"), 2) == 0
    late_half, early_half = first[half : 2 * half], first[2 * half :]
    halves = jnp.stack([late_half, early_half])
    inner_corner = lax.ppermute(
        jnp.where(even, halves[:, half - 2 :], halves[:, :2]), "tile", inner_pairs
    )
    near0, near1 = call(
        functools.partial(late_near_body, tiles),
        [frames(rows, dtype=f32), frames(rows)],
        (first, inner_corner, weight_first, near0, near1),
        0,
        scratch=[pltpu.VMEM((rows, cols, channels), f32)],
    )
    sum0, part, h1 = call(
        functools.partial(late_far_body, tiles),
        [frames(wide, dtype=f32), frames(rows, dtype=f32), frames(wide)],
        (first, corner, weight_first, weight_second, far0, far1, near0, near1),
        unit * (rows + 4),
        scratch=[pltpu.VMEM((2, cols, channels), f32)],
    )
    send, h0, both = call(
        functools.partial(early_body, tiles),
        [frames(1, rows), frames(wide), frames(wide)],
        (first, second, inner_corner, corner, weight_first, weight_second, sum0, part, h1),
        unit * (rows + wide),
        scratch=[pltpu.VMEM((wide, cols, channels), f32)],
    )
    before = lax.ppermute(send, "tm", ring)
    (rest,) = call(
        rest_body,
        [frames(1, rows, dtype=f32)],
        (own, h0, both, weight_second, bias_second),
        2 * unit * rows,
    )
    (pooled,) = call(join_body, [frames(1, rows)], (rest, before), 0)
    return pooled


def solution(mesh):
    in_specs = (P(("clips", "tm"), "tile", None, None), P(), P(), P(), P())
    out_specs = P(("clips", "tm"), "tile", None, None)
    return jax.shard_map(block, mesh=mesh, in_specs=in_specs, out_specs=out_specs, check_vma=False)
```

```python
import functools

import jax
import jax.numpy as jnp
from jax import lax
from jax.experimental import pallas as pl
from jax.experimental.pallas import tpu as pltpu
from jax.sharding import PartitionSpec as P


VMEM = pl.BlockSpec(memory_space=pltpu.VMEM)
HBM = pl.BlockSpec(memory_space=pltpu.HBM)


def call(body, outs, args, flops, in_specs=None, scratch=()):
    return pl.pallas_call(
        body,
        out_shape=outs,
        in_specs=in_specs or [VMEM] * len(args),
        out_specs=[VMEM] * len(outs),
        scratch_shapes=scratch,
        compiler_params=pltpu.CompilerParams(vmem_limit_bytes=16 << 20),
        cost_estimate=pl.CostEstimate(flops=flops, bytes_accessed=0, transcendentals=0),
    )(*args)


def flat(value):
    return value.reshape(-1, value.shape[-1])


def row_taps(slab, rows):
    return [flat(slab[p : p + rows]) for p in range(3)]


def convolved(lhs, weights, rows, cols):
    stacked = jnp.concatenate(lhs, axis=1)
    total = None
    for q in range(3):
        taps = jnp.concatenate([w[q] for w in weights], axis=0)
        part = jnp.dot(stacked, taps, preferred_element_type=jnp.float32)
        part = part.reshape(rows, cols, part.shape[-1])
        if q != 1:
            col = lax.broadcasted_iota(jnp.int32, part.shape, 1)
            edge = 0 if q == 0 else cols - 1
            part = jnp.where(col == edge, 0.0, pltpu.roll(part, 1 if q == 0 else cols - 1, 1))
        total = part if total is None else total + part
    return total


def parity():
    return lax.rem(lax.axis_index("tile"), 2)


def either(first, second):
    even = parity() == 0
    return jnp.concatenate([jnp.where(even, a, b) for a, b in zip(first, second)], axis=0)


def own_edge(own, side):
    odd = parity()
    last = own.shape[0] - 2
    return own[pl.ds((odd if side == 0 else 1 - odd) * last, 2)]


def outer_slab(outer, own, tiles):
    tile = lax.axis_index("tile")
    beyond = (tile == 0) | ((tile == tiles - 1) & (parity() == 1))
    outer = jnp.where(beyond, jnp.zeros_like(outer), outer)
    edge = own_edge(own, 0)
    return either([outer, edge], [edge, outer])


def inner_slab(inner, own):
    edge = own_edge(own, 1)
    return either([edge, inner], [inner, edge])


def places(rows):
    odd = parity()
    return pl.ds(2, rows - 2), pl.ds((1 - odd) * rows, 2), pl.ds(odd * rows, 2)


def weight_rows(w_ref, a):
    return [[w_ref[a, p, q] for q in range(3)] for p in range(3)]


def silu_rows(value, start, rows, tiles):
    hidden = (value / (1.0 + jnp.exp(-value))).astype(jnp.bfloat16)
    row = lax.broadcasted_iota(jnp.int32, hidden.shape, 0) + start
    row = row + lax.axis_index("tile") * rows - 1
    inside = (row >= 0) & (row < tiles * rows)
    return jnp.where(inside, hidden, jnp.zeros_like(hidden))


def edges_body(x_ref, own_ref, outer_ref, inner_ref, sem):
    copy = pltpu.make_async_copy(x_ref, own_ref, sem)
    copy.start()
    copy.wait()
    for f in range(2):
        outer_ref[f] = own_edge(own_ref.at[f], 0)
        inner_ref[f] = own_edge(own_ref.at[f], 1)


def turn_body(m_ref, inner_ref):
    for f in range(2):
        inner_ref[f] = own_edge(m_ref.at[f], 1)


def own_sums(slabs, w_ref, b_ref, acc0_ref, acc1_ref):
    rows, cols = acc0_ref.shape[:2]
    taps = [row_taps(slab, rows) for slab in slabs]
    acc0_ref[...] = b_ref[...] + convolved(taps[0], weight_rows(w_ref, 2), rows, cols)
    weights = weight_rows(w_ref, 1) + weight_rows(w_ref, 2)
    acc1_ref[...] = b_ref[...] + convolved(taps[0] + taps[1], weights, rows, cols)


def own_near_body(x_ref, inner_ref, w_ref, b_ref, acc0_ref, acc1_ref):
    even = parity() == 0
    slabs = []
    for f in range(2):
        below = jnp.concatenate([x_ref[f], inner_ref[f]], axis=0)
        above = jnp.concatenate([inner_ref[f], x_ref[f]], axis=0)
        slabs.append(jnp.where(even, below, above))
    own_sums(slabs, w_ref, b_ref, acc0_ref, acc1_ref)


def own_far_body(tiles, x_ref, outer_ref, w_ref, b_ref, acc0_ref, acc1_ref):
    slabs = [outer_slab(outer_ref[f], x_ref.at[f], tiles) for f in range(2)]
    own_sums(slabs, w_ref, b_ref, acc0_ref, acc1_ref)


def hidden(slab, bases, places_of, w_ref, tiles, whole, h0_ref, h1_ref, sum0_ref, sum1_ref):
    rows, cols = sum0_ref.shape[:2]
    started = lax.axis_index("tm") > 0

    @pl.when(started)
    def _():
        taps = [row_taps(slab(f), rows) for f in range(2)]
        weights = weight_rows(w_ref, 0) + weight_rows(w_ref, 1)
        sum0_ref[...] = bases[0]() + convolved(taps[0] + taps[1], weights, rows, cols)
        sum1_ref[...] = bases[1]() + convolved(taps[1], weight_rows(w_ref, 0), rows, cols)

    @pl.when(jnp.logical_not(started))
    def _():
        sum0_ref[...] = bases[0]()
        sum1_ref[...] = bases[1]()

    h0_ref[...] = silu_rows(sum0_ref[...], places_of.start, whole, tiles)
    h1_ref[...] = silu_rows(sum1_ref[...], places_of.start, whole, tiles)


def from_near(acc_ref, start, rows):
    return lambda: acc_ref[pl.ds(start, rows)]


def middle_body(tiles, m_ref, w_ref, _, acc0_ref, acc1_ref, h0_ref, h1_ref, sum0_ref, sum1_ref):
    rows = m_ref.shape[1]
    start = 2 * parity()
    bases = [from_near(acc_ref, start, rows - 2) for acc_ref in (acc0_ref, acc1_ref)]
    place = places(rows)[0]
    hidden(lambda f: m_ref[f], bases, place, w_ref, tiles, rows, h0_ref, h1_ref, sum0_ref, sum1_ref)


def near_body(
    tiles, m_ref, inner_ref, w_ref, acc0_ref, acc1_ref, h0_ref, h1_ref, sum0_ref, sum1_ref
):
    rows = m_ref.shape[1]
    start = (1 - parity()) * (rows - 2)
    bases = [from_near(acc_ref, start, 2) for acc_ref in (acc0_ref, acc1_ref)]
    place = places(rows)[1]

    def slab(f):
        return inner_slab(inner_ref[f], m_ref.at[f])

    hidden(slab, bases, place, w_ref, tiles, rows, h0_ref, h1_ref, sum0_ref, sum1_ref)


def far_body(
    tiles, m_ref, outer_ref, w_ref, v_ref, acc0_ref, acc1_ref, mid0_ref, mid1_ref, near0_ref,
    near1_ref, send_ref, h0_ref, both_ref, h1_ref, sum0_ref, sum1_ref,
):
    rows, cols = m_ref.shape[1:3]
    middle, near, far = places(rows)

    def slab(f):
        return outer_slab(outer_ref[f], m_ref.at[f], tiles)

    bases = [lambda: acc0_ref[...], lambda: acc1_ref[...]]
    h0_ref[middle], h0_ref[near] = mid0_ref[...], near0_ref[...]
    h1_ref[middle], h1_ref[near] = mid1_ref[...], near1_ref[...]
    hidden(
        slab, bases, far, w_ref, tiles, rows, h0_ref.at[far], h1_ref.at[far], sum0_ref, sum1_ref
    )
    h1 = h1_ref[...]
    both = (h0_ref[...].astype(jnp.float32) + h1.astype(jnp.float32)).astype(jnp.bfloat16)
    both_ref[...] = both
    taps = row_taps(both, rows) + row_taps(h1, rows)
    part = convolved(taps, weight_rows(v_ref, 0) + weight_rows(v_ref, 1), rows, cols)
    send_ref[0] = part.astype(jnp.bfloat16)


def rest_body(x_ref, h0_ref, both_ref, v_ref, b_ref, out_ref):
    rows, cols = x_ref.shape[1:3]
    taps = row_taps(h0_ref[...], rows) + row_taps(both_ref[...], rows)
    part = convolved(taps, weight_rows(v_ref, 1) + weight_rows(v_ref, 2), rows, cols)
    total = x_ref[0].astype(jnp.float32) + x_ref[1].astype(jnp.float32) + part
    out_ref[0] = total * 0.5 + b_ref[...]


def block(x, weight_first, bias_first, weight_second, bias_second):
    _, rows, cols, channels = x.shape
    tiles, times = lax.axis_size("tile"), lax.axis_size("tm")
    forward = [(i, i + 1) for i in range(times - 1)]
    ring = forward + [(times - 1, 0)]
    inner_pairs = [(i, i + 1) for i in range(0, tiles - 1, 2)]
    outer_pairs = [(i, i + 1) for i in range(1, tiles - 1, 2)]
    inner_pairs += [(j, i) for i, j in inner_pairs]
    outer_pairs += [(j, i) for i, j in outer_pairs]
    unpaired = [(0, tiles - 1), (tiles - 1, 0)] if tiles % 2 == 0 else []
    diagonal = [(i * times + s, j * times + t) for i, j in outer_pairs for s, t in ring]
    diagonal += [(i * times + s, j * times + s) for i, j in unpaired for s in range(times)]

    def frames(*lead, dtype=jnp.bfloat16):
        return jax.ShapeDtypeStruct((*lead, cols, channels), dtype)

    f32 = jnp.float32
    earlier = lax.ppermute(x, "tm", ring)
    x, outer_edge, inner_edge = call(
        edges_body,
        [frames(2, rows), frames(2, 2), frames(2, 2)],
        (pltpu.with_memory_space_constraint(x, pltpu.HBM),),
        10**10,
        in_specs=[HBM],
        scratch=[pltpu.SemaphoreType.DMA(())],
    )
    inner = lax.ppermute(inner_edge, "tile", inner_pairs)
    outer = lax.ppermute(outer_edge, "tile", outer_pairs + unpaired)
    corner = lax.ppermute(outer_edge, ("tile", "tm"), diagonal)

    bias_first = bias_first.reshape(1, 1, -1)
    bias_second = bias_second.reshape(1, 1, -1)
    unit = 2 * 9 * channels * channels * cols
    wide = rows + 2
    sums0, sums1 = call(
        own_near_body,
        [frames(rows, dtype=f32), frames(rows, dtype=f32)],
        (x, inner, weight_first, bias_first),
        3 * unit * rows,
    )
    far0, far1 = call(
        functools.partial(own_far_body, tiles),
        [frames(2, dtype=f32), frames(2, dtype=f32)],
        (x, outer, weight_first, bias_first),
        0,
    )
    (inner_edge,) = call(turn_body, [frames(2, 2)], (earlier,), 0)
    inner_corner = lax.ppermute(inner_edge, "tile", inner_pairs)

    def sums(count):
        return [pltpu.VMEM((count, cols, channels), f32)] * 2

    mid0, mid1 = call(
        functools.partial(middle_body, tiles),
        [frames(rows - 2), frames(rows - 2)],
        (earlier, weight_first, weight_second, sums0, sums1),
        0,
        scratch=sums(rows - 2),
    )
    near0, near1 = call(
        functools.partial(near_body, tiles),
        [frames(2), frames(2)],
        (earlier, inner_corner, weight_first, sums0, sums1),
        0,
        scratch=sums(2),
    )
    send, h0, both = call(
        functools.partial(far_body, tiles),
        [frames(1, rows), frames(wide), frames(wide)],
        (earlier, corner, weight_first, weight_second, far0, far1, mid0, mid1, near0, near1),
        unit * (rows + wide),
        scratch=[pltpu.VMEM((wide, cols, channels), jnp.bfloat16), *sums(2)],
    )
    before = lax.ppermute(send, "tm", forward)
    (rest,) = call(
        rest_body,
        [frames(1, rows, dtype=f32)],
        (x, h0, both, weight_second, bias_second),
        2 * unit * rows,
    )
    return (rest + 0.5 * before.astype(f32)).astype(jnp.bfloat16)


def solution(mesh):
    in_specs = (P(("clips", "tm"), "tile", None, None), P(), P(), P(), P())
    out_specs = P(("clips", "tm"), "tile", None, None)
    return jax.shard_map(block, mesh=mesh, in_specs=in_specs, out_specs=out_specs, check_vma=False)
```

```python
import functools

import jax
import jax.numpy as jnp
from jax import lax
from jax.experimental import pallas as pl
from jax.experimental.pallas import tpu as pltpu
from jax.sharding import PartitionSpec as P


VMEM = pl.BlockSpec(memory_space=pltpu.VMEM)
HBM = pl.BlockSpec(memory_space=pltpu.HBM)


def call(body, outs, args, flops, in_specs=None, scratch=()):
    return pl.pallas_call(
        body,
        out_shape=outs,
        in_specs=in_specs or [VMEM] * len(args),
        out_specs=[VMEM] * len(outs),
        scratch_shapes=scratch,
        compiler_params=pltpu.CompilerParams(vmem_limit_bytes=16 << 20),
        cost_estimate=pl.CostEstimate(flops=flops, bytes_accessed=0, transcendentals=0),
    )(*args)


def flat(value):
    return value.reshape(-1, value.shape[-1])


def row_taps(slab, rows):
    return [flat(slab[p : p + rows]) for p in range(3)]


def convolved(lhs, weights, rows, cols):
    stacked = jnp.concatenate(lhs, axis=1)
    total = None
    for q in range(3):
        taps = jnp.concatenate([w[q] for w in weights], axis=0)
        part = jnp.dot(stacked, taps, preferred_element_type=jnp.float32)
        part = part.reshape(rows, cols, part.shape[-1])
        if q != 1:
            col = lax.broadcasted_iota(jnp.int32, part.shape, 1)
            edge = 0 if q == 0 else cols - 1
            part = jnp.where(col == edge, 0.0, pltpu.roll(part, 1 if q == 0 else cols - 1, 1))
        total = part if total is None else total + part
    return total


def parity():
    return lax.rem(lax.axis_index("tile"), 2)


def either(first, second):
    even = parity() == 0
    return jnp.concatenate([jnp.where(even, a, b) for a, b in zip(first, second)], axis=0)


def own_edge(own, side):
    odd = parity()
    last = own.shape[0] - 2
    return own[pl.ds((odd if side == 0 else 1 - odd) * last, 2)]


def outer_slab(outer, own, tiles):
    tile = lax.axis_index("tile")
    beyond = (tile == 0) | ((tile == tiles - 1) & (parity() == 1))
    outer = jnp.where(beyond, jnp.zeros_like(outer), outer)
    edge = own_edge(own, 0)
    return either([outer, edge], [edge, outer])


def inner_slab(inner, own):
    edge = own_edge(own, 1)
    return either([edge, inner], [inner, edge])


def places(rows):
    odd = parity()
    return pl.ds(2, rows - 2), pl.ds((1 - odd) * rows, 2), pl.ds(odd * rows, 2)


def weight_rows(w_ref, a):
    return [[w_ref[a, p, q] for q in range(3)] for p in range(3)]


def silu_rows(value, start, rows, tiles):
    hidden = (value / (1.0 + jnp.exp(-value))).astype(jnp.bfloat16)
    row = lax.broadcasted_iota(jnp.int32, hidden.shape, 0) + start
    row = row + lax.axis_index("tile") * rows - 1
    inside = (row >= 0) & (row < tiles * rows)
    return jnp.where(inside, hidden, jnp.zeros_like(hidden))


def edges_body(x_ref, own_ref, outer_ref, inner_ref, sem):
    copy = pltpu.make_async_copy(x_ref, own_ref, sem)
    copy.start()
    copy.wait()
    for f in range(2):
        outer_ref[f] = own_edge(own_ref.at[f], 0)
        inner_ref[f] = own_edge(own_ref.at[f], 1)


def turn_body(m_ref, inner_ref):
    for f in range(2):
        inner_ref[f] = own_edge(m_ref.at[f], 1)


def own_sums(slabs, w_ref, b_ref, acc0_ref, acc1_ref):
    rows, cols = acc0_ref.shape[:2]
    taps = [row_taps(slab, rows) for slab in slabs]
    acc0_ref[...] = b_ref[...] + convolved(taps[0], weight_rows(w_ref, 2), rows, cols)
    weights = weight_rows(w_ref, 1) + weight_rows(w_ref, 2)
    acc1_ref[...] = b_ref[...] + convolved(taps[0] + taps[1], weights, rows, cols)


def own_near_body(x_ref, inner_ref, w_ref, b_ref, acc0_ref, acc1_ref):
    even = parity() == 0
    slabs = []
    for f in range(2):
        below = jnp.concatenate([x_ref[f], inner_ref[f]], axis=0)
        above = jnp.concatenate([inner_ref[f], x_ref[f]], axis=0)
        slabs.append(jnp.where(even, below, above))
    own_sums(slabs, w_ref, b_ref, acc0_ref, acc1_ref)


def own_far_body(tiles, x_ref, outer_ref, w_ref, b_ref, acc0_ref, acc1_ref):
    slabs = [outer_slab(outer_ref[f], x_ref.at[f], tiles) for f in range(2)]
    own_sums(slabs, w_ref, b_ref, acc0_ref, acc1_ref)


def hidden(slab, bases, places_of, w_ref, tiles, whole, h0_ref, h1_ref, sum0_ref, sum1_ref):
    rows, cols = sum0_ref.shape[:2]
    started = lax.axis_index("tm") > 0

    @pl.when(started)
    def _():
        taps = [row_taps(slab(f), rows) for f in range(2)]
        weights = weight_rows(w_ref, 0) + weight_rows(w_ref, 1)
        sum0_ref[...] = bases[0]() + convolved(taps[0] + taps[1], weights, rows, cols)
        sum1_ref[...] = bases[1]() + convolved(taps[1], weight_rows(w_ref, 0), rows, cols)

    @pl.when(jnp.logical_not(started))
    def _():
        sum0_ref[...] = bases[0]()
        sum1_ref[...] = bases[1]()

    h0_ref[...] = silu_rows(sum0_ref[...], places_of.start, whole, tiles)
    h1_ref[...] = silu_rows(sum1_ref[...], places_of.start, whole, tiles)


def from_near(acc_ref, start, rows):
    return lambda: acc_ref[pl.ds(start, rows)]


def middle_body(tiles, m_ref, w_ref, _, acc0_ref, acc1_ref, h0_ref, h1_ref, sum0_ref, sum1_ref):
    rows = m_ref.shape[1]
    start = 2 * parity()
    bases = [from_near(acc_ref, start, rows - 2) for acc_ref in (acc0_ref, acc1_ref)]
    place = places(rows)[0]
    hidden(lambda f: m_ref[f], bases, place, w_ref, tiles, rows, h0_ref, h1_ref, sum0_ref, sum1_ref)


def partial_rows(times, h0, h1, v_ref, rows, cols, send_ref):
    has_next = lax.axis_index("tm") < times - 1

    @pl.when(has_next)
    def _():
        both = (h0.astype(jnp.float32) + h1.astype(jnp.float32)).astype(jnp.bfloat16)
        taps = row_taps(both, rows) + row_taps(h1, rows)
        part = convolved(taps, weight_rows(v_ref, 0) + weight_rows(v_ref, 1), rows, cols)
        send_ref[...] = part.astype(jnp.bfloat16)

    @pl.when(jnp.logical_not(has_next))
    def _():
        send_ref[...] = jnp.zeros_like(send_ref)


def near_body(
    tiles, times, m_ref, inner_ref, w_ref, v_ref, acc0_ref, acc1_ref, mid0_ref, mid1_ref,
    send_ref, h0_ref, h1_ref, sum0_ref, sum1_ref,
):
    rows, cols = m_ref.shape[1:3]
    odd = parity()
    start = (1 - odd) * (rows - 2)
    bases = [from_near(acc_ref, start, 2) for acc_ref in (acc0_ref, acc1_ref)]
    place = places(rows)[1]

    def slab(f):
        return inner_slab(inner_ref[f], m_ref.at[f])

    middle, near = pl.ds(2 * odd, rows - 2), pl.ds(start, 2)
    h0_ref[middle], h1_ref[middle] = mid0_ref[...], mid1_ref[...]
    hidden(
        slab, bases, place, w_ref, tiles, rows, h0_ref.at[near], h1_ref.at[near], sum0_ref,
        sum1_ref,
    )
    partial_rows(times, h0_ref[...], h1_ref[...], v_ref, rows - 2, cols, send_ref)


def far_body(
    tiles, times, m_ref, outer_ref, w_ref, v_ref, acc0_ref, acc1_ref, near0_ref, near1_ref,
    send_ref, h0_ref, h1_ref, sum0_ref, sum1_ref,
):
    rows, cols = m_ref.shape[1:3]
    odd = parity()
    far = places(rows)[2]
    near = pl.ds(2 * (1 - odd), rows)

    def slab(f):
        return outer_slab(outer_ref[f], m_ref.at[f], tiles)

    bases = [lambda: acc0_ref[...], lambda: acc1_ref[...]]
    h0_ref[near], h1_ref[near] = near0_ref[...], near1_ref[...]
    hidden(
        slab, bases, far, w_ref, tiles, rows, h0_ref.at[far], h1_ref.at[far], sum0_ref, sum1_ref
    )
    side = pl.ds(odd * (rows - 2), 4)
    partial_rows(times, h0_ref[side], h1_ref[side], v_ref, 2, cols, send_ref)


def rest_body(x_ref, h0_ref, h1_ref, v_ref, b_ref, out_ref):
    rows, cols = x_ref.shape[1:3]
    h0, h1 = h0_ref[...], h1_ref[...]
    both = (h0.astype(jnp.float32) + h1.astype(jnp.float32)).astype(jnp.bfloat16)
    taps = row_taps(h0, rows) + row_taps(both, rows)
    part = convolved(taps, weight_rows(v_ref, 1) + weight_rows(v_ref, 2), rows, cols)
    total = x_ref[0].astype(jnp.float32) + x_ref[1].astype(jnp.float32) + part
    out_ref[0] = total * 0.5 + b_ref[...]


def join_body(rest_ref, near_ref, far_ref, out_ref):
    rows = rest_ref.shape[1]
    odd = parity()
    first = lax.axis_index("tm") == 0
    for part_ref, start in ((near_ref, 2 * (1 - odd)), (far_ref, odd * (rows - 2))):
        part = part_ref[...].astype(jnp.float32)
        part = jnp.where(first, jnp.zeros_like(part), part)
        place = pl.ds(start, part.shape[0])
        out_ref[0, place] = (rest_ref[0, place] + 0.5 * part).astype(jnp.bfloat16)


def block(x, weight_first, bias_first, weight_second, bias_second):
    _, rows, cols, channels = x.shape
    tiles, times = lax.axis_size("tile"), lax.axis_size("tm")
    forward = [(i, i + 1) for i in range(times - 1)]
    ring = forward + [(times - 1, 0)]
    inner_pairs = [(i, i + 1) for i in range(0, tiles - 1, 2)]
    outer_pairs = [(i, i + 1) for i in range(1, tiles - 1, 2)]
    inner_pairs += [(j, i) for i, j in inner_pairs]
    outer_pairs += [(j, i) for i, j in outer_pairs]
    unpaired = [(0, tiles - 1), (tiles - 1, 0)] if tiles % 2 == 0 else []
    diagonal = [(i * times + s, j * times + t) for i, j in outer_pairs for s, t in forward]

    def frames(*lead, dtype=jnp.bfloat16):
        return jax.ShapeDtypeStruct((*lead, cols, channels), dtype)

    f32 = jnp.float32
    earlier = lax.ppermute(x, "tm", ring)
    x, outer_edge, inner_edge = call(
        edges_body,
        [frames(2, rows), frames(2, 2), frames(2, 2)],
        (pltpu.with_memory_space_constraint(x, pltpu.HBM),),
        10**10,
        in_specs=[HBM],
        scratch=[pltpu.SemaphoreType.DMA(())],
    )
    inner = lax.ppermute(inner_edge, "tile", inner_pairs)
    outer = lax.ppermute(outer_edge, "tile", outer_pairs + unpaired)
    corner = lax.ppermute(outer_edge, ("tile", "tm"), diagonal)

    bias_first = bias_first.reshape(1, 1, -1)
    bias_second = bias_second.reshape(1, 1, -1)
    unit = 2 * 9 * channels * channels * cols
    wide = rows + 2
    sums0, sums1 = call(
        own_near_body,
        [frames(rows, dtype=f32), frames(rows, dtype=f32)],
        (x, inner, weight_first, bias_first),
        3 * unit * rows,
    )
    far0, far1 = call(
        functools.partial(own_far_body, tiles),
        [frames(2, dtype=f32), frames(2, dtype=f32)],
        (x, outer, weight_first, bias_first),
        0,
    )
    (inner_edge,) = call(turn_body, [frames(2, 2)], (earlier,), 0)
    inner_corner = lax.ppermute(inner_edge, "tile", inner_pairs)

    def sums(count):
        return [pltpu.VMEM((count, cols, channels), f32)] * 2

    mid0, mid1 = call(
        functools.partial(middle_body, tiles),
        [frames(rows - 2), frames(rows - 2)],
        (earlier, weight_first, weight_second, sums0, sums1),
        0,
        scratch=sums(rows - 2),
    )
    near_send, near0, near1 = call(
        functools.partial(near_body, tiles, times),
        [frames(rows - 2), frames(rows), frames(rows)],
        (earlier, inner_corner, weight_first, weight_second, sums0, sums1, mid0, mid1),
        0,
        scratch=sums(2),
    )
    near_part = lax.ppermute(near_send, "tm", ring)
    far_send, h0, h1 = call(
        functools.partial(far_body, tiles, times),
        [frames(2), frames(wide), frames(wide)],
        (earlier, corner, weight_first, weight_second, far0, far1, near0, near1),
        0,
        scratch=sums(2),
    )
    far_part = lax.ppermute(far_send, "tm", ring)
    (rest,) = call(
        rest_body,
        [frames(1, rows, dtype=f32)],
        (x, h0, h1, weight_second, bias_second),
        2 * unit * rows,
    )
    (pooled,) = call(join_body, [frames(1, rows)], (rest, near_part, far_part), 0)
    return pooled


def solution(mesh):
    in_specs = (P(("clips", "tm"), "tile", None, None), P(), P(), P(), P())
    out_specs = P(("clips", "tm"), "tile", None, None)
    return jax.shard_map(block, mesh=mesh, in_specs=in_specs, out_specs=out_specs, check_vma=False)
```

```python
import functools

import jax
import jax.numpy as jnp
from jax import lax
from jax.experimental import pallas as pl
from jax.experimental.pallas import tpu as pltpu
from jax.sharding import PartitionSpec as P


VMEM = pl.BlockSpec(memory_space=pltpu.VMEM)
HBM = pl.BlockSpec(memory_space=pltpu.HBM)


def call(body, outs, args, flops, in_specs=None, scratch=()):
    return pl.pallas_call(
        body,
        out_shape=outs,
        in_specs=in_specs or [VMEM] * len(args),
        out_specs=[VMEM] * len(outs),
        scratch_shapes=scratch,
        compiler_params=pltpu.CompilerParams(vmem_limit_bytes=16 << 20),
        cost_estimate=pl.CostEstimate(flops=flops, bytes_accessed=0, transcendentals=0),
    )(*args)


def flat(value):
    return value.reshape(-1, value.shape[-1])


def row_taps(slab, rows):
    return [flat(slab[p : p + rows]) for p in range(3)]


def convolved(lhs, weights, rows, cols):
    stacked = jnp.concatenate(lhs, axis=1)
    total = None
    for q in range(3):
        taps = jnp.concatenate([w[q] for w in weights], axis=0)
        part = jnp.dot(stacked, taps, preferred_element_type=jnp.float32)
        part = part.reshape(rows, cols, part.shape[-1])
        if q != 1:
            col = lax.broadcasted_iota(jnp.int32, part.shape, 1)
            edge = 0 if q == 0 else cols - 1
            part = jnp.where(col == edge, 0.0, pltpu.roll(part, 1 if q == 0 else cols - 1, 1))
        total = part if total is None else total + part
    return total


def parity():
    return lax.rem(lax.axis_index("tile"), 2)


def either(first, second):
    even = parity() == 0
    return jnp.concatenate([jnp.where(even, a, b) for a, b in zip(first, second)], axis=0)


def own_edge(own, side):
    odd = parity()
    last = own.shape[0] - 2
    return own[pl.ds((odd if side == 0 else 1 - odd) * last, 2)]


def outer_slab(outer, own, tiles):
    tile = lax.axis_index("tile")
    beyond = (tile == 0) | ((tile == tiles - 1) & (parity() == 1))
    outer = jnp.where(beyond, jnp.zeros_like(outer), outer)
    edge = own_edge(own, 0)
    return either([outer, edge], [edge, outer])


def weight_rows(w_ref, a):
    return [[w_ref[a, p, q] for q in range(3)] for p in range(3)]


def silu_rows(value, start, rows, tiles):
    hidden = (value / (1.0 + jnp.exp(-value))).astype(jnp.bfloat16)
    row = lax.broadcasted_iota(jnp.int32, hidden.shape, 0) + start
    row = row + lax.axis_index("tile") * rows - 1
    inside = (row >= 0) & (row < tiles * rows)
    return jnp.where(inside, hidden, jnp.zeros_like(hidden))


def cut_body(x_ref, late_ref, sem):
    copy = pltpu.make_async_copy(x_ref.at[1], late_ref, sem)
    copy.start()
    copy.wait()


def edges_body(x_ref, late_ref, early_ref, outer_ref, inner_ref, sem):
    copy = pltpu.make_async_copy(x_ref.at[0], early_ref, sem)
    copy.start()
    outer_ref[1], inner_ref[1] = own_edge(late_ref, 0), own_edge(late_ref, 1)
    copy.wait()
    outer_ref[0], inner_ref[0] = own_edge(early_ref, 0), own_edge(early_ref, 1)


def turn_body(m_ref, inner_ref):
    inner_ref[...] = own_edge(m_ref, 1)


def own_sums(slabs, w_ref, b_ref, acc0_ref, acc1_ref):
    rows, cols = acc0_ref.shape[:2]
    taps = [row_taps(slab, rows) for slab in slabs]
    acc0_ref[...] = b_ref[...] + convolved(taps[0], weight_rows(w_ref, 2), rows, cols)
    weights = weight_rows(w_ref, 1) + weight_rows(w_ref, 2)
    acc1_ref[...] = b_ref[...] + convolved(taps[0] + taps[1], weights, rows, cols)


def near_slab(frame, inner):
    return jnp.where(
        parity() == 0,
        jnp.concatenate([frame, inner], axis=0),
        jnp.concatenate([inner, frame], axis=0),
    )


def own_near_body(early_ref, late_ref, inner_ref, w_ref, b_ref, acc0_ref, acc1_ref):
    slabs = [near_slab(early_ref[...], inner_ref[0]), near_slab(late_ref[...], inner_ref[1])]
    own_sums(slabs, w_ref, b_ref, acc0_ref, acc1_ref)


def own_far_body(tiles, early_ref, late_ref, outer_ref, w_ref, b_ref, acc0_ref, acc1_ref):
    slabs = [outer_slab(outer_ref[f], ref, tiles) for f, ref in enumerate((early_ref, late_ref))]
    own_sums(slabs, w_ref, b_ref, acc0_ref, acc1_ref)


def add_earlier(total_ref, base, product):
    started = lax.axis_index("tm") > 0

    @pl.when(started)
    def _():
        total_ref[...] = base() + product()

    @pl.when(jnp.logical_not(started))
    def _():
        total_ref[...] = base()


def partial_rows(times, h0, h1, v_ref, rows, cols, send_ref):
    has_next = lax.axis_index("tm") < times - 1

    @pl.when(has_next)
    def _():
        both = (h0.astype(jnp.float32) + h1.astype(jnp.float32)).astype(jnp.bfloat16)
        taps = row_taps(both, rows) + row_taps(h1, rows)
        part = convolved(taps, weight_rows(v_ref, 0) + weight_rows(v_ref, 1), rows, cols)
        send_ref[...] = part.astype(jnp.bfloat16)

    @pl.when(jnp.logical_not(has_next))
    def _():
        send_ref[...] = jnp.zeros_like(send_ref)


def near_place(rows):
    return pl.ds(2 * (1 - parity()), rows)


def late_near_body(
    tiles, m_ref, inner_ref, w_ref, _, acc0_ref, acc1_ref, sum0_ref, h1_ref, sum1_ref
):
    rows, cols = m_ref.shape[:2]

    def product(a):
        taps = row_taps(near_slab(m_ref[...], inner_ref[...]), rows)
        return convolved(taps, weight_rows(w_ref, a), rows, cols)

    add_earlier(sum1_ref, lambda: acc1_ref[...], lambda: product(0))
    h1_ref[...] = silu_rows(sum1_ref[...], near_place(rows).start, rows, tiles)
    add_earlier(sum0_ref, lambda: acc0_ref[...], lambda: product(1))


def early_near_body(
    tiles, times, m_ref, inner_ref, w_ref, v_ref, acc0_ref, h1_ref, send_ref, h0_ref, sum0_ref
):
    rows, cols = m_ref.shape[:2]

    def product():
        taps = row_taps(near_slab(m_ref[...], inner_ref[...]), rows)
        return convolved(taps, weight_rows(w_ref, 0), rows, cols)

    add_earlier(sum0_ref, lambda: acc0_ref[...], product)
    h0 = silu_rows(sum0_ref[...], near_place(rows).start, rows, tiles)
    h0_ref[...] = h0
    partial_rows(times, h0, h1_ref[...], v_ref, rows - 2, cols, send_ref)


def far_body(
    tiles, times, early_ref, late_ref, outer_ref, w_ref, v_ref, acc0_ref, acc1_ref, near0_ref,
    near1_ref, send_ref, h0_ref, h1_ref, sum0_ref, sum1_ref,
):
    rows, cols = early_ref.shape[:2]
    odd = parity()
    near, far, side = near_place(rows), pl.ds(odd * rows, 2), pl.ds(odd * (rows - 2), 4)
    h0_ref[near], h1_ref[near] = near0_ref[...], near1_ref[...]

    def taps(f, frame_ref):
        return row_taps(outer_slab(outer_ref[f], frame_ref, tiles), 2)

    def product0():
        weights = weight_rows(w_ref, 0) + weight_rows(w_ref, 1)
        return convolved(taps(0, early_ref) + taps(1, late_ref), weights, 2, cols)

    def product1():
        return convolved(taps(1, late_ref), weight_rows(w_ref, 0), 2, cols)

    add_earlier(sum0_ref, lambda: acc0_ref[...], product0)
    add_earlier(sum1_ref, lambda: acc1_ref[...], product1)
    h0_ref[far] = silu_rows(sum0_ref[...], far.start, rows, tiles)
    h1_ref[far] = silu_rows(sum1_ref[...], far.start, rows, tiles)
    partial_rows(times, h0_ref[side], h1_ref[side], v_ref, 2, cols, send_ref)


def rest_body(early_ref, late_ref, h0_ref, h1_ref, v_ref, b_ref, out_ref):
    rows, cols = early_ref.shape[:2]
    h0, h1 = h0_ref[...], h1_ref[...]
    both = (h0.astype(jnp.float32) + h1.astype(jnp.float32)).astype(jnp.bfloat16)
    taps = row_taps(h0, rows) + row_taps(both, rows)
    part = convolved(taps, weight_rows(v_ref, 1) + weight_rows(v_ref, 2), rows, cols)
    total = early_ref[...].astype(jnp.float32) + late_ref[...].astype(jnp.float32) + part
    out_ref[0] = total * 0.5 + b_ref[...]


def join_body(rest_ref, near_ref, far_ref, out_ref):
    rows = rest_ref.shape[1]
    odd = parity()
    first = lax.axis_index("tm") == 0
    for part_ref, start in ((near_ref, 2 * (1 - odd)), (far_ref, odd * (rows - 2))):
        part = part_ref[...].astype(jnp.float32)
        part = jnp.where(first, jnp.zeros_like(part), part)
        place = pl.ds(start, part.shape[0])
        out_ref[0, place] = (rest_ref[0, place] + 0.5 * part).astype(jnp.bfloat16)


def block(x, weight_first, bias_first, weight_second, bias_second):
    _, rows, cols, channels = x.shape
    tiles, times = lax.axis_size("tile"), lax.axis_size("tm")
    forward = [(i, i + 1) for i in range(times - 1)]
    ring = forward + [(times - 1, 0)]
    inner_pairs = [(i, i + 1) for i in range(0, tiles - 1, 2)]
    outer_pairs = [(i, i + 1) for i in range(1, tiles - 1, 2)]
    inner_pairs += [(j, i) for i, j in inner_pairs]
    outer_pairs += [(j, i) for i, j in outer_pairs]
    unpaired = [(0, tiles - 1), (tiles - 1, 0)] if tiles % 2 == 0 else []
    diagonal = [(i * times + s, j * times + t) for i, j in outer_pairs for s, t in ring]
    diagonal += [(i * times + s, j * times + s) for i, j in unpaired for s in range(times)]

    def frames(*lead, dtype=jnp.bfloat16):
        return jax.ShapeDtypeStruct((*lead, cols, channels), dtype)

    f32 = jnp.float32
    x = pltpu.with_memory_space_constraint(x, pltpu.HBM)
    dma = [pltpu.SemaphoreType.DMA(())]
    (late,) = call(cut_body, [frames(rows)], (x,), 0, in_specs=[HBM], scratch=dma)
    late_before = lax.ppermute(late, "tm", ring)
    early, outer_edge, inner_edge = call(
        edges_body,
        [frames(rows), frames(2, 2), frames(2, 2)],
        (x, late),
        10**10,
        in_specs=[HBM, VMEM],
        scratch=dma,
    )
    inner = lax.ppermute(inner_edge, "tile", inner_pairs)
    outer = lax.ppermute(outer_edge, "tile", outer_pairs + unpaired)
    early_before = lax.ppermute(early, "tm", forward)
    corner = lax.ppermute(outer_edge, ("tile", "tm"), diagonal)

    bias_first = bias_first.reshape(1, 1, -1)
    bias_second = bias_second.reshape(1, 1, -1)
    unit = 2 * 9 * channels * channels * cols
    wide = rows + 2
    sums0, sums1 = call(
        own_near_body,
        [frames(rows, dtype=f32), frames(rows, dtype=f32)],
        (early, late, inner, weight_first, bias_first),
        3 * unit * rows,
    )
    far0, far1 = call(
        functools.partial(own_far_body, tiles),
        [frames(2, dtype=f32), frames(2, dtype=f32)],
        (early, late, outer, weight_first, bias_first),
        0,
    )

    def sums(count, frame_count):
        return [pltpu.VMEM((count, cols, channels), f32)] * frame_count

    (edge,) = call(turn_body, [frames(2)], (late_before,), 0)
    late_inner = lax.ppermute(edge, "tile", inner_pairs)
    sums0, near1 = call(
        functools.partial(late_near_body, tiles),
        [frames(rows, dtype=f32), frames(rows)],
        (late_before, late_inner, weight_first, weight_second, sums0, sums1),
        0,
        scratch=sums(rows, 1),
    )
    (edge,) = call(turn_body, [frames(2)], (early_before,), 0)
    early_inner = lax.ppermute(edge, "tile", inner_pairs)
    near_send, near0 = call(
        functools.partial(early_near_body, tiles, times),
        [frames(rows - 2), frames(rows)],
        (early_before, early_inner, weight_first, weight_second, sums0, near1),
        0,
        scratch=sums(rows, 1),
    )
    near_part = lax.ppermute(near_send, "tm", ring)
    far_send, h0, h1 = call(
        functools.partial(far_body, tiles, times),
        [frames(2), frames(wide), frames(wide)],
        (
            early_before, late_before, corner, weight_first, weight_second, far0, far1, near0,
            near1,
        ),
        0,
        scratch=sums(2, 2),
    )
    far_part = lax.ppermute(far_send, "tm", ring)
    (rest,) = call(
        rest_body,
        [frames(1, rows, dtype=f32)],
        (early, late, h0, h1, weight_second, bias_second),
        2 * unit * rows,
    )
    (pooled,) = call(join_body, [frames(1, rows)], (rest, near_part, far_part), 0)
    return pooled


def solution(mesh):
    in_specs = (P(("clips", "tm"), "tile", None, None), P(), P(), P(), P())
    out_specs = P(("clips", "tm"), "tile", None, None)
    return jax.shard_map(block, mesh=mesh, in_specs=in_specs, out_specs=out_specs, check_vma=False)
```

```python
import functools

import jax
import jax.numpy as jnp
from jax import lax
from jax.experimental import pallas as pl
from jax.experimental.pallas import tpu as pltpu
from jax.sharding import PartitionSpec as P


VMEM = pl.BlockSpec(memory_space=pltpu.VMEM)
HBM = pl.BlockSpec(memory_space=pltpu.HBM)


def call(body, outs, args, flops, in_specs=None, scratch=()):
    return pl.pallas_call(
        body,
        out_shape=outs,
        in_specs=in_specs or [VMEM] * len(args),
        out_specs=[VMEM] * len(outs),
        scratch_shapes=scratch,
        compiler_params=pltpu.CompilerParams(vmem_limit_bytes=16 << 20),
        cost_estimate=pl.CostEstimate(flops=flops, bytes_accessed=0, transcendentals=0),
    )(*args)


def flat(value):
    return value.reshape(-1, value.shape[-1])


def row_taps(slab, rows):
    return [flat(slab[p : p + rows]) for p in range(3)]


def convolved(lhs, weights, rows, cols):
    stacked = jnp.concatenate(lhs, axis=1)
    total = None
    for q in range(3):
        taps = jnp.concatenate([w[q] for w in weights], axis=0)
        part = jnp.dot(stacked, taps, preferred_element_type=jnp.float32)
        part = part.reshape(rows, cols, part.shape[-1])
        if q != 1:
            col = lax.broadcasted_iota(jnp.int32, part.shape, 1)
            edge = 0 if q == 0 else cols - 1
            part = jnp.where(col == edge, 0.0, pltpu.roll(part, 1 if q == 0 else cols - 1, 1))
        total = part if total is None else total + part
    return total


def parity():
    return lax.rem(lax.axis_index("tile"), 2)


def either(first, second):
    even = parity() == 0
    return jnp.concatenate([jnp.where(even, a, b) for a, b in zip(first, second)], axis=0)


def own_edge(own, side):
    odd = parity()
    last = own.shape[0] - 2
    return own[pl.ds((odd if side == 0 else 1 - odd) * last, 2)]


def outer_slab(outer, own, tiles):
    tile = lax.axis_index("tile")
    beyond = (tile == 0) | ((tile == tiles - 1) & (parity() == 1))
    outer = jnp.where(beyond, jnp.zeros_like(outer), outer)
    edge = own_edge(own, 0)
    return either([outer, edge], [edge, outer])


def inner_slab(inner, own):
    edge = own_edge(own, 1)
    return either([edge, inner], [inner, edge])


def places(rows):
    odd = parity()
    return pl.ds(2, rows - 2), pl.ds((1 - odd) * rows, 2), pl.ds(odd * rows, 2)


def weight_rows(w_ref, a):
    return [[w_ref[a, p, q] for q in range(3)] for p in range(3)]


def silu_rows(value, start, rows, tiles):
    hidden = (value / (1.0 + jnp.exp(-value))).astype(jnp.bfloat16)
    row = lax.broadcasted_iota(jnp.int32, hidden.shape, 0) + start
    row = row + lax.axis_index("tile") * rows - 1
    inside = (row >= 0) & (row < tiles * rows)
    return jnp.where(inside, hidden, jnp.zeros_like(hidden))


def edges_body(x_ref, own_ref, outer_ref, inner_ref, sem):
    copy = pltpu.make_async_copy(x_ref, own_ref, sem)
    copy.start()
    copy.wait()
    for f in range(2):
        outer_ref[f] = own_edge(own_ref.at[f], 0)
        inner_ref[f] = own_edge(own_ref.at[f], 1)


def turn_body(m_ref, inner_ref):
    for f in range(2):
        inner_ref[f] = own_edge(m_ref.at[f], 1)


def own_sums(slabs, w_ref, b_ref, acc0_ref, acc1_ref):
    rows, cols = acc0_ref.shape[:2]
    taps = [row_taps(slab, rows) for slab in slabs]
    acc0_ref[...] = b_ref[...] + convolved(taps[0], weight_rows(w_ref, 2), rows, cols)
    weights = weight_rows(w_ref, 1) + weight_rows(w_ref, 2)
    acc1_ref[...] = b_ref[...] + convolved(taps[0] + taps[1], weights, rows, cols)


def own_near_body(x_ref, inner_ref, w_ref, b_ref, acc0_ref, acc1_ref):
    even = parity() == 0
    slabs = []
    for f in range(2):
        below = jnp.concatenate([x_ref[f], inner_ref[f]], axis=0)
        above = jnp.concatenate([inner_ref[f], x_ref[f]], axis=0)
        slabs.append(jnp.where(even, below, above))
    own_sums(slabs, w_ref, b_ref, acc0_ref, acc1_ref)


def own_far_body(tiles, x_ref, outer_ref, w_ref, b_ref, acc0_ref, acc1_ref):
    slabs = [outer_slab(outer_ref[f], x_ref.at[f], tiles) for f in range(2)]
    own_sums(slabs, w_ref, b_ref, acc0_ref, acc1_ref)


def hidden(slab, bases, places_of, w_ref, tiles, whole, h0_ref, h1_ref, sum0_ref, sum1_ref):
    rows, cols = sum0_ref.shape[:2]
    started = lax.axis_index("tm") > 0

    @pl.when(started)
    def _():
        taps = [row_taps(slab(f), rows) for f in range(2)]
        weights = weight_rows(w_ref, 0) + weight_rows(w_ref, 1)
        sum0_ref[...] = bases[0]() + convolved(taps[0] + taps[1], weights, rows, cols)
        sum1_ref[...] = bases[1]() + convolved(taps[1], weight_rows(w_ref, 0), rows, cols)

    @pl.when(jnp.logical_not(started))
    def _():
        sum0_ref[...] = bases[0]()
        sum1_ref[...] = bases[1]()

    h0_ref[...] = silu_rows(sum0_ref[...], places_of.start, whole, tiles)
    h1_ref[...] = silu_rows(sum1_ref[...], places_of.start, whole, tiles)


def from_near(acc_ref, start, rows):
    return lambda: acc_ref[pl.ds(start, rows)]


def middle_body(tiles, m_ref, w_ref, _, acc0_ref, acc1_ref, h0_ref, h1_ref, sum0_ref, sum1_ref):
    rows = m_ref.shape[1]
    start = 2 * parity()
    bases = [from_near(acc_ref, start, rows - 2) for acc_ref in (acc0_ref, acc1_ref)]
    place = places(rows)[0]
    hidden(lambda f: m_ref[f], bases, place, w_ref, tiles, rows, h0_ref, h1_ref, sum0_ref, sum1_ref)


def partial_rows(times, h0, h1, v_ref, rows, cols, send_ref):
    has_next = lax.axis_index("tm") < times - 1

    @pl.when(has_next)
    def _():
        both = (h0.astype(jnp.float32) + h1.astype(jnp.float32)).astype(jnp.bfloat16)
        taps = row_taps(both, rows) + row_taps(h1, rows)
        part = convolved(taps, weight_rows(v_ref, 0) + weight_rows(v_ref, 1), rows, cols)
        send_ref[...] = part.astype(jnp.bfloat16)

    @pl.when(jnp.logical_not(has_next))
    def _():
        send_ref[...] = jnp.zeros_like(send_ref)


def near_body(
    tiles, times, m_ref, inner_ref, w_ref, v_ref, acc0_ref, acc1_ref, mid0_ref, mid1_ref,
    send_ref, h0_ref, h1_ref, sum0_ref, sum1_ref,
):
    rows, cols = m_ref.shape[1:3]
    odd = parity()
    start = (1 - odd) * (rows - 2)
    bases = [from_near(acc_ref, start, 2) for acc_ref in (acc0_ref, acc1_ref)]
    place = places(rows)[1]

    def slab(f):
        return inner_slab(inner_ref[f], m_ref.at[f])

    middle, near = pl.ds(2 * odd, rows - 2), pl.ds(start, 2)
    h0_ref[middle], h1_ref[middle] = mid0_ref[...], mid1_ref[...]
    hidden(
        slab, bases, place, w_ref, tiles, rows, h0_ref.at[near], h1_ref.at[near], sum0_ref,
        sum1_ref,
    )
    partial_rows(times, h0_ref[...], h1_ref[...], v_ref, rows - 2, cols, send_ref)


def far_body(
    tiles, times, m_ref, outer_ref, w_ref, v_ref, acc0_ref, acc1_ref, near0_ref, near1_ref,
    send_ref, h0_ref, h1_ref, sum0_ref, sum1_ref,
):
    rows, cols = m_ref.shape[1:3]
    odd = parity()
    far = places(rows)[2]
    near = pl.ds(2 * (1 - odd), rows)

    def slab(f):
        return outer_slab(outer_ref[f], m_ref.at[f], tiles)

    bases = [lambda: acc0_ref[...], lambda: acc1_ref[...]]
    h0_ref[near], h1_ref[near] = near0_ref[...], near1_ref[...]
    hidden(
        slab, bases, far, w_ref, tiles, rows, h0_ref.at[far], h1_ref.at[far], sum0_ref, sum1_ref
    )
    side = pl.ds(odd * (rows - 2), 4)
    partial_rows(times, h0_ref[side], h1_ref[side], v_ref, 2, cols, send_ref)


def rest_body(x_ref, h0_ref, h1_ref, v_ref, b_ref, out_ref):
    rows, cols = x_ref.shape[1:3]
    h0, h1 = h0_ref[...], h1_ref[...]
    both = (h0.astype(jnp.float32) + h1.astype(jnp.float32)).astype(jnp.bfloat16)
    taps = row_taps(h0, rows) + row_taps(both, rows)
    part = convolved(taps, weight_rows(v_ref, 1) + weight_rows(v_ref, 2), rows, cols)
    total = x_ref[0].astype(jnp.float32) + x_ref[1].astype(jnp.float32) + part
    out_ref[0] = total * 0.5 + b_ref[...]


def join_body(rest_ref, near_ref, far_ref, out_ref):
    rows = rest_ref.shape[1]
    odd = parity()
    first = lax.axis_index("tm") == 0
    for part_ref, start in ((near_ref, 2 * (1 - odd)), (far_ref, odd * (rows - 2))):
        part = part_ref[...].astype(jnp.float32)
        part = jnp.where(first, jnp.zeros_like(part), part)
        place = pl.ds(start, part.shape[0])
        out_ref[0, place] = (rest_ref[0, place] + 0.5 * part).astype(jnp.bfloat16)


def block(x, weight_first, bias_first, weight_second, bias_second):
    _, rows, cols, channels = x.shape
    clips, tiles, times = (lax.axis_size(axis) for axis in ("clips", "tile", "tm"))
    forward = [(i, i + 1) for i in range(times - 1)]
    ring = forward + [(times - 1, 0)]
    inner_pairs = [(i, i + 1) for i in range(0, tiles - 1, 2)]
    outer_pairs = [(i, i + 1) for i in range(1, tiles - 1, 2)]
    inner_pairs += [(j, i) for i, j in inner_pairs]
    outer_pairs += [(j, i) for i, j in outer_pairs]
    paired = {i for i, _ in outer_pairs}
    unpaired = [i for i in range(tiles) if i not in paired]
    outer_full = [(c * tiles + i, c * tiles + j) for c in range(clips) for i, j in outer_pairs]
    outer_full += [(c * tiles + i, (c + 1) % clips * tiles + i) for c in range(clips) for i in unpaired]
    diagonal = [(i * times + s, j * times + t) for i, j in outer_pairs for s, t in forward]

    def frames(*lead, dtype=jnp.bfloat16):
        return jax.ShapeDtypeStruct((*lead, cols, channels), dtype)

    f32 = jnp.float32
    earlier = lax.ppermute(x, "tm", ring)
    x, outer_edge, inner_edge = call(
        edges_body,
        [frames(2, rows), frames(2, 2), frames(2, 2)],
        (pltpu.with_memory_space_constraint(x, pltpu.HBM),),
        10**10,
        in_specs=[HBM],
        scratch=[pltpu.SemaphoreType.DMA(())],
    )
    inner = lax.ppermute(inner_edge, "tile", inner_pairs)
    outer = lax.ppermute(outer_edge, ("clips", "tile"), outer_full)
    corner = lax.ppermute(outer_edge, ("tile", "tm"), diagonal)

    bias_first = bias_first.reshape(1, 1, -1)
    bias_second = bias_second.reshape(1, 1, -1)
    unit = 2 * 9 * channels * channels * cols
    wide = rows + 2
    sums0, sums1 = call(
        own_near_body,
        [frames(rows, dtype=f32), frames(rows, dtype=f32)],
        (x, inner, weight_first, bias_first),
        3 * unit * rows,
    )
    far0, far1 = call(
        functools.partial(own_far_body, tiles),
        [frames(2, dtype=f32), frames(2, dtype=f32)],
        (x, outer, weight_first, bias_first),
        0,
    )
    (inner_edge,) = call(turn_body, [frames(2, 2)], (earlier,), 0)
    inner_corner = lax.ppermute(inner_edge, "tile", inner_pairs)

    def sums(count):
        return [pltpu.VMEM((count, cols, channels), f32)] * 2

    mid0, mid1 = call(
        functools.partial(middle_body, tiles),
        [frames(rows - 2), frames(rows - 2)],
        (earlier, weight_first, weight_second, sums0, sums1),
        0,
        scratch=sums(rows - 2),
    )
    near_send, near0, near1 = call(
        functools.partial(near_body, tiles, times),
        [frames(rows - 2), frames(rows), frames(rows)],
        (earlier, inner_corner, weight_first, weight_second, sums0, sums1, mid0, mid1),
        0,
        scratch=sums(2),
    )
    near_part = lax.ppermute(near_send, "tm", ring)
    far_send, h0, h1 = call(
        functools.partial(far_body, tiles, times),
        [frames(2), frames(wide), frames(wide)],
        (earlier, corner, weight_first, weight_second, far0, far1, near0, near1),
        0,
        scratch=sums(2),
    )
    far_part = lax.ppermute(far_send, "tm", forward)
    (rest,) = call(
        rest_body,
        [frames(1, rows, dtype=f32)],
        (x, h0, h1, weight_second, bias_second),
        2 * unit * rows,
    )
    (pooled,) = call(join_body, [frames(1, rows)], (rest, near_part, far_part), 0)
    return pooled


def solution(mesh):
    in_specs = (P(("clips", "tm"), "tile", None, None), P(), P(), P(), P())
    out_specs = P(("clips", "tm"), "tile", None, None)
    return jax.shard_map(block, mesh=mesh, in_specs=in_specs, out_specs=out_specs, check_vma=False)
```

```python
import functools

import jax
import jax.numpy as jnp
from jax import lax
from jax.experimental import pallas as pl
from jax.experimental.pallas import tpu as pltpu
from jax.sharding import PartitionSpec as P


VMEM = pl.BlockSpec(memory_space=pltpu.VMEM)
HBM = pl.BlockSpec(memory_space=pltpu.HBM)


def call(body, outs, args, flops, in_specs=None, scratch=()):
    return pl.pallas_call(
        body,
        out_shape=outs,
        in_specs=in_specs or [VMEM] * len(args),
        out_specs=[VMEM] * len(outs),
        scratch_shapes=scratch,
        compiler_params=pltpu.CompilerParams(vmem_limit_bytes=16 << 20),
        cost_estimate=pl.CostEstimate(flops=flops, bytes_accessed=0, transcendentals=0),
    )(*args)


def flat(value):
    return value.reshape(-1, value.shape[-1])


def row_taps(slab, rows):
    return [flat(slab[p : p + rows]) for p in range(3)]


def convolved(lhs, weights, rows, cols):
    stacked = jnp.concatenate(lhs, axis=1)
    total = None
    for q in range(3):
        taps = jnp.concatenate([w[q] for w in weights], axis=0)
        part = jnp.dot(stacked, taps, preferred_element_type=jnp.float32)
        part = part.reshape(rows, cols, part.shape[-1])
        if q != 1:
            col = lax.broadcasted_iota(jnp.int32, part.shape, 1)
            edge = 0 if q == 0 else cols - 1
            part = jnp.where(col == edge, 0.0, pltpu.roll(part, 1 if q == 0 else cols - 1, 1))
        total = part if total is None else total + part
    return total


def parity():
    return lax.rem(lax.axis_index("tile"), 2)


def either(first, second):
    even = parity() == 0
    return jnp.concatenate([jnp.where(even, a, b) for a, b in zip(first, second)], axis=0)


def own_edge(own, side):
    odd = parity()
    last = own.shape[0] - 2
    return own[pl.ds((odd if side == 0 else 1 - odd) * last, 2)]


def outer_slab(outer, own, tiles):
    tile = lax.axis_index("tile")
    beyond = (tile == 0) | ((tile == tiles - 1) & (parity() == 1))
    outer = jnp.where(beyond, jnp.zeros_like(outer), outer)
    edge = own_edge(own, 0)
    return either([outer, edge], [edge, outer])


def inner_slab(inner, own):
    edge = own_edge(own, 1)
    return either([edge, inner], [inner, edge])


def places(rows):
    odd = parity()
    return pl.ds(2, rows - 2), pl.ds((1 - odd) * rows, 2), pl.ds(odd * rows, 2)


def weight_rows(w_ref, a):
    return [[w_ref[a, p, q] for q in range(3)] for p in range(3)]


def silu_rows(value, start, rows, tiles):
    hidden = (value / (1.0 + jnp.exp(-value))).astype(jnp.bfloat16)
    row = lax.broadcasted_iota(jnp.int32, hidden.shape, 0) + start
    row = row + lax.axis_index("tile") * rows - 1
    inside = (row >= 0) & (row < tiles * rows)
    return jnp.where(inside, hidden, jnp.zeros_like(hidden))


def edges_body(x_ref, own_ref, outer_ref, inner_ref, sem):
    copy = pltpu.make_async_copy(x_ref, own_ref, sem)
    copy.start()
    copy.wait()
    for f in range(2):
        outer_ref[f] = own_edge(own_ref.at[f], 0)
        inner_ref[f] = own_edge(own_ref.at[f], 1)


def turn_body(m_ref, inner_ref):
    for f in range(2):
        inner_ref[f] = own_edge(m_ref.at[f], 1)


def own_sums(slabs, w_ref, b_ref, acc0_ref, acc1_ref):
    rows, cols = acc0_ref.shape[:2]
    taps = [row_taps(slab, rows) for slab in slabs]
    acc0_ref[...] = b_ref[...] + convolved(taps[0], weight_rows(w_ref, 2), rows, cols)
    weights = weight_rows(w_ref, 1) + weight_rows(w_ref, 2)
    acc1_ref[...] = b_ref[...] + convolved(taps[0] + taps[1], weights, rows, cols)


def own_near_body(x_ref, inner_ref, w_ref, b_ref, acc0_ref, acc1_ref):
    even = parity() == 0
    slabs = []
    for f in range(2):
        below = jnp.concatenate([x_ref[f], inner_ref[f]], axis=0)
        above = jnp.concatenate([inner_ref[f], x_ref[f]], axis=0)
        slabs.append(jnp.where(even, below, above))
    own_sums(slabs, w_ref, b_ref, acc0_ref, acc1_ref)


def own_far_body(tiles, x_ref, outer_ref, w_ref, b_ref, acc0_ref, acc1_ref):
    slabs = [outer_slab(outer_ref[f], x_ref.at[f], tiles) for f in range(2)]
    own_sums(slabs, w_ref, b_ref, acc0_ref, acc1_ref)


def hidden(slab, bases, places_of, w_ref, tiles, whole, h0_ref, h1_ref, sum0_ref, sum1_ref):
    rows, cols = sum0_ref.shape[:2]
    started = lax.axis_index("tm") > 0

    @pl.when(started)
    def _():
        taps = [row_taps(slab(f), rows) for f in range(2)]
        weights = weight_rows(w_ref, 0) + weight_rows(w_ref, 1)
        sum0_ref[...] = bases[0]() + convolved(taps[0] + taps[1], weights, rows, cols)
        sum1_ref[...] = bases[1]() + convolved(taps[1], weight_rows(w_ref, 0), rows, cols)

    @pl.when(jnp.logical_not(started))
    def _():
        sum0_ref[...] = bases[0]()
        sum1_ref[...] = bases[1]()

    h0_ref[...] = silu_rows(sum0_ref[...], places_of.start, whole, tiles)
    h1_ref[...] = silu_rows(sum1_ref[...], places_of.start, whole, tiles)


def from_near(acc_ref, start, rows):
    return lambda: acc_ref[pl.ds(start, rows)]


def middle_body(tiles, m_ref, w_ref, _, acc0_ref, acc1_ref, h0_ref, h1_ref, sum0_ref, sum1_ref):
    rows = m_ref.shape[1]
    start = 2 * parity()
    bases = [from_near(acc_ref, start, rows - 2) for acc_ref in (acc0_ref, acc1_ref)]
    place = places(rows)[0]
    hidden(lambda f: m_ref[f], bases, place, w_ref, tiles, rows, h0_ref, h1_ref, sum0_ref, sum1_ref)


def partial_rows(times, h0, h1, v_ref, rows, cols, send_ref):
    has_next = lax.axis_index("tm") < times - 1

    @pl.when(has_next)
    def _():
        both = (h0.astype(jnp.float32) + h1.astype(jnp.float32)).astype(jnp.bfloat16)
        taps = row_taps(both, rows) + row_taps(h1, rows)
        part = convolved(taps, weight_rows(v_ref, 0) + weight_rows(v_ref, 1), rows, cols)
        send_ref[...] = part.astype(jnp.bfloat16)

    @pl.when(jnp.logical_not(has_next))
    def _():
        send_ref[...] = jnp.zeros_like(send_ref)


def near_body(
    tiles, times, m_ref, inner_ref, w_ref, v_ref, acc0_ref, acc1_ref, mid0_ref, mid1_ref,
    send_ref, h0_ref, h1_ref, sum0_ref, sum1_ref,
):
    rows, cols = m_ref.shape[1:3]
    odd = parity()
    start = (1 - odd) * (rows - 2)
    bases = [from_near(acc_ref, start, 2) for acc_ref in (acc0_ref, acc1_ref)]
    place = places(rows)[1]

    def slab(f):
        return inner_slab(inner_ref[f], m_ref.at[f])

    middle, near = pl.ds(2 * odd, rows - 2), pl.ds(start, 2)
    h0_ref[middle], h1_ref[middle] = mid0_ref[...], mid1_ref[...]
    hidden(
        slab, bases, place, w_ref, tiles, rows, h0_ref.at[near], h1_ref.at[near], sum0_ref,
        sum1_ref,
    )
    partial_rows(times, h0_ref[...], h1_ref[...], v_ref, rows - 2, cols, send_ref)


def far_body(
    tiles, times, m_ref, outer_ref, w_ref, v_ref, acc0_ref, acc1_ref, near0_ref, near1_ref,
    send_ref, h0_ref, h1_ref, sum0_ref, sum1_ref,
):
    rows, cols = m_ref.shape[1:3]
    odd = parity()
    far = places(rows)[2]
    near = pl.ds(2 * (1 - odd), rows)

    def slab(f):
        return outer_slab(outer_ref[f], m_ref.at[f], tiles)

    bases = [lambda: acc0_ref[...], lambda: acc1_ref[...]]
    h0_ref[near], h1_ref[near] = near0_ref[...], near1_ref[...]
    hidden(
        slab, bases, far, w_ref, tiles, rows, h0_ref.at[far], h1_ref.at[far], sum0_ref, sum1_ref
    )
    side = pl.ds(odd * (rows - 2), 4)
    partial_rows(times, h0_ref[side], h1_ref[side], v_ref, 2, cols, send_ref)


def rest_body(x_ref, h0_ref, h1_ref, v_ref, b_ref, out_ref):
    rows, cols = x_ref.shape[1:3]
    h0, h1 = h0_ref[...], h1_ref[...]
    both = (h0.astype(jnp.float32) + h1.astype(jnp.float32)).astype(jnp.bfloat16)
    taps = row_taps(h0, rows) + row_taps(both, rows)
    part = convolved(taps, weight_rows(v_ref, 1) + weight_rows(v_ref, 2), rows, cols)
    total = x_ref[0].astype(jnp.float32) + x_ref[1].astype(jnp.float32) + part
    out_ref[0] = total * 0.5 + b_ref[...]


def join_body(rest_ref, near_ref, odd_ref, even_ref, out_ref):
    rows = rest_ref.shape[1]
    odd = parity()
    time = lax.axis_index("tm")
    far = jnp.where(lax.rem(time, 2) == 1, odd_ref[...], even_ref[...])
    for part, start in ((near_ref[...], 2 * (1 - odd)), (far, odd * (rows - 2))):
        part = jnp.where(time == 0, jnp.zeros_like(part), part).astype(jnp.float32)
        place = pl.ds(start, part.shape[0])
        out_ref[0, place] = (rest_ref[0, place] + 0.5 * part).astype(jnp.bfloat16)


def block(x, weight_first, bias_first, weight_second, bias_second):
    _, rows, cols, channels = x.shape
    clips, tiles, times = (lax.axis_size(axis) for axis in ("clips", "tile", "tm"))
    forward = [(i, i + 1) for i in range(times - 1)]
    ring = forward + [(times - 1, 0)]
    inner_pairs = [(i, i + 1) for i in range(0, tiles - 1, 2)]
    outer_pairs = [(i, i + 1) for i in range(1, tiles - 1, 2)]
    inner_pairs += [(j, i) for i, j in inner_pairs]
    outer_pairs += [(j, i) for i, j in outer_pairs]
    paired = {i for i, _ in outer_pairs}
    unpaired = [i for i in range(tiles) if i not in paired]
    outer_full = [(c * tiles + i, c * tiles + j) for c in range(clips) for i, j in outer_pairs]
    outer_full += [(c * tiles + i, (c + 1) % clips * tiles + i) for c in range(clips) for i in unpaired]
    diagonal = [(i * times + s, j * times + t) for i, j in outer_pairs for s, t in forward]

    def swaps(first):
        turns = {}
        for t in range(first, times - 1, 2):
            turns[t], turns[t + 1] = t + 1, t
        return [
            (c * times + t, c * times + turns[t] if t in turns else (c + 1) % clips * times + t)
            for c in range(clips)
            for t in range(times)
        ]

    def frames(*lead, dtype=jnp.bfloat16):
        return jax.ShapeDtypeStruct((*lead, cols, channels), dtype)

    f32 = jnp.float32
    earlier = lax.ppermute(x, "tm", ring)
    x, outer_edge, inner_edge = call(
        edges_body,
        [frames(2, rows), frames(2, 2), frames(2, 2)],
        (pltpu.with_memory_space_constraint(x, pltpu.HBM),),
        10**10,
        in_specs=[HBM],
        scratch=[pltpu.SemaphoreType.DMA(())],
    )
    inner = lax.ppermute(inner_edge, "tile", inner_pairs)
    outer = lax.ppermute(outer_edge, ("clips", "tile"), outer_full)
    corner = lax.ppermute(outer_edge, ("tile", "tm"), diagonal)

    bias_first = bias_first.reshape(1, 1, -1)
    bias_second = bias_second.reshape(1, 1, -1)
    unit = 2 * 9 * channels * channels * cols
    wide = rows + 2
    sums0, sums1 = call(
        own_near_body,
        [frames(rows, dtype=f32), frames(rows, dtype=f32)],
        (x, inner, weight_first, bias_first),
        3 * unit * rows,
    )
    far0, far1 = call(
        functools.partial(own_far_body, tiles),
        [frames(2, dtype=f32), frames(2, dtype=f32)],
        (x, outer, weight_first, bias_first),
        0,
    )
    (inner_edge,) = call(turn_body, [frames(2, 2)], (earlier,), 0)
    inner_corner = lax.ppermute(inner_edge, "tile", inner_pairs)

    def sums(count):
        return [pltpu.VMEM((count, cols, channels), f32)] * 2

    mid0, mid1 = call(
        functools.partial(middle_body, tiles),
        [frames(rows - 2), frames(rows - 2)],
        (earlier, weight_first, weight_second, sums0, sums1),
        0,
        scratch=sums(rows - 2),
    )
    near_send, near0, near1 = call(
        functools.partial(near_body, tiles, times),
        [frames(rows - 2), frames(rows), frames(rows)],
        (earlier, inner_corner, weight_first, weight_second, sums0, sums1, mid0, mid1),
        0,
        scratch=sums(2),
    )
    near_part = lax.ppermute(near_send, "tm", ring)
    far_send, h0, h1 = call(
        functools.partial(far_body, tiles, times),
        [frames(2), frames(wide), frames(wide)],
        (earlier, corner, weight_first, weight_second, far0, far1, near0, near1),
        0,
        scratch=sums(2),
    )
    far_odd = lax.ppermute(far_send, ("clips", "tm"), swaps(0))
    far_even = lax.ppermute(far_send, ("clips", "tm"), swaps(1))
    (rest,) = call(
        rest_body,
        [frames(1, rows, dtype=f32)],
        (x, h0, h1, weight_second, bias_second),
        2 * unit * rows,
    )
    (pooled,) = call(join_body, [frames(1, rows)], (rest, near_part, far_odd, far_even), 0)
    return pooled


def solution(mesh):
    in_specs = (P(("clips", "tm"), "tile", None, None), P(), P(), P(), P())
    out_specs = P(("clips", "tm"), "tile", None, None)
    return jax.shard_map(block, mesh=mesh, in_specs=in_specs, out_specs=out_specs, check_vma=False)
```

```python
import functools

import jax
import jax.numpy as jnp
from jax import lax
from jax.experimental import pallas as pl
from jax.experimental.pallas import tpu as pltpu
from jax.sharding import PartitionSpec as P


VMEM = pl.BlockSpec(memory_space=pltpu.VMEM)
HBM = pl.BlockSpec(memory_space=pltpu.HBM)


def call(body, outs, args, flops, in_specs=None, scratch=()):
    return pl.pallas_call(
        body,
        out_shape=outs,
        in_specs=in_specs or [VMEM] * len(args),
        out_specs=[VMEM] * len(outs),
        scratch_shapes=scratch,
        compiler_params=pltpu.CompilerParams(vmem_limit_bytes=16 << 20),
        cost_estimate=pl.CostEstimate(flops=flops, bytes_accessed=0, transcendentals=0),
    )(*args)


def flat(value):
    return value.reshape(-1, value.shape[-1])


def row_taps(slab, rows):
    return [flat(slab[p : p + rows]) for p in range(3)]


def convolved(lhs, weights, rows, cols):
    stacked = jnp.concatenate(lhs, axis=1)
    total = None
    for q in range(3):
        taps = jnp.concatenate([w[q] for w in weights], axis=0)
        part = jnp.dot(stacked, taps, preferred_element_type=jnp.float32)
        part = part.reshape(rows, cols, part.shape[-1])
        if q != 1:
            col = lax.broadcasted_iota(jnp.int32, part.shape, 1)
            edge = 0 if q == 0 else cols - 1
            part = jnp.where(col == edge, 0.0, pltpu.roll(part, 1 if q == 0 else cols - 1, 1))
        total = part if total is None else total + part
    return total


def parity():
    return lax.rem(lax.axis_index("tile"), 2)


def either(first, second):
    even = parity() == 0
    return jnp.concatenate([jnp.where(even, a, b) for a, b in zip(first, second)], axis=0)


def own_edge(own, side):
    odd = parity()
    last = own.shape[0] - 2
    return own[pl.ds((odd if side == 0 else 1 - odd) * last, 2)]


def outer_slab(outer, own, tiles):
    tile = lax.axis_index("tile")
    beyond = (tile == 0) | ((tile == tiles - 1) & (parity() == 1))
    outer = jnp.where(beyond, jnp.zeros_like(outer), outer)
    edge = own_edge(own, 0)
    return either([outer, edge], [edge, outer])


def inner_slab(inner, own):
    edge = own_edge(own, 1)
    return either([edge, inner], [inner, edge])


def places(rows):
    odd = parity()
    return pl.ds(2, rows - 2), pl.ds((1 - odd) * rows, 2), pl.ds(odd * rows, 2)


def weight_rows(w_ref, a):
    return [[w_ref[a, p, q] for q in range(3)] for p in range(3)]


def silu_rows(value, start, rows, tiles):
    hidden = (value / (1.0 + jnp.exp(-value))).astype(jnp.bfloat16)
    row = lax.broadcasted_iota(jnp.int32, hidden.shape, 0) + start
    row = row + lax.axis_index("tile") * rows - 1
    inside = (row >= 0) & (row < tiles * rows)
    return jnp.where(inside, hidden, jnp.zeros_like(hidden))


def edges_body(x_ref, own_ref, outer_ref, inner_ref, sem):
    copy = pltpu.make_async_copy(x_ref, own_ref, sem)
    copy.start()
    copy.wait()
    for f in range(2):
        outer_ref[f] = own_edge(own_ref.at[f], 0)
        inner_ref[f] = own_edge(own_ref.at[f], 1)


def turn_body(m_ref, inner_ref):
    for f in range(2):
        inner_ref[f] = own_edge(m_ref.at[f], 1)


def own_sums(slabs, w_ref, b_ref, acc0_ref, acc1_ref):
    rows, cols = acc0_ref.shape[:2]
    taps = [row_taps(slab, rows) for slab in slabs]
    acc0_ref[...] = b_ref[...] + convolved(taps[0], weight_rows(w_ref, 2), rows, cols)
    weights = weight_rows(w_ref, 1) + weight_rows(w_ref, 2)
    acc1_ref[...] = b_ref[...] + convolved(taps[0] + taps[1], weights, rows, cols)


def own_near_body(x_ref, inner_ref, w_ref, b_ref, acc0_ref, acc1_ref):
    even = parity() == 0
    slabs = []
    for f in range(2):
        below = jnp.concatenate([x_ref[f], inner_ref[f]], axis=0)
        above = jnp.concatenate([inner_ref[f], x_ref[f]], axis=0)
        slabs.append(jnp.where(even, below, above))
    own_sums(slabs, w_ref, b_ref, acc0_ref, acc1_ref)


def own_far_body(tiles, x_ref, outer_ref, w_ref, b_ref, acc0_ref, acc1_ref):
    slabs = [outer_slab(outer_ref[f], x_ref.at[f], tiles) for f in range(2)]
    own_sums(slabs, w_ref, b_ref, acc0_ref, acc1_ref)


def hidden(slab, bases, places_of, w_ref, tiles, whole, h0_ref, h1_ref, sum0_ref, sum1_ref):
    rows, cols = sum0_ref.shape[:2]
    started = lax.axis_index("tm") > 0

    @pl.when(started)
    def _():
        taps = [row_taps(slab(f), rows) for f in range(2)]
        weights = weight_rows(w_ref, 0) + weight_rows(w_ref, 1)
        sum0_ref[...] = bases[0]() + convolved(taps[0] + taps[1], weights, rows, cols)
        sum1_ref[...] = bases[1]() + convolved(taps[1], weight_rows(w_ref, 0), rows, cols)

    @pl.when(jnp.logical_not(started))
    def _():
        sum0_ref[...] = bases[0]()
        sum1_ref[...] = bases[1]()

    h0_ref[...] = silu_rows(sum0_ref[...], places_of.start, whole, tiles)
    h1_ref[...] = silu_rows(sum1_ref[...], places_of.start, whole, tiles)


def from_near(acc_ref, start, rows):
    return lambda: acc_ref[pl.ds(start, rows)]


def middle_body(tiles, m_ref, w_ref, _, acc0_ref, acc1_ref, h0_ref, h1_ref, sum0_ref, sum1_ref):
    rows = m_ref.shape[1]
    start = 2 * parity()
    bases = [from_near(acc_ref, start, rows - 2) for acc_ref in (acc0_ref, acc1_ref)]
    place = places(rows)[0]
    hidden(lambda f: m_ref[f], bases, place, w_ref, tiles, rows, h0_ref, h1_ref, sum0_ref, sum1_ref)


def partial_rows(times, h0, h1, v_ref, rows, cols, send_ref):
    has_next = lax.axis_index("tm") < times - 1

    @pl.when(has_next)
    def _():
        both = (h0.astype(jnp.float32) + h1.astype(jnp.float32)).astype(jnp.bfloat16)
        taps = row_taps(both, rows) + row_taps(h1, rows)
        part = convolved(taps, weight_rows(v_ref, 0) + weight_rows(v_ref, 1), rows, cols)
        send_ref[...] = part.astype(jnp.bfloat16)

    @pl.when(jnp.logical_not(has_next))
    def _():
        send_ref[...] = jnp.zeros_like(send_ref)


def near_body(
    tiles, times, m_ref, inner_ref, w_ref, v_ref, acc0_ref, acc1_ref, mid0_ref, mid1_ref,
    send_ref, h0_ref, h1_ref, sum0_ref, sum1_ref,
):
    rows, cols = m_ref.shape[1:3]
    odd = parity()
    start = (1 - odd) * (rows - 2)
    bases = [from_near(acc_ref, start, 2) for acc_ref in (acc0_ref, acc1_ref)]
    place = places(rows)[1]

    def slab(f):
        return inner_slab(inner_ref[f], m_ref.at[f])

    middle, near = pl.ds(2 * odd, rows - 2), pl.ds(start, 2)
    h0_ref[middle], h1_ref[middle] = mid0_ref[...], mid1_ref[...]
    hidden(
        slab, bases, place, w_ref, tiles, rows, h0_ref.at[near], h1_ref.at[near], sum0_ref,
        sum1_ref,
    )
    partial_rows(times, h0_ref[...], h1_ref[...], v_ref, rows - 2, cols, send_ref)


def far_body(
    tiles, times, m_ref, outer_ref, w_ref, v_ref, acc0_ref, acc1_ref, near0_ref, near1_ref,
    send_ref, h0_ref, h1_ref, sum0_ref, sum1_ref,
):
    rows, cols = m_ref.shape[1:3]
    odd = parity()
    far = places(rows)[2]
    near = pl.ds(2 * (1 - odd), rows)

    def slab(f):
        return outer_slab(outer_ref[f], m_ref.at[f], tiles)

    bases = [lambda: acc0_ref[...], lambda: acc1_ref[...]]
    h0_ref[near], h1_ref[near] = near0_ref[...], near1_ref[...]
    hidden(
        slab, bases, far, w_ref, tiles, rows, h0_ref.at[far], h1_ref.at[far], sum0_ref, sum1_ref
    )
    side = pl.ds(odd * (rows - 2), 4)
    partial_rows(times, h0_ref[side], h1_ref[side], v_ref, 2, cols, send_ref)


def rest_body(x_ref, h0_ref, h1_ref, v_ref, b_ref, out_ref):
    rows, cols = x_ref.shape[1:3]
    h0, h1 = h0_ref[...], h1_ref[...]
    both = (h0.astype(jnp.float32) + h1.astype(jnp.float32)).astype(jnp.bfloat16)
    taps = row_taps(h0, rows) + row_taps(both, rows)
    part = convolved(taps, weight_rows(v_ref, 1) + weight_rows(v_ref, 2), rows, cols)
    total = x_ref[0].astype(jnp.float32) + x_ref[1].astype(jnp.float32) + part
    out_ref[0] = total * 0.5 + b_ref[...]


def join_body(rest_ref, near_ref, far_ref, out_ref):
    rows = rest_ref.shape[1]
    odd = parity()
    first = lax.axis_index("tm") == 0
    for part_ref, start in ((near_ref, 2 * (1 - odd)), (far_ref, odd * (rows - 2))):
        part = part_ref[...].astype(jnp.float32)
        part = jnp.where(first, jnp.zeros_like(part), part)
        place = pl.ds(start, part.shape[0])
        out_ref[0, place] = (rest_ref[0, place] + 0.5 * part).astype(jnp.bfloat16)


def block(x, weight_first, bias_first, weight_second, bias_second):
    _, rows, cols, channels = x.shape
    clips, tiles, times = (lax.axis_size(axis) for axis in ("clips", "tile", "tm"))
    forward = [(i, i + 1) for i in range(times - 1)]
    ring = forward + [(times - 1, 0)]
    inner_pairs = [(i, i + 1) for i in range(0, tiles - 1, 2)]
    outer_pairs = [(i, i + 1) for i in range(1, tiles - 1, 2)]
    inner_pairs += [(j, i) for i, j in inner_pairs]
    outer_pairs += [(j, i) for i, j in outer_pairs]
    paired = {i for i, _ in outer_pairs}
    unpaired = [i for i in range(tiles) if i not in paired]
    outer_full = [(c * tiles + i, c * tiles + j) for c in range(clips) for i, j in outer_pairs]
    outer_full += [(c * tiles + i, (c + 1) % clips * tiles + i) for c in range(clips) for i in unpaired]
    outer_tiles = [(c * tiles + i, c * tiles + j) for c in range(clips) for i, j in outer_pairs]
    diagonal = [(i * times + s, j * times + t) for i, j in outer_tiles for s, t in ring]
    diagonal += [
        (i * times + t, j * times + t)
        for i, j in outer_full
        if i % tiles in unpaired
        for t in range(times)
    ]

    def frames(*lead, dtype=jnp.bfloat16):
        return jax.ShapeDtypeStruct((*lead, cols, channels), dtype)

    f32 = jnp.float32
    earlier = lax.ppermute(x, "tm", ring)
    x, outer_edge, inner_edge = call(
        edges_body,
        [frames(2, rows), frames(2, 2), frames(2, 2)],
        (pltpu.with_memory_space_constraint(x, pltpu.HBM),),
        10**10,
        in_specs=[HBM],
        scratch=[pltpu.SemaphoreType.DMA(())],
    )
    inner = lax.ppermute(inner_edge, "tile", inner_pairs)
    outer = lax.ppermute(outer_edge, ("clips", "tile"), outer_full)
    corner = lax.ppermute(outer_edge, ("clips", "tile", "tm"), diagonal)

    bias_first = bias_first.reshape(1, 1, -1)
    bias_second = bias_second.reshape(1, 1, -1)
    unit = 2 * 9 * channels * channels * cols
    wide = rows + 2
    sums0, sums1 = call(
        own_near_body,
        [frames(rows, dtype=f32), frames(rows, dtype=f32)],
        (x, inner, weight_first, bias_first),
        3 * unit * rows,
    )
    far0, far1 = call(
        functools.partial(own_far_body, tiles),
        [frames(2, dtype=f32), frames(2, dtype=f32)],
        (x, outer, weight_first, bias_first),
        0,
    )
    (inner_edge,) = call(turn_body, [frames(2, 2)], (earlier,), 0)
    inner_corner = lax.ppermute(inner_edge, "tile", inner_pairs)

    def sums(count):
        return [pltpu.VMEM((count, cols, channels), f32)] * 2

    mid0, mid1 = call(
        functools.partial(middle_body, tiles),
        [frames(rows - 2), frames(rows - 2)],
        (earlier, weight_first, weight_second, sums0, sums1),
        0,
        scratch=sums(rows - 2),
    )
    near_send, near0, near1 = call(
        functools.partial(near_body, tiles, times),
        [frames(rows - 2), frames(rows), frames(rows)],
        (earlier, inner_corner, weight_first, weight_second, sums0, sums1, mid0, mid1),
        0,
        scratch=sums(2),
    )
    near_part = lax.ppermute(near_send, "tm", ring)
    far_send, h0, h1 = call(
        functools.partial(far_body, tiles, times),
        [frames(2), frames(wide), frames(wide)],
        (earlier, corner, weight_first, weight_second, far0, far1, near0, near1),
        0,
        scratch=sums(2),
    )
    far_part = lax.ppermute(far_send, "tm", forward)
    (rest,) = call(
        rest_body,
        [frames(1, rows, dtype=f32)],
        (x, h0, h1, weight_second, bias_second),
        2 * unit * rows,
    )
    (pooled,) = call(join_body, [frames(1, rows)], (rest, near_part, far_part), 0)
    return pooled


def solution(mesh):
    in_specs = (P(("clips", "tm"), "tile", None, None), P(), P(), P(), P())
    out_specs = P(("clips", "tm"), "tile", None, None)
    return jax.shard_map(block, mesh=mesh, in_specs=in_specs, out_specs=out_specs, check_vma=False)
```

```python
import functools

import jax
import jax.numpy as jnp
from jax import lax
from jax.experimental import pallas as pl
from jax.experimental.pallas import tpu as pltpu
from jax.sharding import PartitionSpec as P


VMEM = pl.BlockSpec(memory_space=pltpu.VMEM)
HBM = pl.BlockSpec(memory_space=pltpu.HBM)


def call(body, outs, args, flops, in_specs=None, scratch=()):
    return pl.pallas_call(
        body,
        out_shape=outs,
        in_specs=in_specs or [VMEM] * len(args),
        out_specs=[VMEM] * len(outs),
        scratch_shapes=scratch,
        compiler_params=pltpu.CompilerParams(vmem_limit_bytes=16 << 20),
        cost_estimate=pl.CostEstimate(flops=flops, bytes_accessed=0, transcendentals=0),
    )(*args)


def flat(value):
    return value.reshape(-1, value.shape[-1])


def row_taps(slab, rows):
    return [flat(slab[p : p + rows]) for p in range(3)]


def shifted_columns(part, q):
    if q == 1:
        return part
    cols = part.shape[1]
    col = lax.broadcasted_iota(jnp.int32, part.shape, 1)
    edge, steps = (0, 1) if q == 0 else (cols - 1, cols - 1)
    return jnp.where(col == edge, 0.0, pltpu.roll(part, steps, 1))


def convolved(lhs, weights, rows, cols):
    stacked = jnp.concatenate(lhs, axis=1)
    total = None
    for q in range(3):
        taps = jnp.concatenate([w[q] for w in weights], axis=0)
        part = jnp.dot(stacked, taps, preferred_element_type=jnp.float32)
        part = shifted_columns(part.reshape(rows, cols, part.shape[-1]), q)
        total = part if total is None else total + part
    return total


def convolved_pair(first, second, shared, extra, rows, cols):
    lhs = jnp.concatenate([jnp.concatenate(taps, axis=1) for taps in (first, second)], axis=0)
    count = rows * cols
    total = None
    for q in range(3):
        taps = [jnp.concatenate([w[q] for w in weights], axis=0) for weights in (shared, extra)]
        part = jnp.dot(lhs, taps[0], preferred_element_type=jnp.float32)
        more = jnp.dot(lhs[count:], taps[1], preferred_element_type=jnp.float32)
        part = jnp.concatenate([part[:count] + more, part[count:]], axis=0)
        part = shifted_columns(part.reshape(2 * rows, cols, part.shape[-1]), q)
        total = part if total is None else total + part
    return total[:rows], total[rows:]


def parity():
    return lax.rem(lax.axis_index("tile"), 2)


def either(first, second):
    even = parity() == 0
    return jnp.concatenate([jnp.where(even, a, b) for a, b in zip(first, second)], axis=0)


def own_edge(own, side):
    odd = parity()
    last = own.shape[0] - 2
    return own[pl.ds((odd if side == 0 else 1 - odd) * last, 2)]


def outer_slab(outer, own, tiles):
    tile = lax.axis_index("tile")
    beyond = (tile == 0) | ((tile == tiles - 1) & (parity() == 1))
    outer = jnp.where(beyond, jnp.zeros_like(outer), outer)
    edge = own_edge(own, 0)
    return either([outer, edge], [edge, outer])


def inner_slab(inner, own):
    edge = own_edge(own, 1)
    return either([edge, inner], [inner, edge])


def places(rows):
    odd = parity()
    return pl.ds(2, rows - 2), pl.ds((1 - odd) * rows, 2), pl.ds(odd * rows, 2)


def weight_rows(w_ref, a):
    return [[w_ref[a, p, q] for q in range(3)] for p in range(3)]


def silu_rows(value, start, rows, tiles):
    hidden = (0.5 * value * (1.0 + jnp.tanh(0.5 * value))).astype(jnp.bfloat16)
    row = lax.broadcasted_iota(jnp.int32, hidden.shape, 0) + start
    row = row + lax.axis_index("tile") * rows - 1
    inside = (row >= 0) & (row < tiles * rows)
    return jnp.where(inside, hidden, jnp.zeros_like(hidden))


def edges_body(x_ref, own_ref, outer_ref, inner_ref, sem):
    copy = pltpu.make_async_copy(x_ref, own_ref, sem)
    copy.start()
    copy.wait()
    for f in range(2):
        outer_ref[f] = own_edge(own_ref.at[f], 0)
        inner_ref[f] = own_edge(own_ref.at[f], 1)


def turn_body(m_ref, inner_ref):
    for f in range(2):
        inner_ref[f] = own_edge(m_ref.at[f], 1)


def own_sums(slabs, w_ref, b_ref, acc0_ref, acc1_ref):
    rows, cols = acc0_ref.shape[:2]
    taps = [row_taps(slab, rows) for slab in slabs]
    shared, extra = weight_rows(w_ref, 2), weight_rows(w_ref, 1)
    late, early = convolved_pair(taps[1], taps[0], shared, extra, rows, cols)
    acc0_ref[...] = b_ref[...] + early
    acc1_ref[...] = b_ref[...] + late


def own_near_body(x_ref, inner_ref, w_ref, b_ref, acc0_ref, acc1_ref):
    even = parity() == 0
    slabs = []
    for f in range(2):
        below = jnp.concatenate([x_ref[f], inner_ref[f]], axis=0)
        above = jnp.concatenate([inner_ref[f], x_ref[f]], axis=0)
        slabs.append(jnp.where(even, below, above))
    own_sums(slabs, w_ref, b_ref, acc0_ref, acc1_ref)


def own_far_body(tiles, x_ref, outer_ref, w_ref, b_ref, acc0_ref, acc1_ref):
    slabs = [outer_slab(outer_ref[f], x_ref.at[f], tiles) for f in range(2)]
    own_sums(slabs, w_ref, b_ref, acc0_ref, acc1_ref)


def hidden(slab, bases, places_of, w_ref, tiles, whole, h0_ref, h1_ref, sum0_ref, sum1_ref):
    rows, cols = sum0_ref.shape[:2]
    started = lax.axis_index("tm") > 0

    @pl.when(started)
    def _():
        taps = [row_taps(slab(f), rows) for f in range(2)]
        shared, extra = weight_rows(w_ref, 0), weight_rows(w_ref, 1)
        early, late = convolved_pair(taps[0], taps[1], shared, extra, rows, cols)
        sum0_ref[...] = bases[0]() + early
        sum1_ref[...] = bases[1]() + late

    @pl.when(jnp.logical_not(started))
    def _():
        sum0_ref[...] = bases[0]()
        sum1_ref[...] = bases[1]()

    h0_ref[...] = silu_rows(sum0_ref[...], places_of.start, whole, tiles)
    h1_ref[...] = silu_rows(sum1_ref[...], places_of.start, whole, tiles)


def from_near(acc_ref, start, rows):
    return lambda: acc_ref[pl.ds(start, rows)]


def middle_body(tiles, m_ref, w_ref, _, acc0_ref, acc1_ref, h0_ref, h1_ref, sum0_ref, sum1_ref):
    rows = m_ref.shape[1]
    start = 2 * parity()
    bases = [from_near(acc_ref, start, rows - 2) for acc_ref in (acc0_ref, acc1_ref)]
    place = places(rows)[0]
    hidden(lambda f: m_ref[f], bases, place, w_ref, tiles, rows, h0_ref, h1_ref, sum0_ref, sum1_ref)


def partial_rows(times, h0, h1, v_ref, rows, cols, send_ref):
    has_next = lax.axis_index("tm") < times - 1

    @pl.when(has_next)
    def _():
        both = (h0.astype(jnp.float32) + h1.astype(jnp.float32)).astype(jnp.bfloat16)
        taps = row_taps(both, rows) + row_taps(h1, rows)
        part = convolved(taps, weight_rows(v_ref, 0) + weight_rows(v_ref, 1), rows, cols)
        send_ref[...] = part.astype(jnp.bfloat16)

    @pl.when(jnp.logical_not(has_next))
    def _():
        send_ref[...] = jnp.zeros_like(send_ref)


def near_body(
    tiles, times, m_ref, inner_ref, w_ref, v_ref, acc0_ref, acc1_ref, mid0_ref, mid1_ref,
    send_ref, h0_ref, h1_ref, sum0_ref, sum1_ref,
):
    rows, cols = m_ref.shape[1:3]
    odd = parity()
    start = (1 - odd) * (rows - 2)
    bases = [from_near(acc_ref, start, 2) for acc_ref in (acc0_ref, acc1_ref)]
    place = places(rows)[1]

    def slab(f):
        return inner_slab(inner_ref[f], m_ref.at[f])

    middle, near = pl.ds(2 * odd, rows - 2), pl.ds(start, 2)
    h0_ref[middle], h1_ref[middle] = mid0_ref[...], mid1_ref[...]
    hidden(
        slab, bases, place, w_ref, tiles, rows, h0_ref.at[near], h1_ref.at[near], sum0_ref,
        sum1_ref,
    )
    partial_rows(times, h0_ref[...], h1_ref[...], v_ref, rows - 2, cols, send_ref)


def far_body(
    tiles, times, m_ref, outer_ref, w_ref, v_ref, acc0_ref, acc1_ref, near0_ref, near1_ref,
    send_ref, h0_ref, h1_ref, sum0_ref, sum1_ref,
):
    rows, cols = m_ref.shape[1:3]
    odd = parity()
    far = places(rows)[2]
    near = pl.ds(2 * (1 - odd), rows)

    def slab(f):
        return outer_slab(outer_ref[f], m_ref.at[f], tiles)

    bases = [lambda: acc0_ref[...], lambda: acc1_ref[...]]
    h0_ref[near], h1_ref[near] = near0_ref[...], near1_ref[...]
    hidden(
        slab, bases, far, w_ref, tiles, rows, h0_ref.at[far], h1_ref.at[far], sum0_ref, sum1_ref
    )
    side = pl.ds(odd * (rows - 2), 4)
    partial_rows(times, h0_ref[side], h1_ref[side], v_ref, 2, cols, send_ref)


def rest_body(x_ref, h0_ref, h1_ref, v_ref, b_ref, out_ref):
    rows, cols = x_ref.shape[1:3]
    h0, h1 = h0_ref[...], h1_ref[...]
    both = (h0.astype(jnp.float32) + h1.astype(jnp.float32)).astype(jnp.bfloat16)
    taps = row_taps(h0, rows) + row_taps(both, rows)
    part = convolved(taps, weight_rows(v_ref, 1) + weight_rows(v_ref, 2), rows, cols)
    total = x_ref[0].astype(jnp.float32) + x_ref[1].astype(jnp.float32) + part
    out_ref[0] = total * 0.5 + b_ref[...]


def join_body(rest_ref, near_ref, far_ref, out_ref):
    rows = rest_ref.shape[1]
    odd = parity()
    first = lax.axis_index("tm") == 0
    for part_ref, start in ((near_ref, 2 * (1 - odd)), (far_ref, odd * (rows - 2))):
        part = part_ref[...].astype(jnp.float32)
        part = jnp.where(first, jnp.zeros_like(part), part)
        place = pl.ds(start, part.shape[0])
        out_ref[0, place] = (rest_ref[0, place] + 0.5 * part).astype(jnp.bfloat16)


def block(x, weight_first, bias_first, weight_second, bias_second):
    _, rows, cols, channels = x.shape
    clips, tiles, times = (lax.axis_size(axis) for axis in ("clips", "tile", "tm"))
    forward = [(i, i + 1) for i in range(times - 1)]
    ring = forward + [(times - 1, 0)]
    inner_pairs = [(i, i + 1) for i in range(0, tiles - 1, 2)]
    outer_pairs = [(i, i + 1) for i in range(1, tiles - 1, 2)]
    inner_pairs += [(j, i) for i, j in inner_pairs]
    outer_pairs += [(j, i) for i, j in outer_pairs]
    paired = {i for i, _ in outer_pairs}
    unpaired = [i for i in range(tiles) if i not in paired]
    outer_full = [(c * tiles + i, c * tiles + j) for c in range(clips) for i, j in outer_pairs]
    outer_full += [(c * tiles + i, (c + 1) % clips * tiles + i) for c in range(clips) for i in unpaired]
    diagonal = [(i * times + s, j * times + t) for i, j in outer_pairs for s, t in forward]

    def frames(*lead, dtype=jnp.bfloat16):
        return jax.ShapeDtypeStruct((*lead, cols, channels), dtype)

    f32 = jnp.float32
    earlier = lax.ppermute(x, "tm", ring)
    x, outer_edge, inner_edge = call(
        edges_body,
        [frames(2, rows), frames(2, 2), frames(2, 2)],
        (pltpu.with_memory_space_constraint(x, pltpu.HBM),),
        10**10,
        in_specs=[HBM],
        scratch=[pltpu.SemaphoreType.DMA(())],
    )
    inner = lax.ppermute(inner_edge, "tile", inner_pairs)
    outer = lax.ppermute(outer_edge, ("clips", "tile"), outer_full)
    corner = lax.ppermute(outer_edge, ("tile", "tm"), diagonal)

    bias_first = bias_first.reshape(1, 1, -1)
    bias_second = bias_second.reshape(1, 1, -1)
    unit = 2 * 9 * channels * channels * cols
    wide = rows + 2
    sums0, sums1 = call(
        own_near_body,
        [frames(rows, dtype=f32), frames(rows, dtype=f32)],
        (x, inner, weight_first, bias_first),
        3 * unit * rows,
    )
    far0, far1 = call(
        functools.partial(own_far_body, tiles),
        [frames(2, dtype=f32), frames(2, dtype=f32)],
        (x, outer, weight_first, bias_first),
        0,
    )
    (inner_edge,) = call(turn_body, [frames(2, 2)], (earlier,), 0)
    inner_corner = lax.ppermute(inner_edge, "tile", inner_pairs)

    def sums(count):
        return [pltpu.VMEM((count, cols, channels), f32)] * 2

    mid0, mid1 = call(
        functools.partial(middle_body, tiles),
        [frames(rows - 2), frames(rows - 2)],
        (earlier, weight_first, weight_second, sums0, sums1),
        0,
        scratch=sums(rows - 2),
    )
    near_send, near0, near1 = call(
        functools.partial(near_body, tiles, times),
        [frames(rows - 2), frames(rows), frames(rows)],
        (earlier, inner_corner, weight_first, weight_second, sums0, sums1, mid0, mid1),
        0,
        scratch=sums(2),
    )
    near_part = lax.ppermute(near_send, "tm", ring)
    far_send, h0, h1 = call(
        functools.partial(far_body, tiles, times),
        [frames(2), frames(wide), frames(wide)],
        (earlier, corner, weight_first, weight_second, far0, far1, near0, near1),
        0,
        scratch=sums(2),
    )
    far_part = lax.ppermute(far_send, "tm", forward)
    (rest,) = call(
        rest_body,
        [frames(1, rows, dtype=f32)],
        (x, h0, h1, weight_second, bias_second),
        2 * unit * rows,
    )
    (pooled,) = call(join_body, [frames(1, rows)], (rest, near_part, far_part), 0)
    return pooled


def solution(mesh):
    in_specs = (P(("clips", "tm"), "tile", None, None), P(), P(), P(), P())
    out_specs = P(("clips", "tm"), "tile", None, None)
    return jax.shard_map(block, mesh=mesh, in_specs=in_specs, out_specs=out_specs, check_vma=False)
```

```python
import functools

import jax
import jax.numpy as jnp
from jax import lax
from jax.experimental import pallas as pl
from jax.experimental.pallas import tpu as pltpu
from jax.sharding import PartitionSpec as P


VMEM = pl.BlockSpec(memory_space=pltpu.VMEM)
HBM = pl.BlockSpec(memory_space=pltpu.HBM)


def call(body, outs, args, flops, in_specs=None, scratch=()):
    return pl.pallas_call(
        body,
        out_shape=outs,
        in_specs=in_specs or [VMEM] * len(args),
        out_specs=[VMEM] * len(outs),
        scratch_shapes=scratch,
        compiler_params=pltpu.CompilerParams(vmem_limit_bytes=16 << 20),
        cost_estimate=pl.CostEstimate(flops=flops, bytes_accessed=0, transcendentals=0),
    )(*args)


def flat(value):
    return value.reshape(-1, value.shape[-1])


def row_taps(slab, rows):
    return [flat(slab[p : p + rows]) for p in range(3)]


def shifted_columns(part, q):
    if q == 1:
        return part
    cols = part.shape[1]
    col = lax.broadcasted_iota(jnp.int32, part.shape, 1)
    edge, steps = (0, 1) if q == 0 else (cols - 1, cols - 1)
    return jnp.where(col == edge, 0.0, pltpu.roll(part, steps, 1))


def convolved(lhs, weights, rows, cols):
    stacked = jnp.concatenate(lhs, axis=1)
    total = None
    for q in range(3):
        taps = jnp.concatenate([w[q] for w in weights], axis=0)
        part = jnp.dot(stacked, taps, preferred_element_type=jnp.float32)
        part = shifted_columns(part.reshape(rows, cols, part.shape[-1]), q)
        total = part if total is None else total + part
    return total


def convolved_pair(first, second, shared, extra, rows, cols):
    lhs = jnp.concatenate([jnp.concatenate(taps, axis=1) for taps in (first, second)], axis=0)
    count = rows * cols
    total = None
    for q in range(3):
        taps = [jnp.concatenate([w[q] for w in weights], axis=0) for weights in (shared, extra)]
        part = jnp.dot(lhs, taps[0], preferred_element_type=jnp.float32)
        more = jnp.dot(lhs[count:], taps[1], preferred_element_type=jnp.float32)
        part = jnp.concatenate([part[:count] + more, part[count:]], axis=0)
        part = shifted_columns(part.reshape(2 * rows, cols, part.shape[-1]), q)
        total = part if total is None else total + part
    return total[:rows], total[rows:]


def parity():
    return lax.rem(lax.axis_index("tile"), 2)


def either(first, second):
    even = parity() == 0
    return jnp.concatenate([jnp.where(even, a, b) for a, b in zip(first, second)], axis=0)


def own_edge(own, side):
    odd = parity()
    last = own.shape[0] - 2
    return own[pl.ds((odd if side == 0 else 1 - odd) * last, 2)]


def outer_slab(outer, own, tiles):
    tile = lax.axis_index("tile")
    beyond = (tile == 0) | ((tile == tiles - 1) & (parity() == 1))
    outer = jnp.where(beyond, jnp.zeros_like(outer), outer)
    edge = own_edge(own, 0)
    return either([outer, edge], [edge, outer])


def inner_slab(inner, own):
    edge = own_edge(own, 1)
    return either([edge, inner], [inner, edge])


def places(rows):
    odd = parity()
    return pl.ds(2, rows - 2), pl.ds((1 - odd) * rows, 2), pl.ds(odd * rows, 2)


def weight_rows(w_ref, a):
    return [[w_ref[a, p, q] for q in range(3)] for p in range(3)]


def silu_rows(value, start, rows, tiles):
    hidden = (0.5 * value * (1.0 + jnp.tanh(0.5 * value))).astype(jnp.bfloat16)
    row = lax.broadcasted_iota(jnp.int32, hidden.shape, 0) + start
    row = row + lax.axis_index("tile") * rows - 1
    inside = (row >= 0) & (row < tiles * rows)
    return jnp.where(inside, hidden, jnp.zeros_like(hidden))


def edges_body(x_ref, own_ref, outer_ref, inner_ref, sem):
    copy = pltpu.make_async_copy(x_ref, own_ref, sem)
    copy.start()
    copy.wait()
    for f in range(2):
        outer_ref[f] = own_edge(own_ref.at[f], 0)
        inner_ref[f] = own_edge(own_ref.at[f], 1)


def turn_body(m_ref, inner_ref):
    for f in range(2):
        inner_ref[f] = own_edge(m_ref.at[f], 1)


def own_sums(slabs, w_ref, b_ref, acc0_ref, acc1_ref):
    rows, cols = acc0_ref.shape[:2]
    taps = [row_taps(slab, rows) for slab in slabs]
    shared, extra = weight_rows(w_ref, 2), weight_rows(w_ref, 1)
    late, early = convolved_pair(taps[1], taps[0], shared, extra, rows, cols)
    acc0_ref[...] = b_ref[...] + early
    acc1_ref[...] = b_ref[...] + late


def own_near_body(x_ref, inner_ref, w_ref, b_ref, acc0_ref, acc1_ref):
    even = parity() == 0
    slabs = []
    for f in range(2):
        below = jnp.concatenate([x_ref[f], inner_ref[f]], axis=0)
        above = jnp.concatenate([inner_ref[f], x_ref[f]], axis=0)
        slabs.append(jnp.where(even, below, above))
    own_sums(slabs, w_ref, b_ref, acc0_ref, acc1_ref)


def own_far_body(tiles, x_ref, outer_ref, w_ref, b_ref, acc0_ref, acc1_ref):
    slabs = [outer_slab(outer_ref[f], x_ref.at[f], tiles) for f in range(2)]
    own_sums(slabs, w_ref, b_ref, acc0_ref, acc1_ref)


def hidden(slab, bases, place, w_ref, tiles, whole, h0_ref, h1_ref):
    rows, cols = h0_ref.shape[:2]
    taps = [row_taps(slab(f), rows) for f in range(2)]
    shared, extra = weight_rows(w_ref, 0), weight_rows(w_ref, 1)
    early, late = convolved_pair(taps[0], taps[1], shared, extra, rows, cols)
    h0_ref[...] = silu_rows(bases[0]() + early, place.start, whole, tiles)
    h1_ref[...] = silu_rows(bases[1]() + late, place.start, whole, tiles)


def started():
    return lax.axis_index("tm") > 0


def from_near(acc_ref, start, rows):
    return lambda: acc_ref[pl.ds(start, rows)]


def partial_rows(times, h0, h1, v_ref, send_ref):
    rows, cols = send_ref.shape[:2]
    has_next = lax.axis_index("tm") < times - 1

    @pl.when(has_next)
    def _():
        both = (h0.astype(jnp.float32) + h1.astype(jnp.float32)).astype(jnp.bfloat16)
        taps = row_taps(both, rows) + row_taps(h1, rows)
        part = convolved(taps, weight_rows(v_ref, 0) + weight_rows(v_ref, 1), rows, cols)
        send_ref[...] = part.astype(jnp.bfloat16)

    @pl.when(jnp.logical_not(has_next))
    def _():
        send_ref[...] = jnp.zeros_like(send_ref)


def far_side(rows):
    return pl.ds(parity() * (rows - 2), 4)


def near_place(rows):
    return pl.ds(2 * (1 - parity()), rows)


def origin_body(
    tiles, times, v_ref, acc0_ref, acc1_ref, far0_ref, far1_ref, near_ref, far_ref, h0_ref, h1_ref
):
    rows = acc0_ref.shape[0]
    near, far = near_place(rows), places(rows)[2]

    @pl.when(jnp.logical_not(started()))
    def _():
        for h_ref, acc_ref, other_ref in ((h0_ref, acc0_ref, far0_ref), (h1_ref, acc1_ref, far1_ref)):
            h_ref[near] = silu_rows(acc_ref[...], near.start, rows, tiles)
            h_ref[far] = silu_rows(other_ref[...], far.start, rows, tiles)
        partial_rows(times, h0_ref[near], h1_ref[near], v_ref, near_ref)
        side = far_side(rows)
        partial_rows(times, h0_ref[side], h1_ref[side], v_ref, far_ref)


def middle_body(tiles, m_ref, w_ref, acc0_ref, acc1_ref, h0_ref, h1_ref):
    rows = m_ref.shape[1]

    @pl.when(started())
    def _():
        start = 2 * parity()
        bases = [from_near(acc_ref, start, rows - 2) for acc_ref in (acc0_ref, acc1_ref)]
        hidden(lambda f: m_ref[f], bases, places(rows)[0], w_ref, tiles, rows, h0_ref, h1_ref)


def near_body(
    tiles, times, m_ref, inner_ref, w_ref, v_ref, acc0_ref, acc1_ref, mid0_ref, mid1_ref, first_ref,
    send_ref, h0_ref, h1_ref,
):
    rows = m_ref.shape[1]

    @pl.when(started())
    def _():
        odd = parity()
        start = (1 - odd) * (rows - 2)
        bases = [from_near(acc_ref, start, 2) for acc_ref in (acc0_ref, acc1_ref)]
        middle, near = pl.ds(2 * odd, rows - 2), pl.ds(start, 2)

        def slab(f):
            return inner_slab(inner_ref[f], m_ref.at[f])

        h0_ref[middle], h1_ref[middle] = mid0_ref[...], mid1_ref[...]
        place = places(rows)[1]
        hidden(slab, bases, place, w_ref, tiles, rows, h0_ref.at[near], h1_ref.at[near])
        partial_rows(times, h0_ref[...], h1_ref[...], v_ref, send_ref)

    @pl.when(jnp.logical_not(started()))
    def _():
        send_ref[...] = first_ref[...]


def far_body(
    tiles, times, m_ref, outer_ref, w_ref, v_ref, acc0_ref, acc1_ref, near0_ref, near1_ref,
    first_ref, first0_ref, first1_ref, send_ref, h0_ref, h1_ref,
):
    rows = m_ref.shape[1]

    @pl.when(started())
    def _():
        near, far, side = near_place(rows), places(rows)[2], far_side(rows)

        def slab(f):
            return outer_slab(outer_ref[f], m_ref.at[f], tiles)

        bases = [lambda: acc0_ref[...], lambda: acc1_ref[...]]
        h0_ref[near], h1_ref[near] = near0_ref[...], near1_ref[...]
        hidden(slab, bases, far, w_ref, tiles, rows, h0_ref.at[far], h1_ref.at[far])
        partial_rows(times, h0_ref[side], h1_ref[side], v_ref, send_ref)

    @pl.when(jnp.logical_not(started()))
    def _():
        send_ref[...] = first_ref[...]
        h0_ref[...], h1_ref[...] = first0_ref[...], first1_ref[...]


def rest_body(x_ref, h0_ref, h1_ref, v_ref, b_ref, out_ref):
    rows, cols = x_ref.shape[1:3]
    h0, h1 = h0_ref[...], h1_ref[...]
    taps = row_taps(h0, rows) + row_taps(h0, rows) + row_taps(h1, rows)
    weights = weight_rows(v_ref, 1) + 2 * weight_rows(v_ref, 2)
    part = convolved(taps, weights, rows, cols)
    total = x_ref[0].astype(jnp.float32) + x_ref[1].astype(jnp.float32) + part
    out_ref[0] = total * 0.5 + b_ref[...]


def join_body(rest_ref, near_ref, far_ref, out_ref):
    rows = rest_ref.shape[1]
    odd = parity()
    first = lax.axis_index("tm") == 0
    for part_ref, start in ((near_ref, 2 * (1 - odd)), (far_ref, odd * (rows - 2))):
        part = part_ref[...].astype(jnp.float32)
        part = jnp.where(first, jnp.zeros_like(part), part)
        place = pl.ds(start, part.shape[0])
        out_ref[0, place] = (rest_ref[0, place] + 0.5 * part).astype(jnp.bfloat16)


def block(x, weight_first, bias_first, weight_second, bias_second):
    _, rows, cols, channels = x.shape
    clips, tiles, times = (lax.axis_size(axis) for axis in ("clips", "tile", "tm"))
    forward = [(i, i + 1) for i in range(times - 1)]
    ring = forward + [(times - 1, 0)]
    inner_pairs = [(i, i + 1) for i in range(0, tiles - 1, 2)]
    outer_pairs = [(i, i + 1) for i in range(1, tiles - 1, 2)]
    inner_pairs += [(j, i) for i, j in inner_pairs]
    outer_pairs += [(j, i) for i, j in outer_pairs]
    paired = {i for i, _ in outer_pairs}
    unpaired = [i for i in range(tiles) if i not in paired]
    outer_full = [(c * tiles + i, c * tiles + j) for c in range(clips) for i, j in outer_pairs]
    outer_full += [(c * tiles + i, (c + 1) % clips * tiles + i) for c in range(clips) for i in unpaired]
    diagonal = [(i * times + s, j * times + t) for i, j in outer_pairs for s, t in forward]

    def frames(*lead, dtype=jnp.bfloat16):
        return jax.ShapeDtypeStruct((*lead, cols, channels), dtype)

    f32 = jnp.float32
    earlier = lax.ppermute(x, "tm", ring)
    x, outer_edge, inner_edge = call(
        edges_body,
        [frames(2, rows), frames(2, 2), frames(2, 2)],
        (pltpu.with_memory_space_constraint(x, pltpu.HBM),),
        10**10,
        in_specs=[HBM],
        scratch=[pltpu.SemaphoreType.DMA(())],
    )
    inner = lax.ppermute(inner_edge, "tile", inner_pairs)
    outer = lax.ppermute(outer_edge, ("clips", "tile"), outer_full)
    corner = lax.ppermute(outer_edge, ("tile", "tm"), diagonal)

    bias_first = bias_first.reshape(1, 1, -1)
    bias_second = bias_second.reshape(1, 1, -1)
    unit = 2 * 9 * channels * channels * cols
    wide = rows + 2
    sums0, sums1 = call(
        own_near_body,
        [frames(rows, dtype=f32), frames(rows, dtype=f32)],
        (x, inner, weight_first, bias_first),
        3 * unit * rows,
    )
    far0, far1 = call(
        functools.partial(own_far_body, tiles),
        [frames(2, dtype=f32), frames(2, dtype=f32)],
        (x, outer, weight_first, bias_first),
        0,
    )
    first_near, first_far, first0, first1 = call(
        functools.partial(origin_body, tiles, times),
        [frames(rows - 2), frames(2), frames(wide), frames(wide)],
        (weight_second, sums0, sums1, far0, far1),
        0,
    )
    (inner_edge,) = call(turn_body, [frames(2, 2)], (earlier,), 0)
    inner_corner = lax.ppermute(inner_edge, "tile", inner_pairs)
    mid0, mid1 = call(
        functools.partial(middle_body, tiles),
        [frames(rows - 2), frames(rows - 2)],
        (earlier, weight_first, sums0, sums1),
        0,
    )
    near_send, near0, near1 = call(
        functools.partial(near_body, tiles, times),
        [frames(rows - 2), frames(rows), frames(rows)],
        (
            earlier, inner_corner, weight_first, weight_second, sums0, sums1, mid0, mid1,
            first_near,
        ),
        0,
    )
    near_part = lax.ppermute(near_send, "tm", ring)
    far_send, h0, h1 = call(
        functools.partial(far_body, tiles, times),
        [frames(2), frames(wide), frames(wide)],
        (
            earlier, corner, weight_first, weight_second, far0, far1, near0, near1, first_far,
            first0, first1,
        ),
        0,
    )
    far_part = lax.ppermute(far_send, "tm", forward)
    (rest,) = call(
        rest_body,
        [frames(1, rows, dtype=f32)],
        (x, h0, h1, weight_second, bias_second),
        3 * unit * rows,
    )
    (pooled,) = call(join_body, [frames(1, rows)], (rest, near_part, far_part), 0)
    return pooled


def solution(mesh):
    in_specs = (P(("clips", "tm"), "tile", None, None), P(), P(), P(), P())
    out_specs = P(("clips", "tm"), "tile", None, None)
    return jax.shard_map(block, mesh=mesh, in_specs=in_specs, out_specs=out_specs, check_vma=False)
```

```python
import functools

import jax
import jax.numpy as jnp
from jax import lax
from jax.experimental import pallas as pl
from jax.experimental.pallas import tpu as pltpu
from jax.sharding import PartitionSpec as P


VMEM = pl.BlockSpec(memory_space=pltpu.VMEM)
HBM = pl.BlockSpec(memory_space=pltpu.HBM)


def call(body, outs, args, flops, in_specs=None, scratch=()):
    return pl.pallas_call(
        body,
        out_shape=outs,
        in_specs=in_specs or [VMEM] * len(args),
        out_specs=[VMEM] * len(outs),
        scratch_shapes=scratch,
        compiler_params=pltpu.CompilerParams(vmem_limit_bytes=16 << 20),
        cost_estimate=pl.CostEstimate(flops=flops, bytes_accessed=0, transcendentals=0),
    )(*args)


def flat(value):
    return value.reshape(-1, value.shape[-1])


def row_taps(slab, rows):
    return [flat(slab[p : p + rows]) for p in range(3)]


def shifted_columns(part, q):
    if q == 1:
        return part
    cols = part.shape[1]
    col = lax.broadcasted_iota(jnp.int32, part.shape, 1)
    edge, steps = (0, 1) if q == 0 else (cols - 1, cols - 1)
    return jnp.where(col == edge, 0.0, pltpu.roll(part, steps, 1))


def convolved(lhs, weights, rows, cols):
    stacked = jnp.concatenate(lhs, axis=1)
    total = None
    for q in range(3):
        taps = jnp.concatenate([w[q] for w in weights], axis=0)
        part = jnp.dot(stacked, taps, preferred_element_type=jnp.float32)
        part = shifted_columns(part.reshape(rows, cols, part.shape[-1]), q)
        total = part if total is None else total + part
    return total


def convolved_pair(first, second, shared, extra, rows, cols):
    lhs = jnp.concatenate([jnp.concatenate(taps, axis=1) for taps in (first, second)], axis=0)
    count = rows * cols
    total = None
    for q in range(3):
        taps = [jnp.concatenate([w[q] for w in weights], axis=0) for weights in (shared, extra)]
        part = jnp.dot(lhs, taps[0], preferred_element_type=jnp.float32)
        more = jnp.dot(lhs[count:], taps[1], preferred_element_type=jnp.float32)
        part = jnp.concatenate([part[:count] + more, part[count:]], axis=0)
        part = shifted_columns(part.reshape(2 * rows, cols, part.shape[-1]), q)
        total = part if total is None else total + part
    return total[:rows], total[rows:]


def parity():
    return lax.rem(lax.axis_index("tile"), 2)


def either(first, second):
    even = parity() == 0
    return jnp.concatenate([jnp.where(even, a, b) for a, b in zip(first, second)], axis=0)


def own_edge(own, side):
    odd = parity()
    last = own.shape[0] - 2
    return own[pl.ds((odd if side == 0 else 1 - odd) * last, 2)]


def outer_slab(outer, own, tiles):
    tile = lax.axis_index("tile")
    beyond = (tile == 0) | ((tile == tiles - 1) & (parity() == 1))
    outer = jnp.where(beyond, jnp.zeros_like(outer), outer)
    edge = own_edge(own, 0)
    return either([outer, edge], [edge, outer])


def inner_slab(inner, own):
    edge = own_edge(own, 1)
    return either([edge, inner], [inner, edge])


def places(rows):
    odd = parity()
    return pl.ds(2, rows - 2), pl.ds((1 - odd) * rows, 2), pl.ds(odd * rows, 2)


def weight_rows(w_ref, a):
    return [[w_ref[a, p, q] for q in range(3)] for p in range(3)]


def silu_rows(value, start, rows, tiles):
    hidden = (0.5 * value * (1.0 + jnp.tanh(0.5 * value))).astype(jnp.bfloat16)
    row = lax.broadcasted_iota(jnp.int32, hidden.shape, 0) + start
    row = row + lax.axis_index("tile") * rows - 1
    inside = (row >= 0) & (row < tiles * rows)
    return jnp.where(inside, hidden, jnp.zeros_like(hidden))


def edges_body(x_ref, own_ref, outer_ref, inner_ref, sem):
    copy = pltpu.make_async_copy(x_ref, own_ref, sem)
    copy.start()
    copy.wait()
    for f in range(2):
        outer_ref[f] = own_edge(own_ref.at[f], 0)
        inner_ref[f] = own_edge(own_ref.at[f], 1)


def turn_body(m_ref, inner_ref):
    for f in range(2):
        inner_ref[f] = own_edge(m_ref.at[f], 1)


def own_sums(slabs, w_ref, b_ref, acc0_ref, acc1_ref):
    rows, cols = acc0_ref.shape[:2]
    taps = [row_taps(slab, rows) for slab in slabs]
    shared, extra = weight_rows(w_ref, 2), weight_rows(w_ref, 1)
    late, early = convolved_pair(taps[1], taps[0], shared, extra, rows, cols)
    acc0_ref[...] = b_ref[...] + early
    acc1_ref[...] = b_ref[...] + late


def own_near_body(x_ref, inner_ref, w_ref, b_ref, acc0_ref, acc1_ref):
    even = parity() == 0
    slabs = []
    for f in range(2):
        below = jnp.concatenate([x_ref[f], inner_ref[f]], axis=0)
        above = jnp.concatenate([inner_ref[f], x_ref[f]], axis=0)
        slabs.append(jnp.where(even, below, above))
    own_sums(slabs, w_ref, b_ref, acc0_ref, acc1_ref)


def own_far_body(tiles, x_ref, outer_ref, w_ref, b_ref, acc0_ref, acc1_ref):
    slabs = [outer_slab(outer_ref[f], x_ref.at[f], tiles) for f in range(2)]
    own_sums(slabs, w_ref, b_ref, acc0_ref, acc1_ref)


def hidden(slab, bases, place, w_ref, tiles, whole, h0_ref, h1_ref):
    rows, cols = h0_ref.shape[:2]
    taps = [row_taps(slab(f), rows) for f in range(2)]
    shared, extra = weight_rows(w_ref, 0), weight_rows(w_ref, 1)
    early, late = convolved_pair(taps[0], taps[1], shared, extra, rows, cols)
    h0_ref[...] = silu_rows(bases[0]() + early, place.start, whole, tiles)
    h1_ref[...] = silu_rows(bases[1]() + late, place.start, whole, tiles)


def started():
    return lax.axis_index("tm") > 0


def from_near(acc_ref, start, rows):
    return lambda: acc_ref[pl.ds(start, rows)]


def partial_rows(times, h0, h1, v_ref, send_ref):
    rows, cols = send_ref.shape[:2]
    has_next = lax.axis_index("tm") < times - 1

    @pl.when(has_next)
    def _():
        both = (h0.astype(jnp.float32) + h1.astype(jnp.float32)).astype(jnp.bfloat16)
        taps = row_taps(both, rows) + row_taps(h1, rows)
        part = convolved(taps, weight_rows(v_ref, 0) + weight_rows(v_ref, 1), rows, cols)
        send_ref[...] = part.astype(jnp.bfloat16)

    @pl.when(jnp.logical_not(has_next))
    def _():
        send_ref[...] = jnp.zeros_like(send_ref)


def far_side(rows):
    return pl.ds(parity() * (rows - 2), 4)


def near_place(rows):
    return pl.ds(2 * (1 - parity()), rows)


def origin_body(
    tiles, times, v_ref, acc0_ref, acc1_ref, far0_ref, far1_ref, near_ref, far_ref, h0_ref, h1_ref
):
    rows = acc0_ref.shape[0]
    near, far = near_place(rows), places(rows)[2]

    @pl.when(jnp.logical_not(started()))
    def _():
        for h_ref, acc_ref, other_ref in ((h0_ref, acc0_ref, far0_ref), (h1_ref, acc1_ref, far1_ref)):
            h_ref[near] = silu_rows(acc_ref[...], near.start, rows, tiles)
            h_ref[far] = silu_rows(other_ref[...], far.start, rows, tiles)
        partial_rows(times, h0_ref[near], h1_ref[near], v_ref, near_ref)
        side = far_side(rows)
        partial_rows(times, h0_ref[side], h1_ref[side], v_ref, far_ref)


def middle_body(tiles, m_ref, w_ref, acc0_ref, acc1_ref, h0_ref, h1_ref):
    rows = m_ref.shape[1]

    @pl.when(started())
    def _():
        start = 2 * parity()
        bases = [from_near(acc_ref, start, rows - 2) for acc_ref in (acc0_ref, acc1_ref)]
        hidden(lambda f: m_ref[f], bases, places(rows)[0], w_ref, tiles, rows, h0_ref, h1_ref)


def near_body(
    tiles, times, m_ref, inner_ref, w_ref, v_ref, acc0_ref, acc1_ref, mid0_ref, mid1_ref, first_ref,
    send_ref, h0_ref, h1_ref,
):
    rows = m_ref.shape[1]

    @pl.when(started())
    def _():
        odd = parity()
        start = (1 - odd) * (rows - 2)
        bases = [from_near(acc_ref, start, 2) for acc_ref in (acc0_ref, acc1_ref)]
        middle, near = pl.ds(2 * odd, rows - 2), pl.ds(start, 2)

        def slab(f):
            return inner_slab(inner_ref[f], m_ref.at[f])

        h0_ref[middle], h1_ref[middle] = mid0_ref[...], mid1_ref[...]
        place = places(rows)[1]
        hidden(slab, bases, place, w_ref, tiles, rows, h0_ref.at[near], h1_ref.at[near])
        partial_rows(times, h0_ref[...], h1_ref[...], v_ref, send_ref)

    @pl.when(jnp.logical_not(started()))
    def _():
        send_ref[...] = first_ref[...]


def far_body(
    tiles, times, m_ref, outer_ref, w_ref, v_ref, acc0_ref, acc1_ref, near0_ref, near1_ref,
    first_ref, first0_ref, first1_ref, send_ref, h0_ref, h1_ref,
):
    rows = m_ref.shape[1]

    @pl.when(started())
    def _():
        near, far, side = near_place(rows), places(rows)[2], far_side(rows)

        def slab(f):
            return outer_slab(outer_ref[f], m_ref.at[f], tiles)

        bases = [lambda: acc0_ref[...], lambda: acc1_ref[...]]
        h0_ref[near], h1_ref[near] = near0_ref[...], near1_ref[...]
        hidden(slab, bases, far, w_ref, tiles, rows, h0_ref.at[far], h1_ref.at[far])
        partial_rows(times, h0_ref[side], h1_ref[side], v_ref, send_ref)

    @pl.when(jnp.logical_not(started()))
    def _():
        send_ref[...] = first_ref[...]
        h0_ref[...], h1_ref[...] = first0_ref[...], first1_ref[...]


def rest_body(x_ref, h0_ref, h1_ref, v_ref, b_ref, out_ref):
    rows, cols = x_ref.shape[1:3]
    h0, h1 = h0_ref[...], h1_ref[...]
    taps = row_taps(h0, rows) + row_taps(h0, rows) + row_taps(h1, rows)
    weights = weight_rows(v_ref, 1) + 2 * weight_rows(v_ref, 2)
    part = convolved(taps, weights, rows, cols)
    total = x_ref[0].astype(jnp.float32) + x_ref[1].astype(jnp.float32) + part
    out_ref[0] = total * 0.5 + b_ref[...]


def join_body(rest_ref, near_odd_ref, near_even_ref, far_odd_ref, far_even_ref, out_ref):
    rows = rest_ref.shape[1]
    odd = parity()
    time = lax.axis_index("tm")
    from_odd = lax.rem(time, 2) == 1
    near = jnp.where(from_odd, near_odd_ref[...], near_even_ref[...])
    far = jnp.where(from_odd, far_odd_ref[...], far_even_ref[...])
    for part, start in ((near, 2 * (1 - odd)), (far, odd * (rows - 2))):
        part = jnp.where(time == 0, jnp.zeros_like(part), part).astype(jnp.float32)
        place = pl.ds(start, part.shape[0])
        out_ref[0, place] = (rest_ref[0, place] + 0.5 * part).astype(jnp.bfloat16)


def block(x, weight_first, bias_first, weight_second, bias_second):
    _, rows, cols, channels = x.shape
    clips, tiles, times = (lax.axis_size(axis) for axis in ("clips", "tile", "tm"))
    forward = [(i, i + 1) for i in range(times - 1)]
    ring = forward + [(times - 1, 0)]
    inner_pairs = [(i, i + 1) for i in range(0, tiles - 1, 2)]
    outer_pairs = [(i, i + 1) for i in range(1, tiles - 1, 2)]
    inner_pairs += [(j, i) for i, j in inner_pairs]
    outer_pairs += [(j, i) for i, j in outer_pairs]
    paired = {i for i, _ in outer_pairs}
    unpaired = [i for i in range(tiles) if i not in paired]
    outer_full = [(c * tiles + i, c * tiles + j) for c in range(clips) for i, j in outer_pairs]
    outer_full += [(c * tiles + i, (c + 1) % clips * tiles + i) for c in range(clips) for i in unpaired]
    diagonal = [(i * times + s, j * times + t) for i, j in outer_pairs for s, t in forward]

    def swaps(first):
        turns = {}
        for t in range(first, times - 1, 2):
            turns[t], turns[t + 1] = t + 1, t
        return [
            (c * times + t, c * times + turns[t] if t in turns else (c + 1) % clips * times + t)
            for c in range(clips)
            for t in range(times)
        ]

    def frames(*lead, dtype=jnp.bfloat16):
        return jax.ShapeDtypeStruct((*lead, cols, channels), dtype)

    f32 = jnp.float32
    earlier = lax.ppermute(x, "tm", ring)
    x, outer_edge, inner_edge = call(
        edges_body,
        [frames(2, rows), frames(2, 2), frames(2, 2)],
        (pltpu.with_memory_space_constraint(x, pltpu.HBM),),
        10**10,
        in_specs=[HBM],
        scratch=[pltpu.SemaphoreType.DMA(())],
    )
    inner = lax.ppermute(inner_edge, "tile", inner_pairs)
    outer = lax.ppermute(outer_edge, ("clips", "tile"), outer_full)
    corner = lax.ppermute(outer_edge, ("tile", "tm"), diagonal)

    bias_first = bias_first.reshape(1, 1, -1)
    bias_second = bias_second.reshape(1, 1, -1)
    unit = 2 * 9 * channels * channels * cols
    wide = rows + 2
    sums0, sums1 = call(
        own_near_body,
        [frames(rows, dtype=f32), frames(rows, dtype=f32)],
        (x, inner, weight_first, bias_first),
        3 * unit * rows,
    )
    far0, far1 = call(
        functools.partial(own_far_body, tiles),
        [frames(2, dtype=f32), frames(2, dtype=f32)],
        (x, outer, weight_first, bias_first),
        0,
    )
    first_near, first_far, first0, first1 = call(
        functools.partial(origin_body, tiles, times),
        [frames(rows - 2), frames(2), frames(wide), frames(wide)],
        (weight_second, sums0, sums1, far0, far1),
        0,
    )
    (inner_edge,) = call(turn_body, [frames(2, 2)], (earlier,), 0)
    inner_corner = lax.ppermute(inner_edge, "tile", inner_pairs)
    mid0, mid1 = call(
        functools.partial(middle_body, tiles),
        [frames(rows - 2), frames(rows - 2)],
        (earlier, weight_first, sums0, sums1),
        0,
    )
    near_send, near0, near1 = call(
        functools.partial(near_body, tiles, times),
        [frames(rows - 2), frames(rows), frames(rows)],
        (
            earlier, inner_corner, weight_first, weight_second, sums0, sums1, mid0, mid1,
            first_near,
        ),
        0,
    )
    near_odd = lax.ppermute(near_send, ("clips", "tm"), swaps(0))
    near_even = lax.ppermute(near_send, ("clips", "tm"), swaps(1))
    far_send, h0, h1 = call(
        functools.partial(far_body, tiles, times),
        [frames(2), frames(wide), frames(wide)],
        (
            earlier, corner, weight_first, weight_second, far0, far1, near0, near1, first_far,
            first0, first1,
        ),
        0,
    )
    far_odd = lax.ppermute(far_send, ("clips", "tm"), swaps(0))
    far_even = lax.ppermute(far_send, ("clips", "tm"), swaps(1))
    (rest,) = call(
        rest_body,
        [frames(1, rows, dtype=f32)],
        (x, h0, h1, weight_second, bias_second),
        3 * unit * rows,
    )
    (pooled,) = call(join_body, [frames(1, rows)], (rest, near_odd, near_even, far_odd, far_even), 0)
    return pooled


def solution(mesh):
    in_specs = (P(("clips", "tm"), "tile", None, None), P(), P(), P(), P())
    out_specs = P(("clips", "tm"), "tile", None, None)
    return jax.shard_map(block, mesh=mesh, in_specs=in_specs, out_specs=out_specs, check_vma=False)
```

```python
import functools

import jax
import jax.numpy as jnp
from jax import lax
from jax.experimental import pallas as pl
from jax.experimental.pallas import tpu as pltpu
from jax.sharding import PartitionSpec as P


VMEM = pl.BlockSpec(memory_space=pltpu.VMEM)
HBM = pl.BlockSpec(memory_space=pltpu.HBM)


def call(body, outs, args, flops, in_specs=None, scratch=()):
    return pl.pallas_call(
        body,
        out_shape=outs,
        in_specs=in_specs or [VMEM] * len(args),
        out_specs=[VMEM] * len(outs),
        scratch_shapes=scratch,
        compiler_params=pltpu.CompilerParams(vmem_limit_bytes=16 << 20),
        cost_estimate=pl.CostEstimate(flops=flops, bytes_accessed=0, transcendentals=0),
    )(*args)


def flat(value):
    return value.reshape(-1, value.shape[-1])


def row_taps(slab, rows):
    return [flat(slab[p : p + rows]) for p in range(3)]


def shifted_columns(part, q):
    if q == 1:
        return part
    cols = part.shape[1]
    col = lax.broadcasted_iota(jnp.int32, part.shape, 1)
    edge, steps = (0, 1) if q == 0 else (cols - 1, cols - 1)
    return jnp.where(col == edge, 0.0, pltpu.roll(part, steps, 1))


def convolved(lhs, weights, rows, cols):
    stacked = jnp.concatenate(lhs, axis=1)
    total = None
    for q in range(3):
        taps = jnp.concatenate([w[q] for w in weights], axis=0)
        part = jnp.dot(stacked, taps, preferred_element_type=jnp.float32)
        part = shifted_columns(part.reshape(rows, cols, part.shape[-1]), q)
        total = part if total is None else total + part
    return total


def convolved_pair(first, second, shared, extra, rows, cols):
    lhs = jnp.concatenate([jnp.concatenate(taps, axis=1) for taps in (first, second)], axis=0)
    count = rows * cols
    total = None
    for q in range(3):
        taps = [jnp.concatenate([w[q] for w in weights], axis=0) for weights in (shared, extra)]
        part = jnp.dot(lhs, taps[0], preferred_element_type=jnp.float32)
        more = jnp.dot(lhs[count:], taps[1], preferred_element_type=jnp.float32)
        part = jnp.concatenate([part[:count] + more, part[count:]], axis=0)
        part = shifted_columns(part.reshape(2 * rows, cols, part.shape[-1]), q)
        total = part if total is None else total + part
    return total[:rows], total[rows:]


def parity():
    return lax.rem(lax.axis_index("tile"), 2)


def either(first, second):
    even = parity() == 0
    return jnp.concatenate([jnp.where(even, a, b) for a, b in zip(first, second)], axis=0)


def own_edge(own, side):
    odd = parity()
    last = own.shape[0] - 2
    return own[pl.ds((odd if side == 0 else 1 - odd) * last, 2)]


def outer_slab(outer, own, tiles):
    tile = lax.axis_index("tile")
    beyond = (tile == 0) | ((tile == tiles - 1) & (parity() == 1))
    outer = jnp.where(beyond, jnp.zeros_like(outer), outer)
    edge = own_edge(own, 0)
    return either([outer, edge], [edge, outer])


def inner_slab(inner, own):
    edge = own_edge(own, 1)
    return either([edge, inner], [inner, edge])


def places(rows):
    odd = parity()
    return pl.ds(2, rows - 2), pl.ds((1 - odd) * rows, 2), pl.ds(odd * rows, 2)


def weight_rows(w_ref, a):
    return [[w_ref[a, p, q] for q in range(3)] for p in range(3)]


def silu_rows(value, start, rows, tiles):
    hidden = (0.5 * value * (1.0 + jnp.tanh(0.5 * value))).astype(jnp.bfloat16)
    row = lax.broadcasted_iota(jnp.int32, hidden.shape, 0) + start
    row = row + lax.axis_index("tile") * rows - 1
    inside = (row >= 0) & (row < tiles * rows)
    return jnp.where(inside, hidden, jnp.zeros_like(hidden))


def edges_body(x_ref, own_ref, outer_ref, inner_ref, sem):
    copy = pltpu.make_async_copy(x_ref, own_ref, sem)
    copy.start()
    copy.wait()
    for f in range(2):
        outer_ref[f] = own_edge(own_ref.at[f], 0)
        inner_ref[f] = own_edge(own_ref.at[f], 1)


def turn_body(m_ref, inner_ref):
    for f in range(2):
        inner_ref[f] = own_edge(m_ref.at[f], 1)


def own_sums(slabs, w_ref, b_ref, acc0_ref, acc1_ref):
    rows, cols = acc0_ref.shape[:2]
    taps = [row_taps(slab, rows) for slab in slabs]
    shared, extra = weight_rows(w_ref, 2), weight_rows(w_ref, 1)
    late, early = convolved_pair(taps[1], taps[0], shared, extra, rows, cols)
    acc0_ref[...] = b_ref[...] + early
    acc1_ref[...] = b_ref[...] + late


def own_near_body(x_ref, inner_ref, w_ref, b_ref, acc0_ref, acc1_ref):
    even = parity() == 0
    slabs = []
    for f in range(2):
        below = jnp.concatenate([x_ref[f], inner_ref[f]], axis=0)
        above = jnp.concatenate([inner_ref[f], x_ref[f]], axis=0)
        slabs.append(jnp.where(even, below, above))
    own_sums(slabs, w_ref, b_ref, acc0_ref, acc1_ref)


def own_far_body(tiles, x_ref, outer_ref, w_ref, b_ref, acc0_ref, acc1_ref):
    slabs = [outer_slab(outer_ref[f], x_ref.at[f], tiles) for f in range(2)]
    own_sums(slabs, w_ref, b_ref, acc0_ref, acc1_ref)


def hidden(slab, bases, places_of, w_ref, tiles, whole, h0_ref, h1_ref, sum0_ref, sum1_ref):
    rows, cols = sum0_ref.shape[:2]
    started = lax.axis_index("tm") > 0

    @pl.when(started)
    def _():
        taps = [row_taps(slab(f), rows) for f in range(2)]
        shared, extra = weight_rows(w_ref, 0), weight_rows(w_ref, 1)
        early, late = convolved_pair(taps[0], taps[1], shared, extra, rows, cols)
        sum0_ref[...] = bases[0]() + early
        sum1_ref[...] = bases[1]() + late

    @pl.when(jnp.logical_not(started))
    def _():
        sum0_ref[...] = bases[0]()
        sum1_ref[...] = bases[1]()

    h0_ref[...] = silu_rows(sum0_ref[...], places_of.start, whole, tiles)
    h1_ref[...] = silu_rows(sum1_ref[...], places_of.start, whole, tiles)


def from_near(acc_ref, start, rows):
    return lambda: acc_ref[pl.ds(start, rows)]


def middle_body(tiles, m_ref, w_ref, _, acc0_ref, acc1_ref, h0_ref, h1_ref, sum0_ref, sum1_ref):
    rows = m_ref.shape[1]
    start = 2 * parity()
    bases = [from_near(acc_ref, start, rows - 2) for acc_ref in (acc0_ref, acc1_ref)]
    place = places(rows)[0]
    hidden(lambda f: m_ref[f], bases, place, w_ref, tiles, rows, h0_ref, h1_ref, sum0_ref, sum1_ref)


def partial_rows(times, h0, h1, v_ref, rows, cols, send_ref):
    has_next = lax.axis_index("tm") < times - 1

    @pl.when(has_next)
    def _():
        both = (h0.astype(jnp.float32) + h1.astype(jnp.float32)).astype(jnp.bfloat16)
        taps = row_taps(both, rows) + row_taps(h1, rows)
        part = convolved(taps, weight_rows(v_ref, 0) + weight_rows(v_ref, 1), rows, cols)
        send_ref[...] = part.astype(jnp.bfloat16)

    @pl.when(jnp.logical_not(has_next))
    def _():
        send_ref[...] = jnp.zeros_like(send_ref)


def near_body(
    tiles, times, m_ref, inner_ref, w_ref, v_ref, acc0_ref, acc1_ref, mid0_ref, mid1_ref,
    send_ref, h0_ref, h1_ref, sum0_ref, sum1_ref,
):
    rows, cols = m_ref.shape[1:3]
    odd = parity()
    start = (1 - odd) * (rows - 2)
    bases = [from_near(acc_ref, start, 2) for acc_ref in (acc0_ref, acc1_ref)]
    place = places(rows)[1]

    def slab(f):
        return inner_slab(inner_ref[f], m_ref.at[f])

    middle, near = pl.ds(2 * odd, rows - 2), pl.ds(start, 2)
    h0_ref[middle], h1_ref[middle] = mid0_ref[...], mid1_ref[...]
    hidden(
        slab, bases, place, w_ref, tiles, rows, h0_ref.at[near], h1_ref.at[near], sum0_ref,
        sum1_ref,
    )
    partial_rows(times, h0_ref[...], h1_ref[...], v_ref, rows - 2, cols, send_ref)


def far_body(
    tiles, times, m_ref, outer_ref, w_ref, v_ref, acc0_ref, acc1_ref, near0_ref, near1_ref,
    send_ref, h0_ref, h1_ref, sum0_ref, sum1_ref,
):
    rows, cols = m_ref.shape[1:3]
    odd = parity()
    far = places(rows)[2]
    near = pl.ds(2 * (1 - odd), rows)

    def slab(f):
        return outer_slab(outer_ref[f], m_ref.at[f], tiles)

    bases = [lambda: acc0_ref[...], lambda: acc1_ref[...]]
    h0_ref[near], h1_ref[near] = near0_ref[...], near1_ref[...]
    hidden(
        slab, bases, far, w_ref, tiles, rows, h0_ref.at[far], h1_ref.at[far], sum0_ref, sum1_ref
    )
    side = pl.ds(odd * (rows - 2), 4)
    partial_rows(times, h0_ref[side], h1_ref[side], v_ref, 2, cols, send_ref)


def rest_body(x_ref, h0_ref, h1_ref, v_ref, b_ref, out_ref):
    rows, cols = x_ref.shape[1:3]
    h0, h1 = h0_ref[...], h1_ref[...]
    taps = row_taps(h0, rows) + row_taps(h0, rows) + row_taps(h1, rows)
    weights = weight_rows(v_ref, 1) + 2 * weight_rows(v_ref, 2)
    part = convolved(taps, weights, rows, cols)
    total = x_ref[0].astype(jnp.float32) + x_ref[1].astype(jnp.float32) + part
    out_ref[0] = total * 0.5 + b_ref[...]


def join_body(rest_ref, near_ref, far_ref, out_ref):
    rows = rest_ref.shape[1]
    odd = parity()
    first = lax.axis_index("tm") == 0
    for part_ref, start in ((near_ref, 2 * (1 - odd)), (far_ref, odd * (rows - 2))):
        part = part_ref[...].astype(jnp.float32)
        part = jnp.where(first, jnp.zeros_like(part), part)
        place = pl.ds(start, part.shape[0])
        out_ref[0, place] = (rest_ref[0, place] + 0.5 * part).astype(jnp.bfloat16)


def block(x, weight_first, bias_first, weight_second, bias_second):
    _, rows, cols, channels = x.shape
    clips, tiles, times = (lax.axis_size(axis) for axis in ("clips", "tile", "tm"))
    forward = [(i, i + 1) for i in range(times - 1)]
    ring = forward + [(times - 1, 0)]
    inner_pairs = [(i, i + 1) for i in range(0, tiles - 1, 2)]
    outer_pairs = [(i, i + 1) for i in range(1, tiles - 1, 2)]
    inner_pairs += [(j, i) for i, j in inner_pairs]
    outer_pairs += [(j, i) for i, j in outer_pairs]
    paired = {i for i, _ in outer_pairs}
    unpaired = [i for i in range(tiles) if i not in paired]
    outer_full = [(c * tiles + i, c * tiles + j) for c in range(clips) for i, j in outer_pairs]
    outer_full += [(c * tiles + i, (c + 1) % clips * tiles + i) for c in range(clips) for i in unpaired]
    diagonal = [(i * times + s, j * times + t) for i, j in outer_pairs for s, t in forward]

    def frames(*lead, dtype=jnp.bfloat16):
        return jax.ShapeDtypeStruct((*lead, cols, channels), dtype)

    f32 = jnp.float32
    earlier = lax.ppermute(x, "tm", ring)
    x, outer_edge, inner_edge = call(
        edges_body,
        [frames(2, rows), frames(2, 2), frames(2, 2)],
        (pltpu.with_memory_space_constraint(x, pltpu.HBM),),
        10**10,
        in_specs=[HBM],
        scratch=[pltpu.SemaphoreType.DMA(())],
    )
    inner = lax.ppermute(inner_edge, "tile", inner_pairs)
    outer = lax.ppermute(outer_edge, ("clips", "tile"), outer_full)
    corner = lax.ppermute(outer_edge, ("tile", "tm"), diagonal)

    bias_first = bias_first.reshape(1, 1, -1)
    bias_second = bias_second.reshape(1, 1, -1)
    unit = 2 * 9 * channels * channels * cols
    wide = rows + 2
    sums0, sums1 = call(
        own_near_body,
        [frames(rows, dtype=f32), frames(rows, dtype=f32)],
        (x, inner, weight_first, bias_first),
        3 * unit * rows,
    )
    far0, far1 = call(
        functools.partial(own_far_body, tiles),
        [frames(2, dtype=f32), frames(2, dtype=f32)],
        (x, outer, weight_first, bias_first),
        0,
    )
    (inner_edge,) = call(turn_body, [frames(2, 2)], (earlier,), 0)
    inner_corner = lax.ppermute(inner_edge, "tile", inner_pairs)

    def sums(count):
        return [pltpu.VMEM((count, cols, channels), f32)] * 2

    mid0, mid1 = call(
        functools.partial(middle_body, tiles),
        [frames(rows - 2), frames(rows - 2)],
        (earlier, weight_first, weight_second, sums0, sums1),
        0,
        scratch=sums(rows - 2),
    )
    near_send, near0, near1 = call(
        functools.partial(near_body, tiles, times),
        [frames(rows - 2), frames(rows), frames(rows)],
        (earlier, inner_corner, weight_first, weight_second, sums0, sums1, mid0, mid1),
        0,
        scratch=sums(2),
    )
    near_part = lax.ppermute(near_send, "tm", ring)
    far_send, h0, h1 = call(
        functools.partial(far_body, tiles, times),
        [frames(2), frames(wide), frames(wide)],
        (earlier, corner, weight_first, weight_second, far0, far1, near0, near1),
        0,
        scratch=sums(2),
    )
    far_part = lax.ppermute(far_send, "tm", forward)
    (rest,) = call(
        rest_body,
        [frames(1, rows, dtype=f32)],
        (x, h0, h1, weight_second, bias_second),
        3 * unit * rows,
    )
    (pooled,) = call(join_body, [frames(1, rows)], (rest, near_part, far_part), 0)
    return pooled


def solution(mesh):
    in_specs = (P(("clips", "tm"), "tile", None, None), P(), P(), P(), P())
    out_specs = P(("clips", "tm"), "tile", None, None)
    return jax.shard_map(block, mesh=mesh, in_specs=in_specs, out_specs=out_specs, check_vma=False)
```

```python
import functools

import jax
import jax.numpy as jnp
from jax import lax
from jax.experimental import pallas as pl
from jax.experimental.pallas import tpu as pltpu
from jax.sharding import PartitionSpec as P


VMEM = pl.BlockSpec(memory_space=pltpu.VMEM)
HBM = pl.BlockSpec(memory_space=pltpu.HBM)


def call(body, outs, args, flops, in_specs=None, out_specs=None, scratch=(), aliases=None):
    return pl.pallas_call(
        body,
        out_shape=outs,
        in_specs=in_specs or [VMEM] * len(args),
        out_specs=out_specs or [VMEM] * len(outs),
        scratch_shapes=scratch,
        input_output_aliases=aliases or {},
        compiler_params=pltpu.CompilerParams(vmem_limit_bytes=16 << 20),
        cost_estimate=pl.CostEstimate(flops=flops, bytes_accessed=0, transcendentals=0),
    )(*args)


def flat(value):
    return value.reshape(-1, value.shape[-1])


def row_taps(slab, rows):
    return [flat(slab[p : p + rows]) for p in range(3)]


def shifted_columns(part, q):
    if q == 1:
        return part
    cols = part.shape[1]
    col = lax.broadcasted_iota(jnp.int32, part.shape, 1)
    edge, steps = (0, 1) if q == 0 else (cols - 1, cols - 1)
    return jnp.where(col == edge, 0.0, pltpu.roll(part, steps, 1))


def convolved(lhs, weights, rows, cols):
    stacked = jnp.concatenate(lhs, axis=1)
    total = None
    for q in range(3):
        taps = jnp.concatenate([w[q] for w in weights], axis=0)
        part = jnp.dot(stacked, taps, preferred_element_type=jnp.float32)
        part = shifted_columns(part.reshape(rows, cols, part.shape[-1]), q)
        total = part if total is None else total + part
    return total


def convolved_pair(first, second, shared, extra, rows, cols):
    lhs = jnp.concatenate([jnp.concatenate(taps, axis=1) for taps in (first, second)], axis=0)
    count = rows * cols
    total = None
    for q in range(3):
        taps = [jnp.concatenate([w[q] for w in weights], axis=0) for weights in (shared, extra)]
        part = jnp.dot(lhs, taps[0], preferred_element_type=jnp.float32)
        more = jnp.dot(lhs[count:], taps[1], preferred_element_type=jnp.float32)
        part = jnp.concatenate([part[:count] + more, part[count:]], axis=0)
        part = shifted_columns(part.reshape(2 * rows, cols, part.shape[-1]), q)
        total = part if total is None else total + part
    return total[:rows], total[rows:]


def parity():
    return lax.rem(lax.axis_index("tile"), 2)


def either(first, second):
    even = parity() == 0
    return jnp.concatenate([jnp.where(even, a, b) for a, b in zip(first, second)], axis=0)


def own_edge(own, side):
    odd = parity()
    last = own.shape[0] - 2
    return own[pl.ds((odd if side == 0 else 1 - odd) * last, 2)]


def outer_slab(outer, own, tiles):
    tile = lax.axis_index("tile")
    beyond = (tile == 0) | ((tile == tiles - 1) & (parity() == 1))
    outer = jnp.where(beyond, jnp.zeros_like(outer), outer)
    edge = own_edge(own, 0)
    return either([outer, edge], [edge, outer])


def inner_slab(inner, own):
    edge = own_edge(own, 1)
    return either([edge, inner], [inner, edge])


def places(rows):
    odd = parity()
    return pl.ds(2, rows - 2), pl.ds((1 - odd) * rows, 2), pl.ds(odd * rows, 2)


def weight_rows(w_ref, a):
    return [[w_ref[a, p, q] for q in range(3)] for p in range(3)]


def silu_rows(value, start, rows, tiles):
    hidden = (0.5 * value * (1.0 + jnp.tanh(0.5 * value))).astype(jnp.bfloat16)
    row = lax.broadcasted_iota(jnp.int32, hidden.shape, 0) + start
    row = row + lax.axis_index("tile") * rows - 1
    inside = (row >= 0) & (row < tiles * rows)
    return jnp.where(inside, hidden, jnp.zeros_like(hidden))


def edges_body(x_ref, own_ref, outer_ref, inner_ref, sem):
    copy = pltpu.make_async_copy(x_ref, own_ref, sem)
    copy.start()
    copy.wait()
    for f in range(2):
        outer_ref[f] = own_edge(own_ref.at[f], 0)
        inner_ref[f] = own_edge(own_ref.at[f], 1)


def turn_body(m_ref, inner_ref):
    for f in range(2):
        inner_ref[f] = own_edge(m_ref.at[f], 1)


def own_sums(slabs, w_ref, b_ref, acc0_ref, acc1_ref):
    rows, cols = acc0_ref.shape[:2]
    taps = [row_taps(slab, rows) for slab in slabs]
    shared, extra = weight_rows(w_ref, 2), weight_rows(w_ref, 1)
    late, early = convolved_pair(taps[1], taps[0], shared, extra, rows, cols)
    acc0_ref[...] = b_ref[...] + early
    acc1_ref[...] = b_ref[...] + late


def own_near_body(x_ref, inner_ref, w_ref, b_ref, acc0_ref, acc1_ref):
    even = parity() == 0
    slabs = []
    for f in range(2):
        below = jnp.concatenate([x_ref[f], inner_ref[f]], axis=0)
        above = jnp.concatenate([inner_ref[f], x_ref[f]], axis=0)
        slabs.append(jnp.where(even, below, above))
    own_sums(slabs, w_ref, b_ref, acc0_ref, acc1_ref)


def own_far_body(tiles, x_ref, outer_ref, w_ref, b_ref, acc0_ref, acc1_ref):
    slabs = [outer_slab(outer_ref[f], x_ref.at[f], tiles) for f in range(2)]
    own_sums(slabs, w_ref, b_ref, acc0_ref, acc1_ref)


def hidden(slab, bases, places_of, w_ref, tiles, whole, h0_ref, h1_ref, sum0_ref, sum1_ref):
    rows, cols = sum0_ref.shape[:2]
    started = lax.axis_index("tm") > 0

    @pl.when(started)
    def _():
        taps = [row_taps(slab(f), rows) for f in range(2)]
        shared, extra = weight_rows(w_ref, 0), weight_rows(w_ref, 1)
        early, late = convolved_pair(taps[0], taps[1], shared, extra, rows, cols)
        sum0_ref[...] = bases[0]() + early
        sum1_ref[...] = bases[1]() + late

    @pl.when(jnp.logical_not(started))
    def _():
        sum0_ref[...] = bases[0]()
        sum1_ref[...] = bases[1]()

    h0_ref[...] = silu_rows(sum0_ref[...], places_of.start, whole, tiles)
    h1_ref[...] = silu_rows(sum1_ref[...], places_of.start, whole, tiles)


def from_near(acc_ref, start, rows):
    return lambda: acc_ref[pl.ds(start, rows)]


def middle_body(tiles, m_ref, w_ref, _, acc0_ref, acc1_ref, h0_ref, h1_ref, sum0_ref, sum1_ref):
    rows = m_ref.shape[1]
    start = 2 * parity()
    bases = [from_near(acc_ref, start, rows - 2) for acc_ref in (acc0_ref, acc1_ref)]
    place = places(rows)[0]
    hidden(lambda f: m_ref[f], bases, place, w_ref, tiles, rows, h0_ref, h1_ref, sum0_ref, sum1_ref)


def partial_rows(times, h0, h1, v_ref, rows, cols, send_ref):
    has_next = lax.axis_index("tm") < times - 1

    @pl.when(has_next)
    def _():
        both = (h0.astype(jnp.float32) + h1.astype(jnp.float32)).astype(jnp.bfloat16)
        taps = row_taps(both, rows) + row_taps(h1, rows)
        part = convolved(taps, weight_rows(v_ref, 0) + weight_rows(v_ref, 1), rows, cols)
        send_ref[...] = part.astype(jnp.bfloat16)

    @pl.when(jnp.logical_not(has_next))
    def _():
        send_ref[...] = jnp.zeros_like(send_ref)


def near_body(
    tiles, times, m_ref, inner_ref, w_ref, v_ref, acc0_ref, acc1_ref, mid0_ref, mid1_ref,
    send_ref, h0_ref, h1_ref, sum0_ref, sum1_ref,
):
    rows, cols = m_ref.shape[1:3]
    odd = parity()
    start = (1 - odd) * (rows - 2)
    bases = [from_near(acc_ref, start, 2) for acc_ref in (acc0_ref, acc1_ref)]
    place = places(rows)[1]

    def slab(f):
        return inner_slab(inner_ref[f], m_ref.at[f])

    middle, near = pl.ds(2 * odd, rows - 2), pl.ds(start, 2)
    h0_ref[middle], h1_ref[middle] = mid0_ref[...], mid1_ref[...]
    hidden(
        slab, bases, place, w_ref, tiles, rows, h0_ref.at[near], h1_ref.at[near], sum0_ref,
        sum1_ref,
    )
    partial_rows(times, h0_ref[...], h1_ref[...], v_ref, rows - 2, cols, send_ref)


def far_body(
    tiles, times, m_ref, outer_ref, w_ref, v_ref, acc0_ref, acc1_ref, near0_ref, near1_ref,
    send_ref, h0_ref, h1_ref, sum0_ref, sum1_ref,
):
    rows, cols = m_ref.shape[1:3]
    odd = parity()

    def slab(f):
        return outer_slab(outer_ref[f], m_ref.at[f], tiles)

    def beside(h_ref, near_ref):
        near = near_ref[pl.ds(odd * (rows - 2), 2)]
        return either([h_ref[...], near], [near, h_ref[...]])

    bases = [lambda: acc0_ref[...], lambda: acc1_ref[...]]
    place = places(rows)[2]
    hidden(slab, bases, place, w_ref, tiles, rows, h0_ref, h1_ref, sum0_ref, sum1_ref)
    h0, h1 = beside(h0_ref, near0_ref), beside(h1_ref, near1_ref)
    partial_rows(times, h0, h1, v_ref, 2, cols, send_ref)


def rest_body(
    x_ref, near0_ref, near1_ref, far0_ref, far1_ref, v_ref, b_ref, out_ref, h0_ref, h1_ref
):
    rows, cols = x_ref.shape[1:3]
    near, far = pl.ds(2 * (1 - parity()), rows), places(rows)[2]
    h0_ref[near], h1_ref[near] = near0_ref[...], near1_ref[...]
    h0_ref[far], h1_ref[far] = far0_ref[...], far1_ref[...]
    h0, h1 = row_taps(h0_ref[...], rows), row_taps(h1_ref[...], rows)
    weights = weight_rows(v_ref, 1) + 2 * weight_rows(v_ref, 2)
    part = convolved(h0 + h0 + h1, weights, rows, cols)
    total = x_ref[0].astype(jnp.float32) + x_ref[1].astype(jnp.float32) + part
    out_ref[0] = total * 0.5 + b_ref[...]


def join(rest_ref, part_ref, out_ref, start, made_ref, sem):
    part = part_ref[...].astype(jnp.float32)
    part = jnp.where(lax.axis_index("tm") == 0, jnp.zeros_like(part), part)
    place = pl.ds(start, part.shape[0])
    made_ref[...] = (rest_ref[0, place] + 0.5 * part).astype(jnp.bfloat16)
    copy = pltpu.make_async_copy(made_ref, out_ref.at[0, place], sem)
    copy.start()
    copy.wait()


def join_near_body(rest_ref, part_ref, out_ref, made_ref, sem):
    join(rest_ref, part_ref, out_ref, 2 * (1 - parity()), made_ref, sem)


def join_far_body(rest_ref, part_ref, _, out_ref, made_ref, sem):
    join(rest_ref, part_ref, out_ref, parity() * (rest_ref.shape[1] - 2), made_ref, sem)


def block(x, weight_first, bias_first, weight_second, bias_second):
    _, rows, cols, channels = x.shape
    clips, tiles, times = (lax.axis_size(axis) for axis in ("clips", "tile", "tm"))
    forward = [(i, i + 1) for i in range(times - 1)]
    ring = forward + [(times - 1, 0)]
    inner_pairs = [(i, i + 1) for i in range(0, tiles - 1, 2)]
    outer_pairs = [(i, i + 1) for i in range(1, tiles - 1, 2)]
    inner_pairs += [(j, i) for i, j in inner_pairs]
    outer_pairs += [(j, i) for i, j in outer_pairs]
    paired = {i for i, _ in outer_pairs}
    unpaired = [i for i in range(tiles) if i not in paired]
    outer_full = [(c * tiles + i, c * tiles + j) for c in range(clips) for i, j in outer_pairs]
    outer_full += [(c * tiles + i, (c + 1) % clips * tiles + i) for c in range(clips) for i in unpaired]
    diagonal = [(i * times + s, j * times + t) for i, j in outer_pairs for s, t in forward]

    def frames(*lead, dtype=jnp.bfloat16):
        return jax.ShapeDtypeStruct((*lead, cols, channels), dtype)

    f32 = jnp.float32
    earlier = lax.ppermute(x, "tm", ring)
    x, outer_edge, inner_edge = call(
        edges_body,
        [frames(2, rows), frames(2, 2), frames(2, 2)],
        (pltpu.with_memory_space_constraint(x, pltpu.HBM),),
        10**10,
        in_specs=[HBM],
        scratch=[pltpu.SemaphoreType.DMA(())],
    )
    inner = lax.ppermute(inner_edge, "tile", inner_pairs)
    outer = lax.ppermute(outer_edge, ("clips", "tile"), outer_full)
    corner = lax.ppermute(outer_edge, ("tile", "tm"), diagonal)

    bias_first = bias_first.reshape(1, 1, -1)
    bias_second = bias_second.reshape(1, 1, -1)
    unit = 2 * 9 * channels * channels * cols
    wide = rows + 2
    sums0, sums1 = call(
        own_near_body,
        [frames(rows, dtype=f32), frames(rows, dtype=f32)],
        (x, inner, weight_first, bias_first),
        3 * unit * rows,
    )
    far0, far1 = call(
        functools.partial(own_far_body, tiles),
        [frames(2, dtype=f32), frames(2, dtype=f32)],
        (x, outer, weight_first, bias_first),
        0,
    )
    (inner_edge,) = call(turn_body, [frames(2, 2)], (earlier,), 0)
    inner_corner = lax.ppermute(inner_edge, "tile", inner_pairs)

    def sums(count):
        return [pltpu.VMEM((count, cols, channels), f32)] * 2

    mid0, mid1 = call(
        functools.partial(middle_body, tiles),
        [frames(rows - 2), frames(rows - 2)],
        (earlier, weight_first, weight_second, sums0, sums1),
        0,
        scratch=sums(rows - 2),
    )
    near_send, near0, near1 = call(
        functools.partial(near_body, tiles, times),
        [frames(rows - 2), frames(rows), frames(rows)],
        (earlier, inner_corner, weight_first, weight_second, sums0, sums1, mid0, mid1),
        0,
        scratch=sums(2),
    )
    near_part = lax.ppermute(near_send, "tm", ring)
    far_send, last0, last1 = call(
        functools.partial(far_body, tiles, times),
        [frames(2), frames(2), frames(2)],
        (earlier, corner, weight_first, weight_second, far0, far1, near0, near1),
        0,
        scratch=sums(2),
    )
    far_part = lax.ppermute(far_send, "tm", forward)
    (rest,) = call(
        rest_body,
        [frames(1, rows, dtype=f32)],
        (x, near0, near1, last0, last1, weight_second, bias_second),
        3 * unit * rows,
        scratch=[pltpu.VMEM((wide, cols, channels), jnp.bfloat16)] * 2,
    )
    (pooled,) = call(
        join_near_body,
        [frames(1, rows)],
        (rest, near_part),
        0,
        out_specs=[HBM],
        scratch=[pltpu.VMEM((rows - 2, cols, channels), jnp.bfloat16), pltpu.SemaphoreType.DMA(())],
    )
    (pooled,) = call(
        join_far_body,
        [frames(1, rows)],
        (rest, far_part, pooled),
        0,
        in_specs=[VMEM, VMEM, HBM],
        out_specs=[HBM],
        scratch=[pltpu.VMEM((2, cols, channels), jnp.bfloat16), pltpu.SemaphoreType.DMA(())],
        aliases={2: 0},
    )
    return pooled


def solution(mesh):
    in_specs = (P(("clips", "tm"), "tile", None, None), P(), P(), P(), P())
    out_specs = P(("clips", "tm"), "tile", None, None)
    return jax.shard_map(block, mesh=mesh, in_specs=in_specs, out_specs=out_specs, check_vma=False)
```

```python
import functools

import jax
import jax.numpy as jnp
from jax import lax
from jax.experimental import pallas as pl
from jax.experimental.pallas import tpu as pltpu
from jax.sharding import PartitionSpec as P


VMEM = pl.BlockSpec(memory_space=pltpu.VMEM)
HBM = pl.BlockSpec(memory_space=pltpu.HBM)


def call(body, outs, args, flops, in_specs=None, out_specs=None, scratch=(), aliases=None):
    return pl.pallas_call(
        body,
        out_shape=outs,
        in_specs=in_specs or [VMEM] * len(args),
        out_specs=out_specs or [VMEM] * len(outs),
        scratch_shapes=scratch,
        input_output_aliases=aliases or {},
        compiler_params=pltpu.CompilerParams(vmem_limit_bytes=16 << 20),
        cost_estimate=pl.CostEstimate(flops=flops, bytes_accessed=0, transcendentals=0),
    )(*args)


def flat(value):
    return value.reshape(-1, value.shape[-1])


def row_taps(slab, rows):
    return [flat(slab[p : p + rows]) for p in range(3)]


def shifted_columns(part, q):
    if q == 1:
        return part
    cols = part.shape[1]
    col = lax.broadcasted_iota(jnp.int32, part.shape, 1)
    edge, steps = (0, 1) if q == 0 else (cols - 1, cols - 1)
    return jnp.where(col == edge, 0.0, pltpu.roll(part, steps, 1))


def convolved(lhs, weights, rows, cols):
    stacked = jnp.concatenate(lhs, axis=1)
    total = None
    for q in range(3):
        taps = jnp.concatenate([w[q] for w in weights], axis=0)
        part = jnp.dot(stacked, taps, preferred_element_type=jnp.float32)
        part = shifted_columns(part.reshape(rows, cols, part.shape[-1]), q)
        total = part if total is None else total + part
    return total


def convolved_pair(first, second, shared, extra, rows, cols):
    lhs = jnp.concatenate([jnp.concatenate(taps, axis=1) for taps in (first, second)], axis=0)
    count = rows * cols
    total = None
    for q in range(3):
        taps = [jnp.concatenate([w[q] for w in weights], axis=0) for weights in (shared, extra)]
        part = jnp.dot(lhs, taps[0], preferred_element_type=jnp.float32)
        more = jnp.dot(lhs[count:], taps[1], preferred_element_type=jnp.float32)
        part = jnp.concatenate([part[:count] + more, part[count:]], axis=0)
        part = shifted_columns(part.reshape(2 * rows, cols, part.shape[-1]), q)
        total = part if total is None else total + part
    return total[:rows], total[rows:]


def parity():
    return lax.rem(lax.axis_index("tile"), 2)


def either(first, second):
    even = parity() == 0
    return jnp.concatenate([jnp.where(even, a, b) for a, b in zip(first, second)], axis=0)


def own_edge(own, side):
    odd = parity()
    last = own.shape[0] - 2
    return own[pl.ds((odd if side == 0 else 1 - odd) * last, 2)]


def outer_slab(outer, own, tiles):
    tile = lax.axis_index("tile")
    beyond = (tile == 0) | ((tile == tiles - 1) & (parity() == 1))
    outer = jnp.where(beyond, jnp.zeros_like(outer), outer)
    edge = own_edge(own, 0)
    return either([outer, edge], [edge, outer])


def inner_slab(inner, own):
    edge = own_edge(own, 1)
    return either([edge, inner], [inner, edge])


def places(rows):
    odd = parity()
    return pl.ds(2, rows - 2), pl.ds((1 - odd) * rows, 2), pl.ds(odd * rows, 2)


def weight_rows(w_ref, a):
    return [[w_ref[a, p, q] for q in range(3)] for p in range(3)]


def silu_rows(value, start, rows, tiles):
    hidden = (0.5 * value * (1.0 + jnp.tanh(0.5 * value))).astype(jnp.bfloat16)
    row = lax.broadcasted_iota(jnp.int32, hidden.shape, 0) + start
    row = row + lax.axis_index("tile") * rows - 1
    inside = (row >= 0) & (row < tiles * rows)
    return jnp.where(inside, hidden, jnp.zeros_like(hidden))


def edges_body(x_ref, own_ref, outer_ref, inner_ref, sem):
    copy = pltpu.make_async_copy(x_ref, own_ref, sem)
    copy.start()
    copy.wait()
    for f in range(2):
        outer_ref[f] = own_edge(own_ref.at[f], 0)
        inner_ref[f] = own_edge(own_ref.at[f], 1)


def turn_body(m_ref, inner_ref):
    for f in range(2):
        inner_ref[f] = own_edge(m_ref.at[f], 1)


def own_sums(slabs, w_ref, b_ref, acc0_ref, acc1_ref):
    rows, cols = acc0_ref.shape[:2]
    taps = [row_taps(slab, rows) for slab in slabs]
    shared, extra = weight_rows(w_ref, 2), weight_rows(w_ref, 1)
    late, early = convolved_pair(taps[1], taps[0], shared, extra, rows, cols)
    acc0_ref[...] = b_ref[...] + early
    acc1_ref[...] = b_ref[...] + late


def own_near_body(x_ref, inner_ref, w_ref, b_ref, acc0_ref, acc1_ref):
    even = parity() == 0
    slabs = []
    for f in range(2):
        below = jnp.concatenate([x_ref[f], inner_ref[f]], axis=0)
        above = jnp.concatenate([inner_ref[f], x_ref[f]], axis=0)
        slabs.append(jnp.where(even, below, above))
    own_sums(slabs, w_ref, b_ref, acc0_ref, acc1_ref)


def own_far_body(tiles, x_ref, outer_ref, w_ref, b_ref, acc0_ref, acc1_ref):
    slabs = [outer_slab(outer_ref[f], x_ref.at[f], tiles) for f in range(2)]
    own_sums(slabs, w_ref, b_ref, acc0_ref, acc1_ref)


def hidden(slab, bases, place, w_ref, tiles, whole, h0_ref, h1_ref):
    rows, cols = h0_ref.shape[:2]
    started = lax.axis_index("tm") > 0

    def store(sums):
        for h_ref, total in zip((h0_ref, h1_ref), sums):
            h_ref[...] = silu_rows(total, place.start, whole, tiles)

    @pl.when(started)
    def _():
        taps = [row_taps(slab(f), rows) for f in range(2)]
        shared, extra = weight_rows(w_ref, 0), weight_rows(w_ref, 1)
        products = convolved_pair(taps[0], taps[1], shared, extra, rows, cols)
        store([base() + product for base, product in zip(bases, products)])

    @pl.when(jnp.logical_not(started))
    def _():
        store([base() for base in bases])


def from_near(acc_ref, start, rows):
    return lambda: acc_ref[pl.ds(start, rows)]


def middle_body(tiles, m_ref, w_ref, _, acc0_ref, acc1_ref, h0_ref, h1_ref):
    rows = m_ref.shape[1]
    start = 2 * parity()
    bases = [from_near(acc_ref, start, rows - 2) for acc_ref in (acc0_ref, acc1_ref)]
    place = places(rows)[0]
    hidden(lambda f: m_ref[f], bases, place, w_ref, tiles, rows, h0_ref, h1_ref)


def partial_rows(times, h0, h1, v_ref, rows, cols, send_ref):
    has_next = lax.axis_index("tm") < times - 1

    @pl.when(has_next)
    def _():
        both = (h0.astype(jnp.float32) + h1.astype(jnp.float32)).astype(jnp.bfloat16)
        taps = row_taps(both, rows) + row_taps(h1, rows)
        part = convolved(taps, weight_rows(v_ref, 0) + weight_rows(v_ref, 1), rows, cols)
        send_ref[...] = part.astype(jnp.bfloat16)

    @pl.when(jnp.logical_not(has_next))
    def _():
        send_ref[...] = jnp.zeros_like(send_ref)


def near_body(
    tiles, times, m_ref, inner_ref, w_ref, v_ref, acc0_ref, acc1_ref, mid0_ref, mid1_ref,
    send_ref, h0_ref, h1_ref,
):
    rows, cols = m_ref.shape[1:3]
    start = (1 - parity()) * (rows - 2)
    bases = [from_near(acc_ref, start, 2) for acc_ref in (acc0_ref, acc1_ref)]
    place = places(rows)[1]

    def slab(f):
        return inner_slab(inner_ref[f], m_ref.at[f])

    def beside(h_ref, mid_ref):
        below = jnp.concatenate([mid_ref[...], h_ref[...]], axis=0)
        above = jnp.concatenate([h_ref[...], mid_ref[...]], axis=0)
        return jnp.where(parity() == 0, below, above)

    hidden(slab, bases, place, w_ref, tiles, rows, h0_ref, h1_ref)
    h0, h1 = beside(h0_ref, mid0_ref), beside(h1_ref, mid1_ref)
    partial_rows(times, h0, h1, v_ref, rows - 2, cols, send_ref)


def far_body(
    tiles, times, m_ref, outer_ref, w_ref, v_ref, acc0_ref, acc1_ref, mid0_ref, mid1_ref,
    send_ref, h0_ref, h1_ref,
):
    rows, cols = m_ref.shape[1:3]
    odd = parity()

    def slab(f):
        return outer_slab(outer_ref[f], m_ref.at[f], tiles)

    def beside(h_ref, mid_ref):
        middle = mid_ref[pl.ds(odd * (rows - 4), 2)]
        return either([h_ref[...], middle], [middle, h_ref[...]])

    bases = [lambda: acc0_ref[...], lambda: acc1_ref[...]]
    hidden(slab, bases, places(rows)[2], w_ref, tiles, rows, h0_ref, h1_ref)
    h0, h1 = beside(h0_ref, mid0_ref), beside(h1_ref, mid1_ref)
    partial_rows(times, h0, h1, v_ref, 2, cols, send_ref)


def rest_body(
    x_ref, mid0_ref, mid1_ref, near0_ref, near1_ref, far0_ref, far1_ref, v_ref, b_ref, out_ref,
    h0_ref, h1_ref,
):
    rows, cols = x_ref.shape[1:3]
    middle, near, far = places(rows)
    h0_ref[middle], h1_ref[middle] = mid0_ref[...], mid1_ref[...]
    h0_ref[near], h1_ref[near] = near0_ref[...], near1_ref[...]
    h0_ref[far], h1_ref[far] = far0_ref[...], far1_ref[...]
    h0, h1 = row_taps(h0_ref[...], rows), row_taps(h1_ref[...], rows)
    weights = weight_rows(v_ref, 1) + 2 * weight_rows(v_ref, 2)
    part = convolved(h0 + h0 + h1, weights, rows, cols)
    total = x_ref[0].astype(jnp.float32) + x_ref[1].astype(jnp.float32) + part
    out_ref[0] = total * 0.5 + b_ref[...]


def join(rest_ref, part_ref, out_ref, start, made_ref, sem):
    part = part_ref[...].astype(jnp.float32)
    part = jnp.where(lax.axis_index("tm") == 0, jnp.zeros_like(part), part)
    place = pl.ds(start, part.shape[0])
    made_ref[...] = (rest_ref[0, place] + 0.5 * part).astype(jnp.bfloat16)
    copy = pltpu.make_async_copy(made_ref, out_ref.at[0, place], sem)
    copy.start()
    copy.wait()


def join_near_body(rest_ref, part_ref, out_ref, made_ref, sem):
    join(rest_ref, part_ref, out_ref, 2 * (1 - parity()), made_ref, sem)


def join_far_body(rest_ref, part_ref, _, out_ref, made_ref, sem):
    join(rest_ref, part_ref, out_ref, parity() * (rest_ref.shape[1] - 2), made_ref, sem)


def block(x, weight_first, bias_first, weight_second, bias_second):
    _, rows, cols, channels = x.shape
    clips, tiles, times = (lax.axis_size(axis) for axis in ("clips", "tile", "tm"))
    forward = [(i, i + 1) for i in range(times - 1)]
    ring = forward + [(times - 1, 0)]
    inner_pairs = [(i, i + 1) for i in range(0, tiles - 1, 2)]
    outer_pairs = [(i, i + 1) for i in range(1, tiles - 1, 2)]
    inner_pairs += [(j, i) for i, j in inner_pairs]
    outer_pairs += [(j, i) for i, j in outer_pairs]
    paired = {i for i, _ in outer_pairs}
    unpaired = [i for i in range(tiles) if i not in paired]
    outer_full = [(c * tiles + i, c * tiles + j) for c in range(clips) for i, j in outer_pairs]
    outer_full += [(c * tiles + i, (c + 1) % clips * tiles + i) for c in range(clips) for i in unpaired]
    diagonal = [(i * times + s, j * times + t) for i, j in outer_pairs for s, t in forward]

    def frames(*lead, dtype=jnp.bfloat16):
        return jax.ShapeDtypeStruct((*lead, cols, channels), dtype)

    f32 = jnp.float32
    earlier = lax.ppermute(x, "tm", ring)
    x, outer_edge, inner_edge = call(
        edges_body,
        [frames(2, rows), frames(2, 2), frames(2, 2)],
        (pltpu.with_memory_space_constraint(x, pltpu.HBM),),
        10**10,
        in_specs=[HBM],
        scratch=[pltpu.SemaphoreType.DMA(())],
    )
    inner = lax.ppermute(inner_edge, "tile", inner_pairs)
    outer = lax.ppermute(outer_edge, ("clips", "tile"), outer_full)
    corner = lax.ppermute(outer_edge, ("tile", "tm"), diagonal)

    bias_first = bias_first.reshape(1, 1, -1)
    bias_second = bias_second.reshape(1, 1, -1)
    unit = 2 * 9 * channels * channels * cols
    wide = rows + 2
    sums0, sums1 = call(
        own_near_body,
        [frames(rows, dtype=f32), frames(rows, dtype=f32)],
        (x, inner, weight_first, bias_first),
        3 * unit * rows,
    )
    far0, far1 = call(
        functools.partial(own_far_body, tiles),
        [frames(2, dtype=f32), frames(2, dtype=f32)],
        (x, outer, weight_first, bias_first),
        0,
    )
    (inner_edge,) = call(turn_body, [frames(2, 2)], (earlier,), 0)
    inner_corner = lax.ppermute(inner_edge, "tile", inner_pairs)

    mid0, mid1 = call(
        functools.partial(middle_body, tiles),
        [frames(rows - 2), frames(rows - 2)],
        (earlier, weight_first, weight_second, sums0, sums1),
        0,
    )
    near_send, near0, near1 = call(
        functools.partial(near_body, tiles, times),
        [frames(rows - 2), frames(2), frames(2)],
        (earlier, inner_corner, weight_first, weight_second, sums0, sums1, mid0, mid1),
        0,
    )
    near_part = lax.ppermute(near_send, "tm", ring)
    far_send, last0, last1 = call(
        functools.partial(far_body, tiles, times),
        [frames(2), frames(2), frames(2)],
        (earlier, corner, weight_first, weight_second, far0, far1, mid0, mid1),
        0,
    )
    far_part = lax.ppermute(far_send, "tm", forward)
    (rest,) = call(
        rest_body,
        [frames(1, rows, dtype=f32)],
        (x, mid0, mid1, near0, near1, last0, last1, weight_second, bias_second),
        3 * unit * rows,
        scratch=[pltpu.VMEM((wide, cols, channels), jnp.bfloat16)] * 2,
    )
    (pooled,) = call(
        join_near_body,
        [frames(1, rows)],
        (rest, near_part),
        0,
        out_specs=[HBM],
        scratch=[pltpu.VMEM((rows - 2, cols, channels), jnp.bfloat16), pltpu.SemaphoreType.DMA(())],
    )
    (pooled,) = call(
        join_far_body,
        [frames(1, rows)],
        (rest, far_part, pooled),
        0,
        in_specs=[VMEM, VMEM, HBM],
        out_specs=[HBM],
        scratch=[pltpu.VMEM((2, cols, channels), jnp.bfloat16), pltpu.SemaphoreType.DMA(())],
        aliases={2: 0},
    )
    return pooled


def solution(mesh):
    in_specs = (P(("clips", "tm"), "tile", None, None), P(), P(), P(), P())
    out_specs = P(("clips", "tm"), "tile", None, None)
    return jax.shard_map(block, mesh=mesh, in_specs=in_specs, out_specs=out_specs, check_vma=False)
```

```python
import functools

import jax
import jax.numpy as jnp
from jax import lax
from jax.experimental import pallas as pl
from jax.experimental.pallas import tpu as pltpu
from jax.sharding import PartitionSpec as P


VMEM = pl.BlockSpec(memory_space=pltpu.VMEM)
HBM = pl.BlockSpec(memory_space=pltpu.HBM)


def call(body, outs, args, flops, in_specs=None, out_specs=None, scratch=(), aliases=None):
    return pl.pallas_call(
        body,
        out_shape=outs,
        in_specs=in_specs or [VMEM] * len(args),
        out_specs=out_specs or [VMEM] * len(outs),
        scratch_shapes=scratch,
        input_output_aliases=aliases or {},
        compiler_params=pltpu.CompilerParams(vmem_limit_bytes=16 << 20),
        cost_estimate=pl.CostEstimate(flops=flops, bytes_accessed=0, transcendentals=0),
    )(*args)


def flat(value):
    return value.reshape(-1, value.shape[-1])


def row_taps(slab, rows):
    return [flat(slab[p : p + rows]) for p in range(3)]


def shifted_columns(part, q):
    if q == 1:
        return part
    cols = part.shape[1]
    col = lax.broadcasted_iota(jnp.int32, part.shape, 1)
    edge, steps = (0, 1) if q == 0 else (cols - 1, cols - 1)
    return jnp.where(col == edge, 0.0, pltpu.roll(part, steps, 1))


def convolved(lhs, weights, rows, cols):
    stacked = jnp.concatenate(lhs, axis=1)
    total = None
    for q in range(3):
        taps = jnp.concatenate([w[q] for w in weights], axis=0)
        part = jnp.dot(stacked, taps, preferred_element_type=jnp.float32)
        part = shifted_columns(part.reshape(rows, cols, part.shape[-1]), q)
        total = part if total is None else total + part
    return total


def convolved_pair(first, second, shared, extra, rows, cols):
    lhs = jnp.concatenate([jnp.concatenate(taps, axis=1) for taps in (first, second)], axis=0)
    count = rows * cols
    total = None
    for q in range(3):
        taps = [jnp.concatenate([w[q] for w in weights], axis=0) for weights in (shared, extra)]
        part = jnp.dot(lhs, taps[0], preferred_element_type=jnp.float32)
        more = jnp.dot(lhs[count:], taps[1], preferred_element_type=jnp.float32)
        part = jnp.concatenate([part[:count] + more, part[count:]], axis=0)
        part = shifted_columns(part.reshape(2 * rows, cols, part.shape[-1]), q)
        total = part if total is None else total + part
    return total[:rows], total[rows:]


def parity():
    return lax.rem(lax.axis_index("tile"), 2)


def either(first, second):
    even = parity() == 0
    return jnp.concatenate([jnp.where(even, a, b) for a, b in zip(first, second)], axis=0)


def own_edge(own, side):
    odd = parity()
    last = own.shape[0] - 2
    return own[pl.ds((odd if side == 0 else 1 - odd) * last, 2)]


def outer_slab(outer, own, tiles):
    tile = lax.axis_index("tile")
    beyond = (tile == 0) | ((tile == tiles - 1) & (parity() == 1))
    outer = jnp.where(beyond, jnp.zeros_like(outer), outer)
    edge = own_edge(own, 0)
    return either([outer, edge], [edge, outer])


def inner_slab(inner, own):
    edge = own_edge(own, 1)
    return either([edge, inner], [inner, edge])


def places(rows):
    odd = parity()
    return pl.ds(2, rows - 2), pl.ds((1 - odd) * rows, 2), pl.ds(odd * rows, 2)


def weight_rows(w_ref, a):
    return [[w_ref[a, p, q] for q in range(3)] for p in range(3)]


def silu_rows(value, start, rows, tiles):
    half = 0.5 * value
    hidden = (half + half * jnp.tanh(half)).astype(jnp.bfloat16)
    row = lax.broadcasted_iota(jnp.int32, hidden.shape, 0) + start
    row = row + lax.axis_index("tile") * rows - 1
    inside = (row >= 0) & (row < tiles * rows)
    return jnp.where(inside, hidden, jnp.zeros_like(hidden))


def edges_body(x_ref, own_ref, outer_ref, inner_ref, sems):
    copies = [
        pltpu.make_async_copy(x_ref.at[f], own_ref.at[f], sems.at[f]) for f in range(2)
    ]
    for copy in copies:
        copy.start()
    for f, copy in enumerate(copies):
        copy.wait()
        outer_ref[f] = own_edge(own_ref.at[f], 0)
        inner_ref[f] = own_edge(own_ref.at[f], 1)


def turn_body(m_ref, inner_ref):
    for f in range(2):
        inner_ref[f] = own_edge(m_ref.at[f], 1)


def own_sums(slabs, w_ref, b_ref, acc0_ref, acc1_ref):
    rows, cols = acc0_ref.shape[:2]
    taps = [row_taps(slab, rows) for slab in slabs]
    shared, extra = weight_rows(w_ref, 2), weight_rows(w_ref, 1)
    late, early = convolved_pair(taps[1], taps[0], shared, extra, rows, cols)
    acc0_ref[...] = b_ref[...] + early
    acc1_ref[...] = b_ref[...] + late


def own_near_body(x_ref, inner_ref, w_ref, b_ref, acc0_ref, acc1_ref):
    even = parity() == 0
    slabs = []
    for f in range(2):
        below = jnp.concatenate([x_ref[f], inner_ref[f]], axis=0)
        above = jnp.concatenate([inner_ref[f], x_ref[f]], axis=0)
        slabs.append(jnp.where(even, below, above))
    own_sums(slabs, w_ref, b_ref, acc0_ref, acc1_ref)


def own_far_body(tiles, x_ref, outer_ref, w_ref, b_ref, acc0_ref, acc1_ref):
    slabs = [outer_slab(outer_ref[f], x_ref.at[f], tiles) for f in range(2)]
    own_sums(slabs, w_ref, b_ref, acc0_ref, acc1_ref)


def hidden(slab, bases, place, w_ref, tiles, whole, h0_ref, h1_ref):
    rows, cols = h0_ref.shape[:2]
    started = lax.axis_index("tm") > 0

    def store(sums):
        for h_ref, total in zip((h0_ref, h1_ref), sums):
            h_ref[...] = silu_rows(total, place.start, whole, tiles)

    @pl.when(started)
    def _():
        taps = [row_taps(slab(f), rows) for f in range(2)]
        shared, extra = weight_rows(w_ref, 0), weight_rows(w_ref, 1)
        products = convolved_pair(taps[0], taps[1], shared, extra, rows, cols)
        store([base() + product for base, product in zip(bases, products)])

    @pl.when(jnp.logical_not(started))
    def _():
        store([base() for base in bases])


def from_near(acc_ref, start, rows):
    return lambda: acc_ref[pl.ds(start, rows)]


def middle_body(tiles, m_ref, w_ref, _, acc0_ref, acc1_ref, h0_ref, h1_ref):
    rows = m_ref.shape[1]
    start = 2 * parity()
    bases = [from_near(acc_ref, start, rows - 2) for acc_ref in (acc0_ref, acc1_ref)]
    place = places(rows)[0]
    hidden(lambda f: m_ref[f], bases, place, w_ref, tiles, rows, h0_ref, h1_ref)


def partial_rows(times, h0, h1, v_ref, rows, cols, send_ref):
    has_next = lax.axis_index("tm") < times - 1

    @pl.when(has_next)
    def _():
        both = (h0.astype(jnp.float32) + h1.astype(jnp.float32)).astype(jnp.bfloat16)
        taps = row_taps(both, rows) + row_taps(h1, rows)
        part = convolved(taps, weight_rows(v_ref, 0) + weight_rows(v_ref, 1), rows, cols)
        send_ref[...] = part.astype(jnp.bfloat16)

    @pl.when(jnp.logical_not(has_next))
    def _():
        send_ref[...] = jnp.zeros_like(send_ref)


def near_body(
    tiles, times, m_ref, inner_ref, w_ref, v_ref, acc0_ref, acc1_ref, mid0_ref, mid1_ref,
    send_ref, h0_ref, h1_ref,
):
    rows, cols = m_ref.shape[1:3]
    start = (1 - parity()) * (rows - 2)
    bases = [from_near(acc_ref, start, 2) for acc_ref in (acc0_ref, acc1_ref)]
    place = places(rows)[1]

    def slab(f):
        return inner_slab(inner_ref[f], m_ref.at[f])

    def beside(h_ref, mid_ref):
        below = jnp.concatenate([mid_ref[...], h_ref[...]], axis=0)
        above = jnp.concatenate([h_ref[...], mid_ref[...]], axis=0)
        return jnp.where(parity() == 0, below, above)

    hidden(slab, bases, place, w_ref, tiles, rows, h0_ref, h1_ref)
    h0, h1 = beside(h0_ref, mid0_ref), beside(h1_ref, mid1_ref)
    partial_rows(times, h0, h1, v_ref, rows - 2, cols, send_ref)


def far_body(
    tiles, times, m_ref, outer_ref, w_ref, v_ref, acc0_ref, acc1_ref, mid0_ref, mid1_ref,
    send_ref, h0_ref, h1_ref,
):
    rows, cols = m_ref.shape[1:3]
    odd = parity()

    def slab(f):
        return outer_slab(outer_ref[f], m_ref.at[f], tiles)

    def beside(h_ref, mid_ref):
        middle = mid_ref[pl.ds(odd * (rows - 4), 2)]
        return either([h_ref[...], middle], [middle, h_ref[...]])

    bases = [lambda: acc0_ref[...], lambda: acc1_ref[...]]
    hidden(slab, bases, places(rows)[2], w_ref, tiles, rows, h0_ref, h1_ref)
    h0, h1 = beside(h0_ref, mid0_ref), beside(h1_ref, mid1_ref)
    partial_rows(times, h0, h1, v_ref, 2, cols, send_ref)


def rest_body(
    x_ref, mid0_ref, mid1_ref, near0_ref, near1_ref, far0_ref, far1_ref, v_ref, b_ref, out_ref,
    h0_ref, h1_ref,
):
    rows, cols = x_ref.shape[1:3]
    middle, near, far = places(rows)
    h0_ref[middle], h1_ref[middle] = mid0_ref[...], mid1_ref[...]
    h0_ref[near], h1_ref[near] = near0_ref[...], near1_ref[...]
    h0_ref[far], h1_ref[far] = far0_ref[...], far1_ref[...]
    h0, h1 = row_taps(h0_ref[...], rows), row_taps(h1_ref[...], rows)
    weights = weight_rows(v_ref, 1) + 2 * weight_rows(v_ref, 2)
    part = convolved(h0 + h0 + h1, weights, rows, cols)
    total = x_ref[0].astype(jnp.float32) + x_ref[1].astype(jnp.float32) + part
    out_ref[0] = total * 0.5 + b_ref[...]


def join(rest_ref, part_ref, out_ref, start, made_ref, sem):
    part = part_ref[...].astype(jnp.float32)
    part = jnp.where(lax.axis_index("tm") == 0, jnp.zeros_like(part), part)
    place = pl.ds(start, part.shape[0])
    made_ref[...] = (rest_ref[0, place] + 0.5 * part).astype(jnp.bfloat16)
    copy = pltpu.make_async_copy(made_ref, out_ref.at[0, place], sem)
    copy.start()
    copy.wait()


def join_near_body(rest_ref, part_ref, out_ref, made_ref, sem):
    join(rest_ref, part_ref, out_ref, 2 * (1 - parity()), made_ref, sem)


def join_far_body(rest_ref, part_ref, _, out_ref, made_ref, sem):
    join(rest_ref, part_ref, out_ref, parity() * (rest_ref.shape[1] - 2), made_ref, sem)


def block(x, weight_first, bias_first, weight_second, bias_second):
    _, rows, cols, channels = x.shape
    clips, tiles, times = (lax.axis_size(axis) for axis in ("clips", "tile", "tm"))
    forward = [(i, i + 1) for i in range(times - 1)]
    ring = forward + [(times - 1, 0)]
    inner_pairs = [(i, i + 1) for i in range(0, tiles - 1, 2)]
    outer_pairs = [(i, i + 1) for i in range(1, tiles - 1, 2)]
    inner_pairs += [(j, i) for i, j in inner_pairs]
    outer_pairs += [(j, i) for i, j in outer_pairs]
    paired = {i for i, _ in outer_pairs}
    unpaired = [i for i in range(tiles) if i not in paired]
    outer_full = [(c * tiles + i, c * tiles + j) for c in range(clips) for i, j in outer_pairs]
    outer_full += [(c * tiles + i, (c + 1) % clips * tiles + i) for c in range(clips) for i in unpaired]
    diagonal = [(i * times + s, j * times + t) for i, j in outer_pairs for s, t in forward]

    def frames(*lead, dtype=jnp.bfloat16):
        return jax.ShapeDtypeStruct((*lead, cols, channels), dtype)

    f32 = jnp.float32
    earlier = lax.ppermute(x, "tm", ring)
    x, outer_edge, inner_edge = call(
        edges_body,
        [frames(2, rows), frames(2, 2), frames(2, 2)],
        (pltpu.with_memory_space_constraint(x, pltpu.HBM),),
        10**10,
        in_specs=[HBM],
        scratch=[pltpu.SemaphoreType.DMA((2,))],
    )
    inner = lax.ppermute(inner_edge, "tile", inner_pairs)
    outer = lax.ppermute(outer_edge, ("clips", "tile"), outer_full)
    corner = lax.ppermute(outer_edge, ("tile", "tm"), diagonal)

    bias_first = bias_first.reshape(1, 1, -1)
    bias_second = bias_second.reshape(1, 1, -1)
    unit = 2 * 9 * channels * channels * cols
    wide = rows + 2
    sums0, sums1 = call(
        own_near_body,
        [frames(rows, dtype=f32), frames(rows, dtype=f32)],
        (x, inner, weight_first, bias_first),
        3 * unit * rows,
    )
    far0, far1 = call(
        functools.partial(own_far_body, tiles),
        [frames(2, dtype=f32), frames(2, dtype=f32)],
        (x, outer, weight_first, bias_first),
        0,
    )
    (inner_edge,) = call(turn_body, [frames(2, 2)], (earlier,), 0)
    inner_corner = lax.ppermute(inner_edge, "tile", inner_pairs)

    mid0, mid1 = call(
        functools.partial(middle_body, tiles),
        [frames(rows - 2), frames(rows - 2)],
        (earlier, weight_first, weight_second, sums0, sums1),
        0,
    )
    near_send, near0, near1 = call(
        functools.partial(near_body, tiles, times),
        [frames(rows - 2), frames(2), frames(2)],
        (earlier, inner_corner, weight_first, weight_second, sums0, sums1, mid0, mid1),
        0,
    )
    near_part = lax.ppermute(near_send, "tm", ring)
    far_send, last0, last1 = call(
        functools.partial(far_body, tiles, times),
        [frames(2), frames(2), frames(2)],
        (earlier, corner, weight_first, weight_second, far0, far1, mid0, mid1),
        0,
    )
    far_part = lax.ppermute(far_send, "tm", forward)
    (rest,) = call(
        rest_body,
        [frames(1, rows, dtype=f32)],
        (x, mid0, mid1, near0, near1, last0, last1, weight_second, bias_second),
        3 * unit * rows,
        scratch=[pltpu.VMEM((wide, cols, channels), jnp.bfloat16)] * 2,
    )
    (pooled,) = call(
        join_near_body,
        [frames(1, rows)],
        (rest, near_part),
        0,
        out_specs=[HBM],
        scratch=[pltpu.VMEM((rows - 2, cols, channels), jnp.bfloat16), pltpu.SemaphoreType.DMA(())],
    )
    (pooled,) = call(
        join_far_body,
        [frames(1, rows)],
        (rest, far_part, pooled),
        0,
        in_specs=[VMEM, VMEM, HBM],
        out_specs=[HBM],
        scratch=[pltpu.VMEM((2, cols, channels), jnp.bfloat16), pltpu.SemaphoreType.DMA(())],
        aliases={2: 0},
    )
    return pooled


def solution(mesh):
    in_specs = (P(("clips", "tm"), "tile", None, None), P(), P(), P(), P())
    out_specs = P(("clips", "tm"), "tile", None, None)
    return jax.shard_map(block, mesh=mesh, in_specs=in_specs, out_specs=out_specs, check_vma=False)
```
